32 devices in a mesh: grp: 2 (over x), tile: 16 (over z, y, core).
Axes of the slice: x: 2, y: 2, z: 4, core: 2. Of those that a mesh axis runs over, the one named last changes fastest.
Arguments:
- projections: bfloat16 [512, 61, 128], P('grp', None, 'tile'), parts along dimension 0, may hold values from -1.1953125 to 1.1953125
- tilt_angle: float32 [122], P('grp'), parts along dimension 0, may hold values from -1.05 to 1.05
- row_range: int32 [122, 2], P('grp'), parts along dimension 0, may hold values from 0 to 256, as said below
- template_bank: bfloat16 [64, 16, 256], replicated, may hold values from -0.09375 to 0.09375
- rot_index: int32 [8], replicated, may hold values from 0 to 63
Outputs:
- score: float32 [16, 64, 1024], P('tile', 'grp'), parts along dimension 1
The draws below stay inside these ranges and needn't reach their ends.
There are 2 independent parts, one for each index of `grp`. The reference program is written for one: setup_inputs(seed, part) draws one part's arguments, and reference() takes and returns one part's arrays. A program takes and returns all parts, laid end to end along the dimension named above; an argument that names none is the same for every part. Nothing has to cross between parts.
Inputs may be any that keep to these rules, and one draw needn't show every extreme that they name: `row_range`: each tilt's valid rows run from its first value up to but not including its second, which is larger; the tilt of index 30 covers all 256 rows.
All inputs are finite; a program needn't handle non-finite values.
Results may differ from the reference program's by a relative error of at most 0.0095.
Values may be sent and summed in bfloat16 or wider, within the bound.
No kernel may reach another device: no remote copies, remote signals or barrier semaphores. Data moves between devices by JAX's collectives and lax.ppermute only.
A program may use at most 64 MiB of HBM per device.

```python
import math
import jax
import jax.numpy as jnp
from jax import lax

EDGE = 32
XT = 2
ZT = 1
K = 16
NTILT = 61
BANK = 64
NTPL = 8
HALO = 8
L = 48
X = 64
Z = 32
Y = 256
NDET = 128
N_TILE = 16


def draw_row_range(key, part):
    first_key, second_key = jax.random.split(jax.random.fold_in(key, 17))
    tilt_ids = jnp.arange(NTILT, dtype=jnp.int32)
    spans = Y // 4 + jax.random.randint(first_key, (NTILT,), 0, Y // 4 + 1)
    starts = jax.random.randint(second_key, (NTILT,), 0, Y - spans + 1)
    middle = NTILT // 2
    spans = jnp.where(tilt_ids == middle, Y, spans)
    starts = jnp.where(tilt_ids == middle, 0, starts)
    return jnp.stack([starts, starts + spans], axis=1).astype(jnp.int32)


def with_ends(array, rng, low, top_value):
    extent = array.shape
    place = [jax.random.randint(jax.random.fold_in(rng, axis), (), 0, extent[axis]) for axis in range(len(extent))]
    array = array.at[tuple(place)].set(low)
    longest = extent.index(max(extent))
    place[longest] = (place[longest] + 1) % extent[longest]
    return array.at[tuple(place)].set(top_value)


def block_scale(stream_key, shape, pieces, smallest, high):
    gain, own = 1.0, jax.random.fold_in(stream_key, 6)
    for axis_at, parts in pieces:
        draws = jnp.exp(jax.random.uniform(jax.random.fold_in(own, axis_at), (parts,), jnp.float32, smallest / len(pieces), high / len(pieces)))
        gain = gain * jnp.repeat(draws, shape[axis_at] // parts).reshape([-1 if axis == axis_at else 1 for axis in range(len(shape))])
    return gain


def gaussian(key, shape, spread, reach, cuts=(), kind=jnp.bfloat16):
    values = spread * jax.random.normal(key, shape, jnp.float32)
    if cuts:
        values = values * block_scale(key, shape, cuts, -0.22, 0.18)
    return jnp.clip(values, -reach, reach).astype(kind)


def setup_inputs(seed: int = 0, part: int = 0) -> dict:
    splits = jax.random.split(jax.random.key(seed), 6)
    own_keys = jax.random.split(jax.random.fold_in(splits[5], part), 6)
    projections = gaussian(own_keys[0], (Y, NTILT, NDET), 0.2, 1.1953125, ((2, 16),))
    tilt_angle = jnp.clip(jax.random.uniform(own_keys[1], (NTILT,), jnp.float32, -1.05, 1.05), -1.05, 1.05)
    row_range = draw_row_range(jax.random.fold_in(jax.random.fold_in(splits[5], part), 71), part)
    template_bank = gaussian(splits[3], (BANK, K, K * K), (K * K * K) ** -0.5, 0.09375)
    rot_index = with_ends(jax.random.randint(splits[4], (NTPL,), 0, BANK), jax.random.fold_in(splits[4], 1), 0, BANK - 1).astype(jnp.int32)
    return dict(projections=projections, tilt_angle=tilt_angle, row_range=row_range, template_bank=template_bank, rot_index=rot_index)


voxel_scale = 1.4


def phase_tables(length, out_count, in_count):
    row_index = jnp.arange(out_count, dtype=jnp.int32)[:, None]
    col_index = jnp.arange(in_count, dtype=jnp.int32)[None, :]
    phases = ((row_index * col_index) % length).astype(jnp.float32) * (2.0 * math.pi / length)
    return jnp.cos(phases).astype(jnp.bfloat16), jnp.sin(phases).astype(jnp.bfloat16)


def contract(pattern, table, values):
    return jnp.einsum(pattern, values.astype(jnp.float32), table.astype(jnp.float32))


def complex_pass(pattern, cos_t, sin_t, real_part, imag_part, sign):
    real_next = contract(pattern, cos_t, real_part) - sign * contract(pattern, sin_t, imag_part)
    imag_next = contract(pattern, cos_t, imag_part) + sign * contract(pattern, sin_t, real_part)
    return real_next.astype(jnp.bfloat16), imag_next.astype(jnp.bfloat16)


def forward_spectrum(voxels, length):
    cos_z, sin_z = phase_tables(length, length, voxels.shape[-1])
    real_part = contract("...z,kz->...k", cos_z, voxels).astype(jnp.bfloat16)
    imag_part = (-contract("...z,kz->...k", sin_z, voxels)).astype(jnp.bfloat16)
    cos_x, sin_x = phase_tables(length, length, voxels.shape[-2])
    real_part, imag_part = complex_pass("...xz,kx->...kz", cos_x, sin_x, real_part, imag_part, -1.0)
    cos_y, sin_y = phase_tables(length, length, voxels.shape[-3])
    real_part, imag_part = complex_pass("...yxz,ky->...kxz", cos_y, sin_y, real_part, imag_part, -1.0)
    return real_part, imag_part


def inverse_real(real_part, imag_part, length, edge_count):
    cos_t, sin_t = phase_tables(length, edge_count, length)
    real_part, imag_part = complex_pass("...yxz,ky->...kxz", cos_t, sin_t, real_part, imag_part, 1.0)
    real_part, imag_part = complex_pass("...xz,kx->...kz", cos_t, sin_t, real_part, imag_part, 1.0)
    pattern = "...z,kz->...k"
    summed = contract(pattern, cos_t, real_part) - contract(pattern, sin_t, imag_part)
    return summed / float(length ** 3)


def best_scores(tmpl_real, tmpl_imag, tile_real, tile_imag, length, edge_count):
    tr32 = tmpl_real.astype(jnp.float32)
    ti32 = tmpl_imag.astype(jnp.float32)
    er32 = tile_real.astype(jnp.float32)
    ei32 = tile_imag.astype(jnp.float32)
    prod_real = (tr32 * er32 + ti32 * ei32).astype(jnp.bfloat16)
    prod_imag = (tr32 * ei32 - ti32 * er32).astype(jnp.bfloat16)
    return jnp.max(inverse_real(prod_real, prod_imag, length, edge_count), axis=0)


def interp_weights(angles, det_count, x_count, z_count):
    x_offset = jnp.arange(x_count, dtype=jnp.float32) - (x_count - 1) / 2.0
    z_offset = jnp.arange(z_count, dtype=jnp.float32) - (z_count - 1) / 2.0
    detector_pos = voxel_scale * (x_offset[None, :, None] * jnp.cos(angles)[:, None, None]
                                  + z_offset[None, None, :] * jnp.sin(angles)[:, None, None]) + (det_count - 1) / 2.0
    detector = jnp.arange(det_count, dtype=jnp.float32)
    weights = jnp.maximum(0.0, 1.0 - jnp.abs(detector[None, :, None, None] - detector_pos[:, None, :, :]))
    return weights.astype(jnp.bfloat16).reshape(angles.shape[0] * det_count, x_count * z_count)


def reference(projections, tilt_angle, row_range, template_bank, rot_index):
    y_index = jnp.arange(Y, dtype=jnp.int32)
    row_mask = (y_index[:, None] >= row_range[None, :, 0]) & (y_index[:, None] < row_range[None, :, 1])
    masked = projections * row_mask[:, :, None].astype(jnp.bfloat16)
    padded_count = (NTILT + 7) // 8 * 8
    masked = jnp.pad(masked, ((0, 0), (0, padded_count - NTILT), (0, 0))).reshape(Y, padded_count * NDET)
    angles = jnp.pad(tilt_angle, (0, padded_count - NTILT))

    def add_block(summed, block_index):
        strip_rows = lax.dynamic_slice_in_dim(masked, block_index * (8 * NDET), 8 * NDET, 1)
        weights = interp_weights(lax.dynamic_slice_in_dim(angles, block_index * 8, 8, 0), NDET, X, Z)
        return summed + jnp.dot(strip_rows, weights, preferred_element_type=jnp.float32), None

    summed, _ = lax.scan(add_block, jnp.zeros((Y, X * Z), jnp.float32),
                         jnp.arange(padded_count // 8, dtype=jnp.int32))
    volume = summed.astype(jnp.bfloat16).reshape(Y, X, Z)
    padded = jnp.pad(volume, ((HALO, HALO), (HALO, HALO), (HALO, HALO)))
    chosen = jnp.take(template_bank, rot_index, axis=0).reshape(NTPL, K, K, K)
    tmpl_real, tmpl_imag = forward_spectrum(chosen, L)
    zero_index = jnp.zeros((), jnp.int32)

    def tile_scores(tile_number):
        row_block = tile_number // XT
        column_block = tile_number % XT
        region = lax.dynamic_slice(padded, (row_block * EDGE, column_block * EDGE, zero_index),
                                   (L, L, Z + 2 * HALO))
        blocks = []
        for zblock in range(ZT):
            voxels = region[:, :, zblock * EDGE: zblock * EDGE + L]
            tile_real, tile_imag = forward_spectrum(voxels, L)
            blocks.append(best_scores(tmpl_real, tmpl_imag, tile_real, tile_imag, L, EDGE))
        return jnp.concatenate(blocks, axis=2).reshape(EDGE, EDGE * Z)

    return lax.map(tile_scores, jnp.arange(N_TILE, dtype=jnp.int32))
```

```python
import math

import jax
import jax.numpy as jnp
import numpy as np
from jax import lax
from jax.experimental import pallas as pl
from jax.experimental.pallas import tpu as pltpu
from jax.sharding import PartitionSpec as P

EDGE = 32
XT = 2
K = 16
NTILT = 61
NTPL = 8
NDET = 128
HALO = K // 2
LEN = EDGE + K
X = XT * EDGE
Z = EDGE
XR = EDGE + HALO
LZ = Z + HALO
KZ = LZ // 2 + 1
NF = LEN * KZ
FP = 1024
XB = 8
NQ = XR // XB
LB = XB * Z
MAX_ANGLE = 1.05
VOXEL = 1.4
SCALE = 1.0 / (LEN * LEN * LZ)
BF = jnp.bfloat16
F32 = jnp.float32


def reach(q):
    x = np.arange(q * XB, (q + 1) * XB) - (X - 1) / 2.0
    z = np.arange(Z) - (Z - 1) / 2.0
    top = 0.0
    low = 0.0
    angle = np.linspace(-MAX_ANGLE, MAX_ANGLE, 4001)
    first = True
    for xv in (x[0], x[-1]):
        for zv in (z[0], z[-1]):
            pos = VOXEL * (xv * np.cos(angle) + zv * np.sin(angle)) + (NDET - 1) / 2.0
            low = pos.min() if first else min(low, pos.min())
            top = pos.max() if first else max(top, pos.max())
            first = False
    return math.ceil(low - 1.0 - 0.01), math.floor(top + 1.0 + 0.01)


def pair_list(n_det):
    pairs = []
    for q in range(NQ):
        low, top = reach(q)
        pairs.append(list(range(max(low, 0) // n_det, min(top, NDET - 1) // n_det + 1)))
    return pairs


def rounded(table):
    return np.asarray(table, np.float32).astype(jnp.bfloat16)


def plane_tables():
    kx = np.repeat(np.arange(LEN), KZ)
    kz = np.tile(np.arange(KZ), LEN)

    def phase(xs, zs):
        x = np.repeat(xs, len(zs))[:, None]
        z = np.tile(zs, len(xs))[:, None]
        return 2.0 * np.pi * ((kx * x % LEN) / LEN + (kz * z % LZ) / LZ)

    def padded(a):
        return np.pad(a, ((0, 0), (0, FP - NF)))

    def forward(xs, zs):
        p = phase(xs, zs)
        return rounded(np.concatenate([padded(np.cos(p)), padded(-np.sin(p))], 1))

    p = phase(np.arange(EDGE), np.arange(EDGE) - HALO)
    weight = np.where((kz == 0) | (kz == LZ // 2), 1.0, 2.0)
    inverse = rounded(
        np.concatenate([padded(weight * np.cos(p)), padded(-weight * np.sin(p))], 1).T
    )
    shift = 2.0 * np.pi * (kx * HALO % LEN) / LEN
    turn = np.zeros((4, FP), np.float32)
    turn[0, :NF], turn[1, :NF] = np.cos(shift), -np.sin(shift)
    turn[2, :NF] = 1.0
    return (
        forward(np.arange(XR), np.arange(Z)),
        forward(np.arange(K), np.arange(K)),
        inverse,
        turn,
    )


def line_tables():
    def table(outs, ins, sign):
        p = 2.0 * np.pi * (np.outer(np.arange(outs), np.arange(ins)) % LEN) / LEN
        c, s = np.cos(p), np.sin(p) * sign
        return c, s

    c, s = table(LEN, LEN, 1.0)
    region = rounded(np.block([[c, s], [-s, c]]))
    c, s = table(LEN, K, 1.0)
    template = rounded(np.block([[c, s], [-s, c]]))
    c, s = table(EDGE, LEN, 1.0)
    back = rounded(np.block([[c, -s], [s, c]]))
    return region, template, back


def pack_kernel(n_block, proj_ref, range_ref, out_ref):
    rows, y_count = proj_ref.shape
    depth = out_ref.shape[2]
    x = proj_ref[...].astype(F32)
    y = lax.broadcasted_iota(jnp.int32, (rows, y_count), 1)
    keep = (y >= range_ref[:, 0:1]) & (y < range_ref[:, 1:2])
    x = jnp.where(keep, x, 0.0)
    if depth > rows:
        x = jnp.concatenate([x, jnp.zeros((depth - rows, y_count), F32)], 0)
    xt = x.T
    for b in range(n_block):
        low, top = b * EDGE - HALO, b * EDGE - HALO + LEN
        part = xt[max(low, 0) : min(top, y_count)]
        if low < 0:
            part = jnp.concatenate([jnp.zeros((-low, depth), F32), part], 0)
        if top > y_count:
            part = jnp.concatenate([part, jnp.zeros((top - y_count, depth), F32)], 0)
        out_ref[b] = part.astype(BF)


def weight_kernel(n_det, n_tile, pairs, col_ref, turns_ref, w_ref, p_ref):
    col = col_ref[0]
    depth = turns_ref.shape[0]
    lane = lax.broadcasted_iota(jnp.int32, (1, LB), 1)
    z = (lane % Z).astype(F32) - (Z - 1) / 2.0
    step = (lane // Z).astype(F32)
    row = lax.broadcasted_iota(jnp.int32, (depth, 1), 0)
    own = (row % n_det).astype(F32)
    base = 0
    for q, sources in enumerate(pairs):
        block = jnp.where(col == 0, q, NQ - 1 - q) * XB + col * (X - XR)
        x = step + (block.astype(F32) - (X - 1) / 2.0)
        pos = VOXEL * (x * turns_ref[:, 0:1] + z * turns_ref[:, 1:2])
        p_ref[...] = pos + ((NDET - 1) / 2.0 - own)

        def build(j, carry, base=base, first=sources[0]):
            src = first + j
            src = jnp.where(col == 0, src, n_tile - 1 - src)
            shift = (src * n_det).astype(F32)
            w_ref[base + j] = jnp.maximum(0.0, 1.0 - jnp.abs(p_ref[...] - shift)).astype(BF)
            return carry

        lax.fori_loop(0, len(sources), build, 0)
        base += len(sources)


def template_kernel(col_ref, rot_ref, bank_ref, plane_ref, line_ref, turn_ref, out_ref):
    col = col_ref[0]
    chosen = jnp.concatenate([bank_ref[rot_ref[r]] for r in range(NTPL)], 0)
    flat = jnp.dot(chosen, plane_ref[...], preferred_element_type=F32).astype(BF)
    cos = jnp.where(col == 0, turn_ref[0:1], turn_ref[2:3])
    sin = jnp.where(col == 0, turn_ref[1:2], turn_ref[3:4])
    for r in range(NTPL):
        part = flat[r * K : (r + 1) * K]
        stacked = jnp.concatenate([part[:, :FP], part[:, FP:]], 0)
        full = jnp.dot(line_ref[...], stacked, preferred_element_type=F32)
        real, imag = full[:LEN], -full[LEN:]
        out_ref[r, :LEN] = (real * cos - imag * sin).astype(BF)
        out_ref[r, LEN:] = (real * sin + imag * cos).astype(BF)


def score_kernel(
    n_block,
    pairs,
    col_ref,
    own_ref,
    other_ref,
    w_ref,
    tmpl_ref,
    plane_ref,
    line_ref,
    back_ref,
    inverse_ref,
    out_ref,
    vol_ref,
    mid_ref,
):
    col = col_ref[0]
    base = 0
    for q, sources in enumerate(pairs):
        total = jnp.zeros((LEN, LB), F32)
        for j, src in enumerate(sources):
            chip = jnp.where(col == 0, src // 2, n_block - 1 - src // 2)
            part = own_ref[chip] if src % 2 == 0 else other_ref[chip]
            total += jnp.dot(part, w_ref[base + j], preferred_element_type=F32)
        block = jnp.where(col == 0, q, NQ - 1 - q)
        vol_ref[:, pl.ds(pl.multiple_of(block * LB, LB), LB)] = total.astype(BF)
        base += len(sources)
    flat = jnp.dot(vol_ref[...], plane_ref[...], preferred_element_type=F32).astype(BF)
    stacked = jnp.concatenate([flat[:, :FP], flat[:, FP:]], 0)
    full = jnp.dot(line_ref[...], stacked, preferred_element_type=F32)
    real, imag = full[:LEN], full[LEN:]
    for r in range(NTPL):
        t_real = tmpl_ref[r, :LEN].astype(F32)
        t_imag = tmpl_ref[r, LEN:].astype(F32)
        prod = jnp.concatenate(
            [
                (t_real * real - t_imag * imag).astype(BF),
                (t_real * imag + t_imag * real).astype(BF),
            ],
            0,
        )
        line = jnp.dot(back_ref[...], prod, preferred_element_type=F32).astype(BF)
        mid_ref[r * EDGE : (r + 1) * EDGE, :FP] = line[:EDGE]
        mid_ref[r * EDGE : (r + 1) * EDGE, FP:] = line[EDGE:]
    corr = jnp.dot(mid_ref[...], inverse_ref[...], preferred_element_type=F32)
    best = corr[:EDGE]
    for r in range(1, NTPL):
        best = jnp.maximum(best, corr[r * EDGE : (r + 1) * EDGE])
    out_ref[0] = best * SCALE


VMEM = pl.BlockSpec(memory_space=pltpu.VMEM)
SMEM = pl.BlockSpec(memory_space=pltpu.SMEM)
LIMIT = pltpu.CompilerParams(vmem_limit_bytes=48 << 20)


def solution(mesh):
    n_tile = mesh.shape["tile"]
    n_block = n_tile // XT
    n_det = NDET // n_tile
    rows = NTILT * n_det
    depth = (rows + 127) // 128 * 128
    pairs = pair_list(n_det)
    n_pair = sum(len(p) for p in pairs)
    plane, plane_t, inverse, turn = plane_tables()
    line, line_t, back = line_tables()

    def local(projections, tilt_angle, row_range, template_bank, rot_index):
        y_count = projections.shape[0]
        position = lax.axis_index("tile")
        col = (position % XT).astype(jnp.int32).reshape(1)
        by_y = jnp.transpose(projections, (1, 2, 0)).reshape(rows, y_count)
        ranges = jnp.repeat(row_range, n_det, axis=0)
        send = pl.pallas_call(
            lambda *refs: pack_kernel(n_block, *refs),
            out_shape=jax.ShapeDtypeStruct((n_block, LEN, depth), BF),
            in_specs=[VMEM, VMEM],
            out_specs=VMEM,
            compiler_params=LIMIT,
        )(by_y, ranges)
        same = [[c + XT * k for k in range(n_block)] for c in range(XT)]
        own = lax.all_to_all(send, "tile", 0, 0, tiled=True, axis_index_groups=same)
        other = lax.ppermute(own, "tile", [(i, i ^ 1) for i in range(n_tile)])
        turns = jnp.stack([jnp.cos(tilt_angle), jnp.sin(tilt_angle)], 1)
        turns = jnp.pad(jnp.repeat(turns, n_det, axis=0), ((0, depth - rows), (0, 0)))
        weights = pl.pallas_call(
            lambda *refs: weight_kernel(n_det, n_tile, pairs, *refs),
            out_shape=jax.ShapeDtypeStruct((n_pair, depth, LB), BF),
            in_specs=[SMEM, VMEM],
            out_specs=VMEM,
            scratch_shapes=[pltpu.VMEM((depth, LB), F32)],
            compiler_params=LIMIT,
        )(col, turns)
        spectra = pl.pallas_call(
            template_kernel,
            out_shape=jax.ShapeDtypeStruct((NTPL, 2 * LEN, FP), BF),
            in_specs=[SMEM, SMEM, VMEM, VMEM, VMEM, VMEM],
            out_specs=VMEM,
            compiler_params=LIMIT,
        )(col, rot_index, template_bank, jnp.asarray(plane_t), jnp.asarray(line_t), jnp.asarray(turn))
        return pl.pallas_call(
            lambda *refs: score_kernel(n_block, pairs, *refs),
            out_shape=jax.ShapeDtypeStruct((1, EDGE, EDGE * Z), F32),
            in_specs=[SMEM] + [VMEM] * 8,
            out_specs=VMEM,
            scratch_shapes=[
                pltpu.VMEM((LEN, XR * Z), BF),
                pltpu.VMEM((NTPL * EDGE, 2 * FP), BF),
            ],
            compiler_params=LIMIT,
        )(
            col,
            own,
            other,
            weights,
            spectra,
            jnp.asarray(plane),
            jnp.asarray(line),
            jnp.asarray(back),
            jnp.asarray(inverse),
        )

    return jax.shard_map(
        local,
        mesh=mesh,
        in_specs=(P("grp", None, "tile"), P("grp"), P("grp", None), P(), P()),
        out_specs=P("tile", "grp", None),
        check_vma=False,
    )
```

```python
import math

import jax
import jax.numpy as jnp
import numpy as np
from jax import lax
from jax.experimental import pallas as pl
from jax.experimental.pallas import tpu as pltpu
from jax.sharding import Mesh
from jax.sharding import PartitionSpec as P

EDGE = 32
XT = 2
K = 16
NTILT = 61
NTPL = 8
NDET = 128
HALO = K // 2
LEN = EDGE + K
X = XT * EDGE
Z = EDGE
XR = EDGE + HALO
LZ = Z + HALO
KZ = LZ // 2 + 1
NF = LEN * KZ
FP = 1024
XB = 8
NQ = XR // XB
LB = XB * Z
MAX_ANGLE = 1.05
VOXEL = 1.4
SCALE = 1.0 / (LEN * LEN * LZ)
BF = jnp.bfloat16
F32 = jnp.float32


def reach(q):
    x = np.arange(q * XB, (q + 1) * XB) - (X - 1) / 2.0
    z = np.arange(Z) - (Z - 1) / 2.0
    top = 0.0
    low = 0.0
    angle = np.linspace(-MAX_ANGLE, MAX_ANGLE, 4001)
    first = True
    for xv in (x[0], x[-1]):
        for zv in (z[0], z[-1]):
            pos = VOXEL * (xv * np.cos(angle) + zv * np.sin(angle)) + (NDET - 1) / 2.0
            low = pos.min() if first else min(low, pos.min())
            top = pos.max() if first else max(top, pos.max())
            first = False
    return math.ceil(low - 1.0 - 0.01), math.floor(top + 1.0 + 0.01)


def pair_list(n_det):
    pairs = []
    for q in range(NQ):
        low, top = reach(q)
        pairs.append(list(range(max(low, 0) // n_det, min(top, NDET - 1) // n_det + 1)))
    return pairs


def rounded(table):
    return np.asarray(table, np.float32).astype(jnp.bfloat16)


def plane_tables():
    kz = np.repeat(np.arange(KZ), LEN)
    kx = np.tile(np.arange(LEN), KZ)

    def waves(k, at, length):
        p = 2.0 * np.pi * (np.outer(at, k) % length) / length
        out = np.zeros((2, len(at), FP), np.float32)
        out[0, :, : len(k)], out[1, :, : len(k)] = np.cos(p), np.sin(p)
        return out

    vx = np.repeat(np.arange(EDGE), EDGE)
    vz = np.tile(np.arange(EDGE) - HALO, EDGE)
    weight = np.full((KZ, 1), 2.0)
    weight[0] = weight[-1] = 1.0
    return (
        waves(kx, np.arange(XR), LEN),
        waves(kz, np.arange(Z), LZ),
        waves(vx, np.arange(LEN), LEN),
        waves(vz, np.arange(KZ), LZ) * weight,
        waves(kx, np.array([HALO, 0]), LEN) * np.array([1.0, -1.0])[:, None, None],
    )


def line_tables():
    def table(outs, ins, sign):
        p = 2.0 * np.pi * (np.outer(np.arange(outs), np.arange(ins)) % LEN) / LEN
        c, s = np.cos(p), np.sin(p) * sign
        return c, s

    c, s = table(LEN, LEN, 1.0)
    region = rounded(np.block([[c, s], [-s, c]]))
    c, s = table(LEN, K, 1.0)
    template = rounded(np.block([[c, s], [-s, c]]))
    c, s = table(EDGE, LEN, 1.0)
    back = rounded(np.block([[c, -s], [s, c]]))
    return region, template, back


def pack_kernel(n_block, range_ref, proj_ref, out_ref):
    n_tilt, n_det, y_count = proj_ref.shape
    depth = out_ref.shape[2]
    y = lax.broadcasted_iota(jnp.int32, (n_det, y_count), 1)
    parts = []
    for t in range(n_tilt):
        keep = (y >= range_ref[0, t]) & (y < range_ref[1, t])
        parts.append(jnp.where(keep, proj_ref[t].astype(F32), 0.0))
    if depth > n_tilt * n_det:
        parts.append(jnp.zeros((depth - n_tilt * n_det, y_count), F32))
    xt = jnp.concatenate(parts, 0).T
    for b in range(n_block):
        low, top = b * EDGE - HALO, b * EDGE - HALO + LEN
        part = xt[max(low, 0) : min(top, y_count)]
        if low < 0:
            part = jnp.concatenate([jnp.zeros((-low, depth), F32), part], 0)
        if top > y_count:
            part = jnp.concatenate([part, jnp.zeros((top - y_count, depth), F32)], 0)
        out_ref[b] = part.astype(BF)


def build_weights(n_det, n_tile, pairs, col, turns_ref, w_ref, p_ref):
    depth = turns_ref.shape[0]
    lane = lax.broadcasted_iota(jnp.int32, (1, LB), 1)
    z = (lane % Z).astype(F32) - (Z - 1) / 2.0
    step = (lane // Z).astype(F32)
    row = lax.broadcasted_iota(jnp.int32, (depth, 1), 0)
    own = (row % n_det).astype(F32)
    base = 0
    for q, sources in enumerate(pairs):
        block = jnp.where(col == 0, q, NQ - 1 - q) * XB + col * (X - XR)
        x = step + (block.astype(F32) - (X - 1) / 2.0)
        pos = VOXEL * (x * turns_ref[:, 0:1] + z * turns_ref[:, 1:2])
        p_ref[...] = pos + ((NDET - 1) / 2.0 - own)

        def build(j, carry, base=base, first=sources[0]):
            src = first + j
            src = jnp.where(col == 0, src, n_tile - 1 - src)
            shift = (src * n_det).astype(F32)
            w_ref[base + j] = jnp.maximum(0.0, 1.0 - jnp.abs(p_ref[...] - shift)).astype(BF)
            return carry

        lax.fori_loop(0, len(sources), build, 0)
        base += len(sources)


def build_planes(fx_ref, fz_ref, ix_ref, iz_ref, plane_ref, inverse_ref):
    def forward(x, carry):
        cos_x, sin_x = fx_ref[0, pl.ds(x, 1)], fx_ref[1, pl.ds(x, 1)]
        cos_z, sin_z = fz_ref[0], fz_ref[1]
        at = pl.ds(pl.multiple_of(x * Z, Z), Z)
        plane_ref[at, :FP] = (cos_x * cos_z - sin_x * sin_z).astype(BF)
        plane_ref[at, FP:] = (-sin_x * cos_z - cos_x * sin_z).astype(BF)
        return carry

    lax.fori_loop(0, XR, forward, 0)

    def inverse(k, carry):
        cos_z, sin_z = iz_ref[0, pl.ds(k, 1)], iz_ref[1, pl.ds(k, 1)]
        cos_x, sin_x = ix_ref[0], ix_ref[1]
        low = pl.multiple_of(k * LEN, 16)
        inverse_ref[pl.ds(low, LEN)] = (cos_x * cos_z - sin_x * sin_z).astype(BF)
        inverse_ref[pl.ds(FP + low, LEN)] = (-sin_x * cos_z - cos_x * sin_z).astype(BF)
        return carry

    lax.fori_loop(0, KZ, inverse, 0)
    inverse_ref[NF:FP] = jnp.zeros((FP - NF, EDGE * EDGE), BF)
    inverse_ref[FP + NF :] = jnp.zeros((FP - NF, EDGE * EDGE), BF)


def build_templates(col, rot_ref, bank_ref, plane_ref, line_ref, turn_ref, out_ref):
    chosen = jnp.concatenate([bank_ref[rot_ref[r]] for r in range(NTPL)], 0)
    plane = jnp.concatenate([plane_ref[b * Z : b * Z + K] for b in range(K)], 0)
    flat = jnp.dot(chosen, plane, preferred_element_type=F32).astype(BF)
    cos = jnp.where(col == 0, turn_ref[0, 0:1], turn_ref[0, 1:2])
    sin = jnp.where(col == 0, turn_ref[1, 0:1], turn_ref[1, 1:2])
    for r in range(NTPL):
        part = flat[r * K : (r + 1) * K]
        stacked = jnp.concatenate([part[:, :FP], part[:, FP:]], 0)
        full = jnp.dot(line_ref[...], stacked, preferred_element_type=F32)
        real, imag = full[:LEN], -full[LEN:]
        out_ref[r, :LEN] = (real * cos - imag * sin).astype(BF)
        out_ref[r, LEN:] = (real * sin + imag * cos).astype(BF)


def prepare_kernel(
    n_det,
    n_tile,
    pairs,
    col_ref,
    rot_ref,
    turns_ref,
    bank_ref,
    fx_ref,
    fz_ref,
    ix_ref,
    iz_ref,
    line_ref,
    turn_ref,
    w_ref,
    plane_ref,
    inverse_ref,
    tmpl_ref,
    done_ref,
    p_ref,
):
    col = col_ref[0]
    build_planes(fx_ref, fz_ref, ix_ref, iz_ref, plane_ref, inverse_ref)
    build_weights(n_det, n_tile, pairs, col, turns_ref, w_ref, p_ref)
    build_templates(col, rot_ref, bank_ref, plane_ref, line_ref, turn_ref, tmpl_ref)
    done_ref[...] = jnp.zeros_like(done_ref)


def partial_sums(n_block, pairs, parity, col, data_ref, w_ref):
    base = 0
    for sources in pairs:
        total = jnp.zeros((LEN, LB), F32)
        for j, src in enumerate(sources):
            if src % 2 == parity:
                chip = jnp.where(col == 0, src // 2, n_block - 1 - src // 2)
                total += jnp.dot(data_ref[chip], w_ref[base + j], preferred_element_type=F32)
        base += len(sources)
        yield total


def half_kernel(n_block, pairs, col_ref, done_ref, own_ref, w_ref, out_ref):
    del done_ref
    for q, total in enumerate(partial_sums(n_block, pairs, 0, col_ref[0], own_ref, w_ref)):
        out_ref[q] = total


def score_kernel(
    n_block,
    pairs,
    col_ref,
    half_ref,
    other_ref,
    w_ref,
    tmpl_ref,
    plane_ref,
    line_ref,
    back_ref,
    inverse_ref,
    out_ref,
    vol_ref,
    mid_ref,
):
    col = col_ref[0]
    for q, total in enumerate(partial_sums(n_block, pairs, 1, col, other_ref, w_ref)):
        block = jnp.where(col == 0, q, NQ - 1 - q)
        at = pl.ds(pl.multiple_of(block * LB, LB), LB)
        vol_ref[:, at] = (total + half_ref[q]).astype(BF)
    flat = jnp.dot(vol_ref[...], plane_ref[...], preferred_element_type=F32).astype(BF)
    stacked = jnp.concatenate([flat[:, :FP], flat[:, FP:]], 0)
    full = jnp.dot(line_ref[...], stacked, preferred_element_type=F32)
    real, imag = full[:LEN], full[LEN:]
    for r in range(NTPL):
        t_real = tmpl_ref[r, :LEN].astype(F32)
        t_imag = tmpl_ref[r, LEN:].astype(F32)
        prod = jnp.concatenate(
            [
                (t_real * real - t_imag * imag).astype(BF),
                (t_real * imag + t_imag * real).astype(BF),
            ],
            0,
        )
        line = jnp.dot(back_ref[...], prod, preferred_element_type=F32).astype(BF)
        mid_ref[r * EDGE : (r + 1) * EDGE, :FP] = line[:EDGE]
        mid_ref[r * EDGE : (r + 1) * EDGE, FP:] = line[EDGE:]
    corr = jnp.dot(mid_ref[...], inverse_ref[...], preferred_element_type=F32)
    best = corr[:EDGE]
    for r in range(1, NTPL):
        best = jnp.maximum(best, corr[r * EDGE : (r + 1) * EDGE])
    out_ref[0] = best * SCALE


VMEM = pl.BlockSpec(memory_space=pltpu.VMEM)
SMEM = pl.BlockSpec(memory_space=pltpu.SMEM)


def limit(mib):
    return pltpu.CompilerParams(vmem_limit_bytes=mib << 20)


def cost(flops, nbytes):
    return pl.CostEstimate(flops=flops, bytes_accessed=nbytes, transcendentals=0)


def solution(mesh):
    n_tile = mesh.shape["tile"]
    n_block = n_tile // XT
    n_det = NDET // n_tile
    rows = NTILT * n_det
    depth = (rows + 127) // 128 * 128
    pairs = pair_list(n_det)
    n_pair = sum(len(p) for p in pairs)
    tables = plane_tables()
    line, line_t, back = line_tables()

    def local(projections, tilt_angle, row_range, template_bank, rot_index):
        col = lax.axis_index("core").astype(jnp.int32).reshape(1)
        by_y = jnp.transpose(projections, (1, 2, 0))
        send = pl.pallas_call(
            lambda *refs: pack_kernel(n_block, *refs),
            out_shape=jax.ShapeDtypeStruct((n_block, LEN, depth), BF),
            in_specs=[SMEM, VMEM],
            out_specs=VMEM,
            compiler_params=limit(4),
        )(row_range.T, by_y)
        own = lax.all_to_all(send, "chip", 0, 0, tiled=True)
        turns = jnp.stack([jnp.cos(tilt_angle), jnp.sin(tilt_angle)], 1)
        turns = jnp.pad(jnp.repeat(turns, n_det, axis=0), ((0, depth - rows), (0, 0)))
        weights, plane, inverse, spectra, done = pl.pallas_call(
            lambda *refs: prepare_kernel(n_det, n_tile, pairs, *refs),
            out_shape=(
                jax.ShapeDtypeStruct((n_pair, depth, LB), BF),
                jax.ShapeDtypeStruct((XR * Z, 2 * FP), BF),
                jax.ShapeDtypeStruct((2 * FP, EDGE * EDGE), BF),
                jax.ShapeDtypeStruct((NTPL, 2 * LEN, FP), BF),
                jax.ShapeDtypeStruct((8, 128), F32),
            ),
            in_specs=[SMEM, SMEM] + [VMEM] * 8,
            out_specs=(VMEM,) * 5,
            scratch_shapes=[pltpu.VMEM((depth, LB), F32)],
            compiler_params=limit(28),
            cost_estimate=cost(1 << 32, 24 << 20),
        )(
            col,
            rot_index,
            turns,
            template_bank,
            *[jnp.asarray(t) for t in tables[:4]],
            jnp.asarray(line_t),
            jnp.asarray(tables[4]),
        )
        own, done = lax.optimization_barrier((own, done))
        other = lax.ppermute(own, "core", [(0, 1), (1, 0)])
        half = pl.pallas_call(
            lambda *refs: half_kernel(n_block, pairs, *refs),
            out_shape=jax.ShapeDtypeStruct((NQ, LEN, LB), F32),
            in_specs=[SMEM, VMEM, VMEM, VMEM],
            out_specs=VMEM,
            compiler_params=limit(16),
            cost_estimate=cost(n_pair * LEN * depth * LB, n_pair * depth * LB),
        )(col, done, own, weights)
        return pl.pallas_call(
            lambda *refs: score_kernel(n_block, pairs, *refs),
            out_shape=jax.ShapeDtypeStruct((1, EDGE, EDGE * Z), F32),
            in_specs=[SMEM] + [VMEM] * 8,
            out_specs=VMEM,
            scratch_shapes=[
                pltpu.VMEM((LEN, XR * Z), BF),
                pltpu.VMEM((NTPL * EDGE, 2 * FP), BF),
            ],
            compiler_params=limit(28),
            cost_estimate=cost(4 << 30, 20 << 20),
        )(
            col,
            half,
            other,
            weights,
            spectra,
            plane,
            jnp.asarray(line),
            jnp.asarray(back),
            inverse,
        )

    tile = ("chip", "core")
    split = Mesh(mesh.devices.reshape(-1, n_block, XT), ("grp",) + tile)
    return jax.shard_map(
        local,
        mesh=split,
        in_specs=(P("grp", None, tile), P("grp"), P("grp", None), P(), P()),
        out_specs=P(tile, "grp", None),
        check_vma=False,
    )
```

```python
import math

import jax
import jax.numpy as jnp
import numpy as np
from jax import lax
from jax.experimental import pallas as pl
from jax.experimental.pallas import tpu as pltpu
from jax.sharding import PartitionSpec as P

EDGE = 32
XT = 2
K = 16
NTILT = 61
NTPL = 8
NDET = 128
HALO = K // 2
LEN = EDGE + K
X = XT * EDGE
Z = EDGE
XR = EDGE + HALO
LZ = Z + HALO
KZ = LZ // 2 + 1
NF = LEN * KZ
FP = 1024
XB = 8
NQ = XR // XB
LB = XB * Z
MAX_ANGLE = 1.05
VOXEL = 1.4
SCALE = 1.0 / (LEN * LEN * LZ)
BF = jnp.bfloat16
F32 = jnp.float32


def reach(q):
    x = np.arange(q * XB, (q + 1) * XB) - (X - 1) / 2.0
    z = np.arange(Z) - (Z - 1) / 2.0
    top = 0.0
    low = 0.0
    angle = np.linspace(-MAX_ANGLE, MAX_ANGLE, 4001)
    first = True
    for xv in (x[0], x[-1]):
        for zv in (z[0], z[-1]):
            pos = VOXEL * (xv * np.cos(angle) + zv * np.sin(angle)) + (NDET - 1) / 2.0
            low = pos.min() if first else min(low, pos.min())
            top = pos.max() if first else max(top, pos.max())
            first = False
    return math.ceil(low - 1.0 - 0.01), math.floor(top + 1.0 + 0.01)


def pair_list(n_det):
    pairs = []
    for q in range(NQ):
        low, top = reach(q)
        pairs.append(list(range(max(low, 0) // n_det, min(top, NDET - 1) // n_det + 1)))
    return pairs


def rounded(table):
    return np.asarray(table, np.float32).astype(jnp.bfloat16)


def plane_tables():
    kz = np.repeat(np.arange(KZ), LEN)
    kx = np.tile(np.arange(LEN), KZ)

    def waves(k, at, length):
        p = 2.0 * np.pi * (np.outer(at, k) % length) / length
        out = np.zeros((2, len(at), FP), np.float32)
        out[0, :, : len(k)], out[1, :, : len(k)] = np.cos(p), np.sin(p)
        return out

    vx = np.repeat(np.arange(EDGE), EDGE)
    vz = np.tile(np.arange(EDGE) - HALO, EDGE)
    weight = np.full((KZ, 1), 2.0)
    weight[0] = weight[-1] = 1.0
    return (
        waves(kx, np.arange(XR), LEN),
        waves(kz, np.arange(Z), LZ),
        waves(vx, np.arange(LEN), LEN),
        waves(vz, np.arange(KZ), LZ) * weight,
        waves(kx, np.array([HALO, 0]), LEN) * np.array([1.0, -1.0])[:, None, None],
    )


def line_tables():
    def table(outs, ins, sign):
        p = 2.0 * np.pi * (np.outer(np.arange(outs), np.arange(ins)) % LEN) / LEN
        c, s = np.cos(p), np.sin(p) * sign
        return c, s

    c, s = table(LEN, LEN, 1.0)
    region = rounded(np.block([[c, s], [-s, c]]))
    c, s = table(LEN, K, 1.0)
    template = rounded(np.block([[c, s], [-s, c]]))
    c, s = table(EDGE, LEN, 1.0)
    back = rounded(np.block([[c, -s], [s, c]]))
    return region, template, back


def pack_kernel(
    near_bit,
    masks,
    at_ref,
    range_hbm,
    proj_hbm,
    home_ref,
    near_ref,
    give_ref,
    mine_ref,
    proj_ref,
    range_ref,
    rows_ref,
    sem,
):
    fetch = [
        pltpu.make_async_copy(range_hbm, range_ref, sem.at[0]),
        pltpu.make_async_copy(proj_hbm, proj_ref, sem.at[1]),
    ]
    for copy in fetch:
        copy.start()
    for copy in fetch:
        copy.wait()
    n_tilt, n_det, y_count = proj_ref.shape
    depth = home_ref.shape[1]
    y = lax.broadcasted_iota(jnp.int32, (n_det, y_count), 1)
    parts = []
    for t in range(n_tilt):
        keep = (y >= range_ref[0, t]) & (y < range_ref[1, t])
        parts.append(jnp.where(keep, proj_ref[t].astype(F32), 0.0))
    if depth > n_tilt * n_det:
        parts.append(jnp.zeros((depth - n_tilt * n_det, y_count), F32))
    edge = jnp.zeros((HALO, depth), F32)
    rows_ref[...] = jnp.concatenate([edge, jnp.concatenate(parts, 0).T, edge], 0).astype(BF)
    chip, core = at_ref[0], at_ref[1]

    def rows(target):
        return rows_ref[pl.ds(pl.multiple_of(target * EDGE, EDGE), LEN)]

    home_ref[...] = rows(chip)
    near_ref[...] = rows(chip ^ near_bit)
    give_ref[0] = home_ref[...]
    for j, mask in enumerate(masks):
        mine_ref[j] = rows(chip ^ mask ^ (near_bit * core))
        give_ref[1 + j] = rows(chip ^ mask ^ (near_bit * (1 - core)))


def merge_kernel(mine_ref, got_ref, *out_refs):
    for j, out_ref in enumerate(out_refs):
        out_ref[0] = mine_ref[j]
        out_ref[1] = got_ref[1 + j]


def build_weights(n_det, n_tile, pairs, col, turns_ref, w_ref, p_ref):
    depth = p_ref.shape[0]
    lane = lax.broadcasted_iota(jnp.int32, (1, LB), 1)
    z = (lane % Z).astype(F32) - (Z - 1) / 2.0
    step = (lane // Z).astype(F32)
    own = lax.broadcasted_iota(jnp.int32, (n_det, LB), 0).astype(F32)
    if depth > NTILT * n_det:
        p_ref[NTILT * n_det :] = jnp.zeros((depth - NTILT * n_det, LB), F32)
    base = 0
    for q, sources in enumerate(pairs):
        block = jnp.where(col == 0, q, NQ - 1 - q) * XB + col * (X - XR)
        x = step + (block.astype(F32) - (X - 1) / 2.0)
        for t in range(NTILT):
            pos = VOXEL * (x * turns_ref[0, t] + z * turns_ref[1, t])
            p_ref[t * n_det : (t + 1) * n_det] = pos + ((NDET - 1) / 2.0 - own)

        def build(j, carry, base=base, first=sources[0]):
            src = first + j
            src = jnp.where(col == 0, src, n_tile - 1 - src)
            shift = (src * n_det).astype(F32)
            w_ref[base + j] = jnp.maximum(0.0, 1.0 - jnp.abs(p_ref[...] - shift)).astype(BF)
            return carry

        lax.fori_loop(0, len(sources), build, 0)
        base += len(sources)


def build_planes(fx_ref, fz_ref, ix_ref, iz_ref, plane_ref, inverse_ref):
    def forward(x, carry):
        cos_x, sin_x = fx_ref[0, pl.ds(x, 1)], fx_ref[1, pl.ds(x, 1)]
        cos_z, sin_z = fz_ref[0], fz_ref[1]
        at = pl.ds(pl.multiple_of(x * Z, Z), Z)
        plane_ref[at, :FP] = (cos_x * cos_z - sin_x * sin_z).astype(BF)
        plane_ref[at, FP:] = (-sin_x * cos_z - cos_x * sin_z).astype(BF)
        return carry

    lax.fori_loop(0, XR, forward, 0)

    def inverse(k, carry):
        cos_z, sin_z = iz_ref[0, pl.ds(k, 1)], iz_ref[1, pl.ds(k, 1)]
        cos_x, sin_x = ix_ref[0], ix_ref[1]
        low = pl.multiple_of(k * LEN, 16)
        inverse_ref[pl.ds(low, LEN)] = (cos_x * cos_z - sin_x * sin_z).astype(BF)
        inverse_ref[pl.ds(FP + low, LEN)] = (-sin_x * cos_z - cos_x * sin_z).astype(BF)
        return carry

    lax.fori_loop(0, KZ, inverse, 0)
    inverse_ref[NF:FP] = jnp.zeros((FP - NF, EDGE * EDGE), BF)
    inverse_ref[FP + NF :] = jnp.zeros((FP - NF, EDGE * EDGE), BF)


def build_templates(col, rot_ref, bank_ref, plane_ref, line_ref, turn_ref, out_ref):
    chosen = jnp.concatenate([bank_ref[rot_ref[r]] for r in range(NTPL)], 0)
    plane = jnp.concatenate([plane_ref[b * Z : b * Z + K] for b in range(K)], 0)
    flat = jnp.dot(chosen, plane, preferred_element_type=F32).astype(BF)
    cos = jnp.where(col == 0, turn_ref[0, 0:1], turn_ref[0, 1:2])
    sin = jnp.where(col == 0, turn_ref[1, 0:1], turn_ref[1, 1:2])
    for r in range(NTPL):
        part = flat[r * K : (r + 1) * K]
        stacked = jnp.concatenate([part[:, :FP], part[:, FP:]], 0)
        full = jnp.dot(line_ref[...], stacked, preferred_element_type=F32)
        real, imag = full[:LEN], -full[LEN:]
        out_ref[r, :LEN] = (real * cos - imag * sin).astype(BF)
        out_ref[r, LEN:] = (real * sin + imag * cos).astype(BF)


def prepare_kernel(
    n_det,
    n_tile,
    pairs,
    at_ref,
    rot_hbm,
    turns_hbm,
    bank_hbm,
    fx_hbm,
    fz_hbm,
    ix_hbm,
    iz_hbm,
    line_hbm,
    turn_hbm,
    w_ref,
    plane_ref,
    inverse_ref,
    tmpl_ref,
    done_ref,
    p_ref,
    rot_ref,
    turns_ref,
    *rest,
):
    *buffers, sem = rest
    sources = (turns_hbm, rot_hbm, bank_hbm, fx_hbm, fz_hbm, ix_hbm, iz_hbm, line_hbm, turn_hbm)
    targets = (turns_ref, rot_ref, *buffers)
    fetch = [
        pltpu.make_async_copy(a, b, sem.at[i]) for i, (a, b) in enumerate(zip(sources, targets))
    ]
    for copy in fetch:
        copy.start()
    fetch[0].wait()
    col = at_ref[1]
    build_weights(n_det, n_tile, pairs, col, turns_ref, w_ref, p_ref)
    for copy in fetch[1:]:
        copy.wait()
    bank_ref, fx_ref, fz_ref, ix_ref, iz_ref, line_ref, turn_ref = buffers
    build_planes(fx_ref, fz_ref, ix_ref, iz_ref, plane_ref, inverse_ref)
    build_templates(col, rot_ref, bank_ref, plane_ref, line_ref, turn_ref, tmpl_ref)
    done_ref[...] = jnp.zeros_like(done_ref)


def score_kernel(near_bit, masks, pairs, n_tile, *refs):
    n_op = len(masks)
    at_ref, home_ref, got_ref, near_ref, near_swap_ref = refs[:5]
    recv_refs, swap_refs = refs[5 : 5 + n_op], refs[5 + n_op : 5 + 2 * n_op]
    w_ref, tmpl_ref, plane_ref, line_ref, back_ref, inverse_ref = refs[5 + 2 * n_op : 11 + 2 * n_op]
    _, out_ref, data_ref, vol_ref, mid_ref = refs[11 + 2 * n_op :]
    chip, core = at_ref[0], at_ref[1]
    mate = 1 - core
    data_ref[chip * XT + core] = home_ref[...]
    data_ref[chip * XT + mate] = got_ref[0]
    data_ref[(chip ^ near_bit) * XT + core] = near_ref[...]
    data_ref[(chip ^ near_bit) * XT + mate] = near_swap_ref[...]
    for j, mask in enumerate(masks):
        here = (chip ^ mask ^ (near_bit * core)) * XT
        there = (chip ^ mask ^ (near_bit * mate)) * XT
        data_ref[here + core] = recv_refs[j][0]
        data_ref[here + mate] = recv_refs[j][1]
        data_ref[there + mate] = swap_refs[j][0]
        data_ref[there + core] = swap_refs[j][1]
    base = 0
    for q, sources in enumerate(pairs):
        total = jnp.zeros((LEN, LB), F32)
        for j, src in enumerate(sources):
            part = data_ref[jnp.where(core == 0, src, n_tile - 1 - src)]
            total += jnp.dot(part, w_ref[base + j], preferred_element_type=F32)
        base += len(sources)
        block = jnp.where(core == 0, q, NQ - 1 - q)
        vol_ref[:, pl.ds(pl.multiple_of(block * LB, LB), LB)] = total.astype(BF)
    flat = jnp.dot(vol_ref[...], plane_ref[...], preferred_element_type=F32).astype(BF)
    stacked = jnp.concatenate([flat[:, :FP], flat[:, FP:]], 0)
    full = jnp.dot(line_ref[...], stacked, preferred_element_type=F32)
    real, imag = full[:LEN], full[LEN:]
    for r in range(NTPL):
        t_real = tmpl_ref[r, :LEN].astype(F32)
        t_imag = tmpl_ref[r, LEN:].astype(F32)
        prod = jnp.concatenate(
            [
                (t_real * real - t_imag * imag).astype(BF),
                (t_real * imag + t_imag * real).astype(BF),
            ],
            0,
        )
        line = jnp.dot(back_ref[...], prod, preferred_element_type=F32).astype(BF)
        mid_ref[r * EDGE : (r + 1) * EDGE, :FP] = line[:EDGE]
        mid_ref[r * EDGE : (r + 1) * EDGE, FP:] = line[EDGE:]
    corr = jnp.dot(mid_ref[...], inverse_ref[...], preferred_element_type=F32)
    best = corr[:EDGE]
    for r in range(1, NTPL):
        best = jnp.maximum(best, corr[r * EDGE : (r + 1) * EDGE])
    out_ref[0] = best * SCALE


VMEM = pl.BlockSpec(memory_space=pltpu.VMEM)
SMEM = pl.BlockSpec(memory_space=pltpu.SMEM)
HBM = pl.BlockSpec(memory_space=pltpu.HBM)


def limit(mib):
    return pltpu.CompilerParams(vmem_limit_bytes=mib << 20)


def cost(flops, nbytes):
    return pl.CostEstimate(flops=flops, bytes_accessed=nbytes, transcendentals=0)


def shape(*dims, dtype=BF):
    return jax.ShapeDtypeStruct(dims, dtype)


def solution(mesh):
    n_tile = mesh.shape["tile"]
    n_block = n_tile // XT
    n_det = NDET // n_tile
    depth = (NTILT * n_det + 127) // 128 * 128
    near_bit = 2
    masks = [k for k in range(1, n_block) if not k & near_bit]
    n_op = len(masks)
    pairs = pair_list(n_det)
    n_pair = sum(len(p) for p in pairs)
    tables = plane_tables()
    line, line_t, back = line_tables()
    mate = [(i, i ^ 1) for i in range(n_tile)]
    near_pairs = [(i, i ^ (near_bit * XT)) for i in range(n_tile)]

    def route(mask):
        return [(i, i ^ (mask * XT) ^ (near_bit * XT * (i % XT))) for i in range(n_tile)]

    def local(projections, tilt_angle, row_range, template_bank, rot_index):
        y_count = projections.shape[0]
        position = lax.axis_index("tile").astype(jnp.int32)
        at = jnp.stack([position // XT, position % XT])
        by_y = jnp.transpose(projections, (1, 2, 0))
        home, near, give, mine = pl.pallas_call(
            lambda *refs: pack_kernel(near_bit, masks, *refs),
            out_shape=(
                shape(LEN, depth),
                shape(LEN, depth),
                shape(1 + n_op, LEN, depth),
                shape(n_op, LEN, depth),
            ),
            in_specs=[SMEM, HBM, HBM],
            out_specs=(VMEM,) * 4,
            scratch_shapes=[
                pltpu.VMEM(by_y.shape, BF),
                pltpu.SMEM((2, NTILT), jnp.int32),
                pltpu.VMEM((y_count + 2 * HALO, depth), BF),
                pltpu.SemaphoreType.DMA((2,)),
            ],
            compiler_params=limit(8),
        )(at, row_range.T, by_y)
        got = lax.ppermute(give, "tile", mate)
        near_in = lax.ppermute(near, "tile", near_pairs)
        payload = pl.pallas_call(
            merge_kernel,
            out_shape=(shape(2, LEN, depth),) * n_op,
            in_specs=[VMEM, VMEM],
            out_specs=(VMEM,) * n_op,
            compiler_params=limit(8),
        )(mine, got)
        arrived = [lax.ppermute(p, "tile", route(m)) for p, m in zip(payload, masks)]
        turns = jnp.stack([jnp.cos(tilt_angle), jnp.sin(tilt_angle)])
        weights, plane, inverse, spectra, done = pl.pallas_call(
            lambda *refs: prepare_kernel(n_det, n_tile, pairs, *refs),
            out_shape=(
                shape(n_pair, depth, LB),
                shape(XR * Z, 2 * FP),
                shape(2 * FP, EDGE * EDGE),
                shape(NTPL, 2 * LEN, FP),
                shape(8, 128, dtype=F32),
            ),
            in_specs=[SMEM] + [HBM] * 9,
            out_specs=(VMEM,) * 5,
            scratch_shapes=[
                pltpu.VMEM((depth, LB), F32),
                pltpu.SMEM((NTPL,), jnp.int32),
                pltpu.SMEM((2, NTILT), F32),
                pltpu.VMEM(template_bank.shape, BF),
                *[pltpu.VMEM(t.shape, F32) for t in tables[:4]],
                pltpu.VMEM(line_t.shape, BF),
                pltpu.VMEM(tables[4].shape, F32),
                pltpu.SemaphoreType.DMA((9,)),
            ],
            compiler_params=limit(28),
            cost_estimate=cost(1 << 32, 24 << 20),
        )(
            at,
            rot_index,
            turns,
            template_bank,
            *[jnp.asarray(t, F32) for t in tables[:4]],
            jnp.asarray(line_t),
            jnp.asarray(tables[4], F32),
        )
        near_in, done, *arrived = lax.optimization_barrier((near_in, done, *arrived))
        near_swap = lax.ppermute(near_in, "tile", mate)
        swapped = [lax.ppermute(a, "tile", mate) for a in arrived]
        return pl.pallas_call(
            lambda *refs: score_kernel(near_bit, masks, pairs, n_tile, *refs),
            out_shape=shape(1, EDGE, EDGE * Z, dtype=F32),
            in_specs=[SMEM] + [VMEM] * (11 + 2 * n_op),
            out_specs=VMEM,
            scratch_shapes=[
                pltpu.VMEM((n_tile, LEN, depth), BF),
                pltpu.VMEM((LEN, XR * Z), BF),
                pltpu.VMEM((NTPL * EDGE, 2 * FP), BF),
            ],
            compiler_params=limit(28),
            cost_estimate=cost(4 << 30, 20 << 20),
        )(
            at,
            home,
            got,
            near_in,
            near_swap,
            *arrived,
            *swapped,
            weights,
            spectra,
            plane,
            jnp.asarray(line),
            jnp.asarray(back),
            inverse,
            done,
        )

    return jax.shard_map(
        local,
        mesh=mesh,
        in_specs=(P("grp", None, "tile"), P("grp"), P("grp", None), P(), P()),
        out_specs=P("tile", "grp", None),
        check_vma=False,
    )
```

```python
import math

import jax
import jax.numpy as jnp
import numpy as np
from jax import lax
from jax.experimental import pallas as pl
from jax.experimental.pallas import tpu as pltpu
from jax.sharding import PartitionSpec as P

EDGE = 32
XT = 2
K = 16
NTILT = 61
NTPL = 8
NDET = 128
HALO = K // 2
LEN = EDGE + K
X = XT * EDGE
Z = EDGE
XR = EDGE + HALO
LZ = Z + HALO
KZ = LZ // 2 + 1
NF = LEN * KZ
FP = 1024
XB = 8
NQ = XR // XB
LB = XB * Z
MAX_ANGLE = 1.05
VOXEL = 1.4
SCALE = 1.0 / (LEN * LEN * LZ)
BF = jnp.bfloat16
F32 = jnp.float32


def reach(q):
    x = np.arange(q * XB, (q + 1) * XB) - (X - 1) / 2.0
    z = np.arange(Z) - (Z - 1) / 2.0
    top = 0.0
    low = 0.0
    angle = np.linspace(-MAX_ANGLE, MAX_ANGLE, 4001)
    first = True
    for xv in (x[0], x[-1]):
        for zv in (z[0], z[-1]):
            pos = VOXEL * (xv * np.cos(angle) + zv * np.sin(angle)) + (NDET - 1) / 2.0
            low = pos.min() if first else min(low, pos.min())
            top = pos.max() if first else max(top, pos.max())
            first = False
    return math.ceil(low - 1.0 - 0.01), math.floor(top + 1.0 + 0.01)


def pair_list(n_det):
    pairs = []
    for q in range(NQ):
        low, top = reach(q)
        pairs.append(list(range(max(low, 0) // n_det, min(top, NDET - 1) // n_det + 1)))
    return pairs


def rounded(table):
    return np.asarray(table, np.float32).astype(jnp.bfloat16)


def plane_tables():
    kz = np.repeat(np.arange(KZ), LEN)
    kx = np.tile(np.arange(LEN), KZ)

    def waves(k, at, length):
        p = 2.0 * np.pi * (np.outer(at, k) % length) / length
        out = np.zeros((2, len(at), FP), np.float32)
        out[0, :, : len(k)], out[1, :, : len(k)] = np.cos(p), np.sin(p)
        return out

    vx = np.repeat(np.arange(EDGE), EDGE)
    vz = np.tile(np.arange(EDGE) - HALO, EDGE)
    weight = np.full((KZ, 1), 2.0)
    weight[0] = weight[-1] = 1.0
    return (
        waves(kx, np.arange(XR), LEN),
        waves(kz, np.arange(Z), LZ),
        waves(vx, np.arange(LEN), LEN),
        waves(vz, np.arange(KZ), LZ) * weight,
        waves(kx, np.array([HALO, 0]), LEN) * np.array([1.0, -1.0])[:, None, None],
    )


def line_tables():
    def table(outs, ins, sign):
        p = 2.0 * np.pi * (np.outer(np.arange(outs), np.arange(ins)) % LEN) / LEN
        c, s = np.cos(p), np.sin(p) * sign
        return c, s

    c, s = table(LEN, LEN, 1.0)
    region = rounded(np.block([[c, s], [-s, c]]))
    c, s = table(LEN, K, 1.0)
    template = rounded(np.block([[c, s], [-s, c]]))
    c, s = table(EDGE, LEN, 1.0)
    back = rounded(np.block([[c, -s], [s, c]]))
    return region, template, back


def pack_kernel(
    near_bit,
    masks,
    at_ref,
    range_hbm,
    proj_hbm,
    home_ref,
    near_ref,
    give_ref,
    mine_ref,
    proj_ref,
    range_ref,
    rows_ref,
    sem,
):
    fetch = [
        pltpu.make_async_copy(range_hbm, range_ref, sem.at[0]),
        pltpu.make_async_copy(proj_hbm, proj_ref, sem.at[1]),
    ]
    for copy in fetch:
        copy.start()
    for copy in fetch:
        copy.wait()
    n_tilt, n_det, y_count = proj_ref.shape
    depth = home_ref.shape[1]
    y = lax.broadcasted_iota(jnp.int32, (n_det, y_count), 1)
    parts = []
    for t in range(n_tilt):
        keep = (y >= range_ref[0, t]) & (y < range_ref[1, t])
        parts.append(jnp.where(keep, proj_ref[t].astype(F32), 0.0))
    if depth > n_tilt * n_det:
        parts.append(jnp.zeros((depth - n_tilt * n_det, y_count), F32))
    edge = jnp.zeros((HALO, depth), F32)
    rows_ref[...] = jnp.concatenate([edge, jnp.concatenate(parts, 0).T, edge], 0).astype(BF)
    chip, core = at_ref[0], at_ref[1]

    def rows(target):
        return rows_ref[pl.ds(pl.multiple_of(target * EDGE, EDGE), LEN)]

    home_ref[...] = rows(chip)
    near_ref[...] = rows(chip ^ near_bit)
    give_ref[0] = home_ref[...]
    for j, mask in enumerate(masks):
        mine_ref[j] = rows(chip ^ mask ^ (near_bit * core))
        give_ref[1 + j] = rows(chip ^ mask ^ (near_bit * (1 - core)))


def merge_kernel(mine_ref, got_ref, *out_refs):
    for j, out_ref in enumerate(out_refs):
        out_ref[0] = mine_ref[j]
        out_ref[1] = got_ref[1 + j]


def build_weights(n_det, n_tile, pairs, col, turns_ref, w_ref, whole_ref, part_ref):
    depth = whole_ref.shape[0]
    lane = lax.broadcasted_iota(jnp.int32, (1, LB), 1)
    z = (lane % Z).astype(F32) - (Z - 1) / 2.0
    step = (lane // Z).astype(F32)
    pack = 16 // n_det
    own = lax.broadcasted_iota(jnp.int32, (n_det, LB), 0).astype(F32)
    top = NTILT // pack * pack
    tail = depth - top * n_det
    base = 0
    for q, sources in enumerate(pairs):
        block = jnp.where(col == 0, q, NQ - 1 - q) * XB + col * (X - XR)
        x = step + (block.astype(F32) - (X - 1) / 2.0)

        def tilt(t, z=z, x=x):
            pos = VOXEL * (x * turns_ref[0, t] + z * turns_ref[1, t]) + (NDET - 1) / 2.0
            whole = jnp.floor(pos)
            return own - whole, jnp.broadcast_to(pos - whole, own.shape)

        for first in range(0, NTILT, pack):
            got = [tilt(t) for t in range(first, min(first + pack, NTILT))]
            rows = pack * n_det if first < top else tail
            gap = rows - len(got) * n_det
            for ref, values in ((whole_ref, [g[0] for g in got]), (part_ref, [g[1] for g in got])):
                if gap:
                    values.append(jnp.zeros((gap, LB), F32))
                ref[first * n_det : first * n_det + rows] = jnp.concatenate(values, 0).astype(BF)

        def build(j, carry, base=base, first=sources[0]):
            src = first + j
            src = jnp.where(col == 0, src, n_tile - 1 - src)
            shift = (src * n_det).astype(F32).astype(BF)
            off = (whole_ref[...] + shift) - part_ref[...]
            one = jnp.ones((), BF)
            w_ref[base + j] = jnp.maximum(one - jnp.abs(off), jnp.zeros((), BF))
            return carry

        lax.fori_loop(0, len(sources), build, 0)
        base += len(sources)


def build_planes(fx_ref, fz_ref, ix_ref, iz_ref, plane_ref, inverse_ref):
    mid = LEN // 2
    flip = fx_ref[0, mid : mid + 1]

    def forward(x, carry, both):
        cos_x, sin_x = fx_ref[0, pl.ds(x, 1)], fx_ref[1, pl.ds(x, 1)]
        cos_z, sin_z = fz_ref[0], fz_ref[1]
        real = cos_x * cos_z - sin_x * sin_z
        imag = -sin_x * cos_z - cos_x * sin_z
        at = pl.ds(pl.multiple_of(x * Z, Z), Z)
        plane_ref[at, :FP] = real.astype(BF)
        plane_ref[at, FP:] = imag.astype(BF)
        if both:
            at = pl.ds(pl.multiple_of((x + mid) * Z, Z), Z)
            plane_ref[at, :FP] = (real * flip).astype(BF)
            plane_ref[at, FP:] = (imag * flip).astype(BF)
        return carry

    lax.fori_loop(0, XR - mid, lambda x, c: forward(x, c, True), 0)
    lax.fori_loop(XR - mid, mid, lambda x, c: forward(x, c, False), 0)
    turn = ix_ref[0, mid : mid + 1]

    def inverse(k, carry):
        cos_z, sin_z = iz_ref[0, pl.ds(k, 1)], iz_ref[1, pl.ds(k, 1)]
        cos_x, sin_x = ix_ref[0, :mid], ix_ref[1, :mid]
        real = cos_x * cos_z - sin_x * sin_z
        imag = -sin_x * cos_z - cos_x * sin_z
        low = pl.multiple_of(k * LEN, 16)
        inverse_ref[pl.ds(low, LEN)] = jnp.concatenate([real, real * turn], 0).astype(BF)
        inverse_ref[pl.ds(FP + low, LEN)] = jnp.concatenate([imag, imag * turn], 0).astype(BF)
        return carry

    lax.fori_loop(0, KZ, inverse, 0)
    inverse_ref[NF:FP] = jnp.zeros((FP - NF, EDGE * EDGE), BF)
    inverse_ref[FP + NF :] = jnp.zeros((FP - NF, EDGE * EDGE), BF)


def build_templates(col, rot_ref, bank_ref, plane_ref, line_ref, turn_ref, out_ref):
    chosen = jnp.concatenate([bank_ref[rot_ref[r]] for r in range(NTPL)], 0)
    plane = jnp.concatenate([plane_ref[b * Z : b * Z + K] for b in range(K)], 0)
    flat = jnp.dot(chosen, plane, preferred_element_type=F32).astype(BF)
    cos = jnp.where(col == 0, turn_ref[0, 0:1], turn_ref[0, 1:2])
    sin = jnp.where(col == 0, turn_ref[1, 0:1], turn_ref[1, 1:2])
    for r in range(NTPL):
        part = flat[r * K : (r + 1) * K]
        stacked = jnp.concatenate([part[:, :FP], part[:, FP:]], 0)
        full = jnp.dot(line_ref[...], stacked, preferred_element_type=F32)
        real, imag = full[:LEN], -full[LEN:]
        out_ref[r, :LEN] = (real * cos - imag * sin).astype(BF)
        out_ref[r, LEN:] = (real * sin + imag * cos).astype(BF)


def prepare_kernel(
    n_det,
    n_tile,
    pairs,
    at_ref,
    turns_hbm,
    rot_hbm,
    bank_hbm,
    fx_hbm,
    fz_hbm,
    ix_hbm,
    iz_hbm,
    line_hbm,
    turn_hbm,
    w_ref,
    plane_ref,
    inverse_ref,
    tmpl_ref,
    done_ref,
    whole_ref,
    part_ref,
    rot_ref,
    turns_ref,
    *rest,
):
    *buffers, sem = rest
    sources = (turns_hbm, rot_hbm, bank_hbm, fx_hbm, fz_hbm, ix_hbm, iz_hbm, line_hbm, turn_hbm)
    targets = (turns_ref, rot_ref, *buffers)
    fetch = [
        pltpu.make_async_copy(a, b, sem.at[i]) for i, (a, b) in enumerate(zip(sources, targets))
    ]
    for copy in fetch:
        copy.start()
    fetch[0].wait()
    col = at_ref[1]
    build_weights(n_det, n_tile, pairs, col, turns_ref, w_ref, whole_ref, part_ref)
    for copy in fetch[1:]:
        copy.wait()
    bank_ref, fx_ref, fz_ref, ix_ref, iz_ref, line_ref, turn_ref = buffers
    build_planes(fx_ref, fz_ref, ix_ref, iz_ref, plane_ref, inverse_ref)
    build_templates(col, rot_ref, bank_ref, plane_ref, line_ref, turn_ref, tmpl_ref)
    done_ref[...] = jnp.zeros_like(done_ref)


def score_kernel(near_bit, masks, pairs, n_tile, *refs):
    n_op = len(masks)
    at_ref, home_ref, got_ref, near_ref, near_swap_ref = refs[:5]
    recv_refs, swap_refs = refs[5 : 5 + n_op], refs[5 + n_op : 5 + 2 * n_op]
    w_ref, tmpl_ref, plane_ref, line_ref, back_ref, inverse_ref = refs[5 + 2 * n_op : 11 + 2 * n_op]
    _, out_ref, data_ref, vol_ref, mid_ref = refs[11 + 2 * n_op :]
    chip, core = at_ref[0], at_ref[1]
    mate = 1 - core
    data_ref[chip * XT + core] = home_ref[...]
    data_ref[chip * XT + mate] = got_ref[0]
    data_ref[(chip ^ near_bit) * XT + core] = near_ref[...]
    data_ref[(chip ^ near_bit) * XT + mate] = near_swap_ref[...]
    for j, mask in enumerate(masks):
        here = (chip ^ mask ^ (near_bit * core)) * XT
        there = (chip ^ mask ^ (near_bit * mate)) * XT
        data_ref[here + core] = recv_refs[j][0]
        data_ref[here + mate] = recv_refs[j][1]
        data_ref[there + mate] = swap_refs[j][0]
        data_ref[there + core] = swap_refs[j][1]
    base = 0
    for q, sources in enumerate(pairs):
        total = jnp.zeros((LEN, LB), F32)
        for j, src in enumerate(sources):
            part = data_ref[jnp.where(core == 0, src, n_tile - 1 - src)]
            total += jnp.dot(part, w_ref[base + j], preferred_element_type=F32)
        base += len(sources)
        block = jnp.where(core == 0, q, NQ - 1 - q)
        vol_ref[:, pl.ds(pl.multiple_of(block * LB, LB), LB)] = total.astype(BF)
    flat = jnp.dot(vol_ref[...], plane_ref[...], preferred_element_type=F32).astype(BF)
    stacked = jnp.concatenate([flat[:, :FP], flat[:, FP:]], 0)
    full = jnp.dot(line_ref[...], stacked, preferred_element_type=F32)
    real, imag = full[:LEN], full[LEN:]
    for r in range(NTPL):
        t_real = tmpl_ref[r, :LEN].astype(F32)
        t_imag = tmpl_ref[r, LEN:].astype(F32)
        prod = jnp.concatenate(
            [
                (t_real * real - t_imag * imag).astype(BF),
                (t_real * imag + t_imag * real).astype(BF),
            ],
            0,
        )
        line = jnp.dot(back_ref[...], prod, preferred_element_type=F32).astype(BF)
        mid_ref[r * EDGE : (r + 1) * EDGE, :FP] = line[:EDGE]
        mid_ref[r * EDGE : (r + 1) * EDGE, FP:] = line[EDGE:]
    corr = jnp.dot(mid_ref[...], inverse_ref[...], preferred_element_type=F32)
    best = corr[:EDGE]
    for r in range(1, NTPL):
        best = jnp.maximum(best, corr[r * EDGE : (r + 1) * EDGE])
    out_ref[0] = best * SCALE


VMEM = pl.BlockSpec(memory_space=pltpu.VMEM)
SMEM = pl.BlockSpec(memory_space=pltpu.SMEM)
HBM = pl.BlockSpec(memory_space=pltpu.HBM)


def limit(mib):
    return pltpu.CompilerParams(vmem_limit_bytes=mib << 20)


def cost(flops, nbytes):
    return pl.CostEstimate(flops=flops, bytes_accessed=nbytes, transcendentals=0)


def pinned(array):
    return pltpu.with_memory_space_constraint(array, pltpu.HBM)


def shape(*dims, dtype=BF):
    return jax.ShapeDtypeStruct(dims, dtype)


def solution(mesh):
    n_tile = mesh.shape["tile"]
    n_block = n_tile // XT
    n_det = NDET // n_tile
    depth = (NTILT * n_det + 127) // 128 * 128
    near_bit = n_block // 2
    masks = [k for k in range(1, n_block) if not k & near_bit]
    n_op = len(masks)
    pairs = pair_list(n_det)
    n_pair = sum(len(p) for p in pairs)
    tables = plane_tables()
    line, line_t, back = line_tables()
    mate = [(i, i ^ 1) for i in range(n_tile)]
    near_pairs = [(i, i ^ (near_bit * XT)) for i in range(n_tile)]

    def route(mask):
        return [(i, i ^ (mask * XT) ^ (near_bit * XT * (i % XT))) for i in range(n_tile)]

    def local(projections, tilt_angle, row_range, template_bank, rot_index):
        y_count = projections.shape[0]
        position = lax.axis_index("tile").astype(jnp.int32)
        at = jnp.stack([position // XT, position % XT])
        by_y = jnp.transpose(projections, (1, 2, 0))
        home, near, give, mine = pl.pallas_call(
            lambda *refs: pack_kernel(near_bit, masks, *refs),
            out_shape=(
                shape(LEN, depth),
                shape(LEN, depth),
                shape(1 + n_op, LEN, depth),
                shape(n_op, LEN, depth),
            ),
            in_specs=[SMEM, HBM, HBM],
            out_specs=(VMEM,) * 4,
            scratch_shapes=[
                pltpu.VMEM(by_y.shape, BF),
                pltpu.SMEM((2, NTILT), jnp.int32),
                pltpu.VMEM((y_count + 2 * HALO, depth), BF),
                pltpu.SemaphoreType.DMA((2,)),
            ],
            compiler_params=limit(8),
        )(at, pinned(row_range.T), pinned(by_y))
        got = lax.ppermute(give, "tile", mate)
        near_in = lax.ppermute(near, "tile", near_pairs)
        payload = pl.pallas_call(
            merge_kernel,
            out_shape=(shape(2, LEN, depth),) * n_op,
            in_specs=[VMEM, VMEM],
            out_specs=(VMEM,) * n_op,
            compiler_params=limit(8),
        )(mine, got)
        arrived = [lax.ppermute(p, "tile", route(m)) for p, m in zip(payload, masks)]
        turns = jnp.stack([jnp.cos(tilt_angle), jnp.sin(tilt_angle)])
        weights, plane, inverse, spectra, done = pl.pallas_call(
            lambda *refs: prepare_kernel(n_det, n_tile, pairs, *refs),
            out_shape=(
                shape(n_pair, depth, LB),
                shape(XR * Z, 2 * FP),
                shape(2 * FP, EDGE * EDGE),
                shape(NTPL, 2 * LEN, FP),
                shape(8, 128, dtype=F32),
            ),
            in_specs=[SMEM] + [HBM] * 9,
            out_specs=(VMEM,) * 5,
            scratch_shapes=[
                pltpu.VMEM((depth, LB), BF),
                pltpu.VMEM((depth, LB), BF),
                pltpu.SMEM((NTPL,), jnp.int32),
                pltpu.SMEM((2, NTILT), F32),
                pltpu.VMEM(template_bank.shape, BF),
                *[pltpu.VMEM(t.shape, F32) for t in tables[:4]],
                pltpu.VMEM(line_t.shape, BF),
                pltpu.VMEM(tables[4].shape, F32),
                pltpu.SemaphoreType.DMA((9,)),
            ],
            compiler_params=limit(28),
            cost_estimate=cost(1 << 32, 24 << 20),
        )(
            at,
            *[
                pinned(a)
                for a in (
                    turns,
                    rot_index,
                    template_bank,
                    *[jnp.asarray(t, F32) for t in tables[:4]],
                    jnp.asarray(line_t),
                    jnp.asarray(tables[4], F32),
                )
            ],
        )
        near_in, done, *arrived = lax.optimization_barrier((near_in, done, *arrived))
        near_swap = lax.ppermute(near_in, "tile", mate)
        swapped = [lax.ppermute(a, "tile", mate) for a in arrived]
        return pl.pallas_call(
            lambda *refs: score_kernel(near_bit, masks, pairs, n_tile, *refs),
            out_shape=shape(1, EDGE, EDGE * Z, dtype=F32),
            in_specs=[SMEM] + [VMEM] * (11 + 2 * n_op),
            out_specs=VMEM,
            scratch_shapes=[
                pltpu.VMEM((n_tile, LEN, depth), BF),
                pltpu.VMEM((LEN, XR * Z), BF),
                pltpu.VMEM((NTPL * EDGE, 2 * FP), BF),
            ],
            compiler_params=limit(28),
            cost_estimate=cost(4 << 30, 20 << 20),
        )(
            at,
            home,
            got,
            near_in,
            near_swap,
            *arrived,
            *swapped,
            weights,
            spectra,
            plane,
            jnp.asarray(line),
            jnp.asarray(back),
            inverse,
            done,
        )

    return jax.shard_map(
        local,
        mesh=mesh,
        in_specs=(P("grp", None, "tile"), P("grp"), P("grp", None), P(), P()),
        out_specs=P("tile", "grp", None),
        check_vma=False,
    )
```

```python
import math

import jax
import jax.numpy as jnp
import numpy as np
from jax import lax
from jax.experimental import pallas as pl
from jax.experimental.pallas import tpu as pltpu
from jax.sharding import PartitionSpec as P

EDGE = 32
XT = 2
K = 16
NTILT = 61
NTPL = 8
NDET = 128
HALO = K // 2
LEN = EDGE + K
X = XT * EDGE
Z = EDGE
XR = EDGE + HALO
LZ = Z + HALO
KZ = LZ // 2 + 1
NF = LEN * KZ
FP = 1024
VH = XR * Z // 2
OH = EDGE * EDGE // 2
XB = 8
NQ = XR // XB
LB = XB * Z
MAX_ANGLE = 1.05
VOXEL = 1.4
SCALE = 1.0 / (LEN * LEN * LZ)
BF = jnp.bfloat16
F32 = jnp.float32


def reach(q):
    x = np.arange(q * XB, (q + 1) * XB) - (X - 1) / 2.0
    z = np.arange(Z) - (Z - 1) / 2.0
    top = 0.0
    low = 0.0
    angle = np.linspace(-MAX_ANGLE, MAX_ANGLE, 4001)
    first = True
    for xv in (x[0], x[-1]):
        for zv in (z[0], z[-1]):
            pos = VOXEL * (xv * np.cos(angle) + zv * np.sin(angle)) + (NDET - 1) / 2.0
            low = pos.min() if first else min(low, pos.min())
            top = pos.max() if first else max(top, pos.max())
            first = False
    return math.ceil(low - 1.0 - 0.01), math.floor(top + 1.0 + 0.01)


def pair_list(n_det):
    pairs = []
    for q in range(NQ):
        low, top = reach(q)
        pairs.append(list(range(max(low, 0) // n_det, min(top, NDET - 1) // n_det + 1)))
    return pairs


def rounded(table):
    return np.asarray(table, np.float32).astype(jnp.bfloat16)


def plane_tables():
    kz = np.repeat(np.arange(KZ), LEN)
    kx = np.tile(np.arange(LEN), KZ)
    mid = (EDGE - 1) / 2.0

    def waves(k, at, length, width):
        p = 2.0 * np.pi * (np.outer(at, k) % length) / length
        out = np.zeros((2, len(at), width), np.float32)
        out[0, :, : len(k)], out[1, :, : len(k)] = np.cos(p), np.sin(p)
        return out

    vx = np.repeat(np.arange(EDGE // 2) - mid, EDGE)
    vz = np.tile(np.arange(EDGE) - mid, EDGE // 2)
    weight = np.full((KZ, 1), 2.0)
    weight[0] = weight[-1] = 1.0
    turn = np.zeros((2, XT, FP))
    for col in range(XT):
        back = HALO if col == 0 else 0
        p = 2.0 * np.pi * (kx * (mid - back) / LEN + kz * (mid - HALO) / LZ)
        turn[0, col, :NF], turn[1, col, :NF] = np.cos(p), np.sin(p)
    return (
        waves(kx, np.arange(XR // 2) - (XR - 1) / 2.0, LEN, FP),
        waves(kz, np.arange(Z) - (Z - 1) / 2.0, LZ, FP),
        waves(vx, np.arange(LEN // 2), LEN, OH),
        waves(vz, np.arange(KZ), LZ, OH) * weight,
        turn,
    )


def line_tables():
    def table(outs, ins, sign):
        p = 2.0 * np.pi * (np.outer(np.arange(outs), np.arange(ins)) % LEN) / LEN
        c, s = np.cos(p), np.sin(p) * sign
        return c, s

    c, s = table(LEN, LEN, 1.0)
    region = rounded(np.block([[c, s], [-s, c]]))
    c, s = table(LEN, K, 1.0)
    template = rounded(np.block([[c, s], [-s, c]]))
    c, s = table(EDGE, LEN, 1.0)
    back = rounded(np.block([[c, -s], [s, c]]))
    return region, template, back


def pack_kernel(
    near_bit,
    masks,
    at_ref,
    range_hbm,
    angle_hbm,
    proj_hbm,
    turns_ref,
    home_ref,
    near_ref,
    give_ref,
    mine_ref,
    proj_ref,
    angle_ref,
    range_ref,
    rows_ref,
    sem,
):
    fetch = [
        pltpu.make_async_copy(range_hbm, range_ref, sem.at[0]),
        pltpu.make_async_copy(angle_hbm, angle_ref, sem.at[1]),
        pltpu.make_async_copy(proj_hbm, proj_ref, sem.at[2]),
    ]
    for copy in fetch:
        copy.start()
    fetch[1].wait()
    turns_ref[0:1] = jnp.cos(angle_ref[...])
    turns_ref[1:2] = jnp.sin(angle_ref[...])
    fetch[0].wait()
    fetch[2].wait()
    n_tilt, n_det, y_count = proj_ref.shape
    depth = home_ref.shape[1]
    y = lax.broadcasted_iota(jnp.int32, (n_det, y_count), 1)
    parts = []
    for t in range(n_tilt):
        keep = (y >= range_ref[0, t]) & (y < range_ref[1, t])
        parts.append(jnp.where(keep, proj_ref[t].astype(F32), 0.0))
    if depth > n_tilt * n_det:
        parts.append(jnp.zeros((depth - n_tilt * n_det, y_count), F32))
    edge = jnp.zeros((HALO, depth), F32)
    rows_ref[...] = jnp.concatenate([edge, jnp.concatenate(parts, 0).T, edge], 0).astype(BF)
    chip, core = at_ref[0], at_ref[1]

    def rows(target):
        return rows_ref[pl.ds(pl.multiple_of(target * EDGE, EDGE), LEN)]

    home_ref[...] = rows(chip)
    near_ref[...] = rows(chip ^ near_bit)
    give_ref[0] = home_ref[...]
    for j, mask in enumerate(masks):
        mine_ref[j] = rows(chip ^ mask ^ (near_bit * core))
        give_ref[1 + j] = rows(chip ^ mask ^ (near_bit * (1 - core)))


def merge_kernel(mine_ref, got_ref, done_ref, *out_refs):
    done_ref[...] = jnp.zeros_like(done_ref)
    for j, out_ref in enumerate(out_refs):
        out_ref[0] = mine_ref[j]
        out_ref[1] = got_ref[1 + j]


def build_weights(n_det, n_tile, pairs, col, turns_ref, w_ref, whole_ref, part_ref):
    depth = whole_ref.shape[0]
    lane = lax.broadcasted_iota(jnp.int32, (n_det, LB), 1)
    step = lane // Z
    pack = 16 // n_det
    own = lax.broadcasted_iota(jnp.int32, (n_det, LB), 0).astype(F32)
    top = NTILT // pack * pack
    tail = depth - top * n_det
    base = 0
    for q, sources in enumerate(pairs):
        block = jnp.where(col == 0, q, NQ - 1 - q)
        flip = (block * LB + lane) >= VH
        x = jnp.where(flip, XB - 1 - step + jnp.where(block == NQ // 2, XB // 2, 0), step)
        x = x + (block * XB + col * (X - XR))
        x = VOXEL * (x.astype(F32) - (X - 1) / 2.0)
        z = jnp.where(flip, Z - 1 - lane % Z, lane % Z)
        z = VOXEL * (z.astype(F32) - (Z - 1) / 2.0)

        def tilt(t, z=z, x=x):
            pos = x * turns_ref[0, t] + z * turns_ref[1, t] + (NDET - 1) / 2.0
            whole = jnp.floor(pos)
            return own - whole, pos - whole

        for first in range(0, NTILT, pack):
            got = [tilt(t) for t in range(first, min(first + pack, NTILT))]
            rows = pack * n_det if first < top else tail
            gap = rows - len(got) * n_det
            for ref, values in ((whole_ref, [g[0] for g in got]), (part_ref, [g[1] for g in got])):
                if gap:
                    values.append(jnp.zeros((gap, LB), F32))
                ref[first * n_det : first * n_det + rows] = jnp.concatenate(values, 0).astype(BF)

        def build(j, carry, base=base, first=sources[0]):
            src = first + j
            src = jnp.where(col == 0, src, n_tile - 1 - src)
            shift = (src * n_det).astype(F32).astype(BF)
            off = (whole_ref[...] + shift) - part_ref[...]
            one = jnp.ones((), BF)
            w_ref[base + j] = jnp.maximum(one - jnp.abs(off), jnp.zeros((), BF))
            return carry

        lax.fori_loop(0, len(sources), build, 0)
        base += len(sources)


def build_planes(fx_ref, fz_ref, ix_ref, iz_ref, plane_ref, inverse_ref):
    def forward(x, carry):
        cos_x, sin_x = fx_ref[0, pl.ds(x, 1)], fx_ref[1, pl.ds(x, 1)]
        cos_z, sin_z = fz_ref[0], fz_ref[1]
        at = pl.ds(pl.multiple_of(x * Z, Z), Z)
        plane_ref[at, :FP] = (cos_x * cos_z - sin_x * sin_z).astype(BF)
        plane_ref[at, FP:] = (-sin_x * cos_z - cos_x * sin_z).astype(BF)
        return carry

    lax.fori_loop(0, XR // 2, forward, 0)
    odd = lax.broadcasted_iota(jnp.int32, (1, OH), 1) // EDGE % 2
    turn = 1.0 - 2.0 * odd.astype(F32)

    def inverse(k, carry):
        cos_z, sin_z = iz_ref[0, pl.ds(k, 1)], iz_ref[1, pl.ds(k, 1)]
        cos_x, sin_x = ix_ref[0], ix_ref[1]
        real = cos_x * cos_z - sin_x * sin_z
        imag = -sin_x * cos_z - cos_x * sin_z
        low = pl.multiple_of(k * LEN, 16)
        inverse_ref[pl.ds(low, LEN)] = jnp.concatenate([real, imag * turn], 0).astype(BF)
        inverse_ref[pl.ds(FP + low, LEN)] = jnp.concatenate([imag, -real * turn], 0).astype(BF)
        return carry

    lax.fori_loop(0, KZ, inverse, 0)
    inverse_ref[NF:FP] = jnp.zeros((FP - NF, OH), BF)
    inverse_ref[FP + NF :] = jnp.zeros((FP - NF, OH), BF)


def build_templates(col, rot_ref, bank_ref, plane_ref, line_ref, turn_ref, out_ref):
    chosen = jnp.concatenate([bank_ref[rot_ref[r]] for r in range(NTPL)], 0)
    plane = jnp.concatenate([plane_ref[b * Z : b * Z + K] for b in range(K)], 0)
    flat = jnp.dot(chosen, plane, preferred_element_type=F32).astype(BF)
    cos = jnp.where(col == 0, turn_ref[0, 0:1], turn_ref[0, 1:2])
    sin = jnp.where(col == 0, turn_ref[1, 0:1], turn_ref[1, 1:2])
    for r in range(NTPL):
        part = flat[r * K : (r + 1) * K]
        stacked = jnp.concatenate([part[:, :FP], part[:, FP:]], 0)
        full = jnp.dot(line_ref[...], stacked, preferred_element_type=F32)
        real, imag = full[:LEN], -full[LEN:]
        out_ref[r, :LEN] = (real * cos - imag * sin).astype(BF)
        out_ref[r, LEN:] = (real * sin + imag * cos).astype(BF)


def weight_kernel(n_det, n_tile, pairs, at_ref, turns_ref, _, w_ref, done_ref, whole_ref, part_ref):
    build_weights(n_det, n_tile, pairs, at_ref[1], turns_ref, w_ref, whole_ref, part_ref)
    done_ref[...] = jnp.zeros_like(done_ref)


def table_kernel(at_ref, _, *refs):
    sources, outs, targets, sem = refs[:8], refs[8:12], refs[12:20], refs[20]
    fetch = [
        pltpu.make_async_copy(a, b, sem.at[i]) for i, (a, b) in enumerate(zip(sources, targets))
    ]
    for copy in fetch:
        copy.start()
    for copy in fetch:
        copy.wait()
    rot_ref, bank_ref, fx_ref, fz_ref, ix_ref, iz_ref, line_ref, turn_ref = targets
    plane_ref, inverse_ref, tmpl_ref, done_ref = outs
    build_planes(fx_ref, fz_ref, ix_ref, iz_ref, plane_ref, inverse_ref)
    build_templates(at_ref[1], rot_ref, bank_ref, plane_ref, line_ref, turn_ref, tmpl_ref)
    done_ref[...] = jnp.zeros_like(done_ref)


def score_kernel(near_bit, masks, pairs, n_tile, *refs):
    n_op = len(masks)
    at_ref, home_ref, got_ref, near_ref, near_swap_ref = refs[:5]
    recv_refs, swap_refs = refs[5 : 5 + n_op], refs[5 + n_op : 5 + 2 * n_op]
    w_ref, tmpl_ref, plane_ref, line_ref, back_ref, inverse_ref = refs[5 + 2 * n_op : 11 + 2 * n_op]
    _, _, out_ref, data_ref, vol_ref, mid_ref = refs[11 + 2 * n_op :]
    chip, core = at_ref[0], at_ref[1]
    mate = 1 - core
    data_ref[chip * XT + core] = home_ref[...]
    data_ref[chip * XT + mate] = got_ref[0]
    data_ref[(chip ^ near_bit) * XT + core] = near_ref[...]
    data_ref[(chip ^ near_bit) * XT + mate] = near_swap_ref[...]
    for j, mask in enumerate(masks):
        here = (chip ^ mask ^ (near_bit * core)) * XT
        there = (chip ^ mask ^ (near_bit * mate)) * XT
        data_ref[here + core] = recv_refs[j][0]
        data_ref[here + mate] = recv_refs[j][1]
        data_ref[there + mate] = swap_refs[j][0]
        data_ref[there + core] = swap_refs[j][1]
    base = 0
    for q, sources in enumerate(pairs):
        total = jnp.zeros((LEN, LB), F32)
        for j, src in enumerate(sources):
            part = data_ref[jnp.where(core == 0, src, n_tile - 1 - src)]
            total += jnp.dot(part, w_ref[base + j], preferred_element_type=F32)
        base += len(sources)
        block = jnp.where(core == 0, q, NQ - 1 - q)
        vol_ref[:, pl.ds(pl.multiple_of(block * LB, LB), LB)] = total
    near_half = vol_ref[:, :VH]
    far_half = jnp.concatenate(
        [vol_ref[:, 4 * LB :], vol_ref[:, 3 * LB : 4 * LB], vol_ref[:, VH : 3 * LB]], 1
    )
    even, odd = (near_half + far_half).astype(BF), (near_half - far_half).astype(BF)
    stacked = jnp.concatenate(
        [
            jnp.dot(even, plane_ref[:, :FP], preferred_element_type=F32).astype(BF),
            jnp.dot(odd, plane_ref[:, FP:], preferred_element_type=F32).astype(BF),
        ],
        0,
    )
    full = jnp.dot(line_ref[...], stacked, preferred_element_type=F32)
    real, imag = full[:LEN], full[LEN:]
    for r in range(NTPL):
        t_real = tmpl_ref[r, :LEN].astype(F32)
        t_imag = tmpl_ref[r, LEN:].astype(F32)
        prod = jnp.concatenate(
            [
                (t_real * real - t_imag * imag).astype(BF),
                (t_real * imag + t_imag * real).astype(BF),
            ],
            0,
        )
        line = jnp.dot(back_ref[...], prod, preferred_element_type=F32).astype(BF)
        mid_ref[r * EDGE : (r + 1) * EDGE, :FP] = line[:EDGE]
        mid_ref[r * EDGE : (r + 1) * EDGE, FP:] = line[EDGE:]
    even = jnp.dot(mid_ref[:, :FP], inverse_ref[:FP], preferred_element_type=F32)
    odd = jnp.dot(mid_ref[:, FP:], inverse_ref[FP:], preferred_element_type=F32)
    best = even[:EDGE] + odd[:EDGE]
    mirrored = even[:EDGE] - odd[:EDGE]
    for r in range(1, NTPL):
        at = slice(r * EDGE, (r + 1) * EDGE)
        best = jnp.maximum(best, even[at] + odd[at])
        mirrored = jnp.maximum(mirrored, even[at] - odd[at])
    out_ref[0, :, :OH] = best * SCALE
    mirrored = mirrored * SCALE
    order = 127 - lax.broadcasted_iota(jnp.int32, (EDGE, 128), 1)
    for low in range(0, OH, 128):
        part = jnp.take_along_axis(mirrored[:, low : low + 128], order, axis=1)
        out_ref[0, :, 2 * OH - 128 - low : 2 * OH - low] = part


VMEM = pl.BlockSpec(memory_space=pltpu.VMEM)
SMEM = pl.BlockSpec(memory_space=pltpu.SMEM)
HBM = pl.BlockSpec(memory_space=pltpu.HBM)


def limit(mib):
    return pltpu.CompilerParams(vmem_limit_bytes=mib << 20)


def cost(flops, nbytes):
    return pl.CostEstimate(flops=flops, bytes_accessed=nbytes, transcendentals=0)


def pinned(array):
    return pltpu.with_memory_space_constraint(array, pltpu.HBM)


def shape(*dims, dtype=BF):
    return jax.ShapeDtypeStruct(dims, dtype)


def solution(mesh):
    n_tile = mesh.shape["tile"]
    n_block = n_tile // XT
    n_det = NDET // n_tile
    depth = (NTILT * n_det + 127) // 128 * 128
    near_bit = n_block // 2
    masks = [k for k in range(1, n_block) if not k & near_bit]
    n_op = len(masks)
    pairs = pair_list(n_det)
    n_pair = sum(len(p) for p in pairs)
    tables = plane_tables()
    line, line_t, back = line_tables()
    mate = [(i, i ^ 1) for i in range(n_tile)]
    near_pairs = [(i, i ^ (near_bit * XT)) for i in range(n_tile)]

    def route(mask):
        return [(i, i ^ (mask * XT) ^ (near_bit * XT * (i % XT))) for i in range(n_tile)]

    def local(projections, tilt_angle, row_range, template_bank, rot_index):
        y_count = projections.shape[0]
        position = lax.axis_index("tile").astype(jnp.int32)
        at = jnp.stack([position // XT, position % XT])
        by_y = jnp.transpose(projections, (1, 2, 0))
        turns, home, near, give, mine = pl.pallas_call(
            lambda *refs: pack_kernel(near_bit, masks, *refs),
            out_shape=(
                shape(2, NTILT, dtype=F32),
                shape(LEN, depth),
                shape(LEN, depth),
                shape(1 + n_op, LEN, depth),
                shape(n_op, LEN, depth),
            ),
            in_specs=[SMEM, HBM, HBM, HBM],
            out_specs=(VMEM,) * 5,
            scratch_shapes=[
                pltpu.VMEM(by_y.shape, BF),
                pltpu.VMEM((1, NTILT), F32),
                pltpu.SMEM((2, NTILT), jnp.int32),
                pltpu.VMEM((y_count + 2 * HALO, depth), BF),
                pltpu.SemaphoreType.DMA((3,)),
            ],
            compiler_params=limit(8),
        )(at, pinned(row_range.T), pinned(tilt_angle.reshape(1, NTILT)), pinned(by_y))
        got = lax.ppermute(give, "tile", mate)
        near_in = lax.ppermute(near, "tile", near_pairs)
        merged, *payload = pl.pallas_call(
            merge_kernel,
            out_shape=(shape(8, 128, dtype=F32),) + (shape(2, LEN, depth),) * n_op,
            in_specs=[VMEM, VMEM],
            out_specs=(VMEM,) * (1 + n_op),
            compiler_params=limit(8),
        )(mine, got)
        arrived = [lax.ppermute(p, "tile", route(m)) for p, m in zip(payload, masks)]
        weights, done_w = pl.pallas_call(
            lambda *refs: weight_kernel(n_det, n_tile, pairs, *refs),
            out_shape=(shape(n_pair, depth, LB), shape(8, 128, dtype=F32)),
            in_specs=[SMEM, SMEM, VMEM],
            out_specs=(VMEM,) * 2,
            scratch_shapes=[pltpu.VMEM((depth, LB), BF)] * 2,
            compiler_params=limit(16),
            cost_estimate=cost(1 << 32, 9 << 20),
        )(at, turns, merged)
        last = arrived[-1]
        near_in, done_w, *arrived = lax.optimization_barrier((near_in, done_w, *arrived[:-1]))
        constants = (
            rot_index,
            template_bank,
            *[jnp.asarray(t, F32) for t in tables[:4]],
            jnp.asarray(line_t),
            jnp.asarray(tables[4], F32),
        )
        plane, inverse, spectra, done_t = pl.pallas_call(
            table_kernel,
            out_shape=(
                shape(VH, 2 * FP),
                shape(2 * FP, OH),
                shape(NTPL, 2 * LEN, FP),
                shape(8, 128, dtype=F32),
            ),
            in_specs=[SMEM, VMEM] + [HBM] * 8,
            out_specs=(VMEM,) * 4,
            scratch_shapes=[
                pltpu.SMEM((NTPL,), jnp.int32),
                *[pltpu.VMEM(c.shape, c.dtype) for c in constants[1:]],
                pltpu.SemaphoreType.DMA((8,)),
            ],
            compiler_params=limit(20),
            cost_estimate=cost(1 << 32, 8 << 20),
        )(at, done_w, *[pinned(c) for c in constants])
        last, done_t = lax.optimization_barrier((last, done_t))
        arrived.append(last)
        near_swap = lax.ppermute(near_in, "tile", mate)
        swapped = [lax.ppermute(a, "tile", mate) for a in arrived]
        return pl.pallas_call(
            lambda *refs: score_kernel(near_bit, masks, pairs, n_tile, *refs),
            out_shape=shape(1, EDGE, EDGE * Z, dtype=F32),
            in_specs=[SMEM] + [VMEM] * (12 + 2 * n_op),
            out_specs=VMEM,
            scratch_shapes=[
                pltpu.VMEM((n_tile, LEN, depth), BF),
                pltpu.VMEM((LEN, XR * Z), F32),
                pltpu.VMEM((NTPL * EDGE, 2 * FP), BF),
            ],
            compiler_params=limit(28),
            cost_estimate=cost(4 << 30, 20 << 20),
        )(
            at,
            home,
            got,
            near_in,
            near_swap,
            *arrived,
            *swapped,
            weights,
            spectra,
            plane,
            jnp.asarray(line),
            jnp.asarray(back),
            inverse,
            done_w,
            done_t,
        )

    return jax.shard_map(
        local,
        mesh=mesh,
        in_specs=(P("grp", None, "tile"), P("grp"), P("grp", None), P(), P()),
        out_specs=P("tile", "grp", None),
        check_vma=False,
    )
```

```python
import math

import jax
import jax.numpy as jnp
import numpy as np
from jax import lax
from jax.experimental import pallas as pl
from jax.experimental.pallas import tpu as pltpu
from jax.sharding import PartitionSpec as P

EDGE = 32
XT = 2
K = 16
NTILT = 61
NTPL = 8
NDET = 128
HALO = K // 2
LEN = EDGE + K
X = XT * EDGE
Z = EDGE
XR = EDGE + HALO
LZ = Z + HALO
KZ = LZ // 2 + 1
NF = LEN * KZ
FP = 1024
VH = XR * Z // 2
OH = EDGE * EDGE // 2
XB = 8
NQ = XR // XB
LB = XB * Z
MAX_ANGLE = 1.05
VOXEL = 1.4
SCALE = 1.0 / (LEN * LEN * LZ)
BF = jnp.bfloat16
F32 = jnp.float32


def reach(q):
    x = np.arange(q * XB, (q + 1) * XB) - (X - 1) / 2.0
    z = np.arange(Z) - (Z - 1) / 2.0
    top = 0.0
    low = 0.0
    angle = np.linspace(-MAX_ANGLE, MAX_ANGLE, 4001)
    first = True
    for xv in (x[0], x[-1]):
        for zv in (z[0], z[-1]):
            pos = VOXEL * (xv * np.cos(angle) + zv * np.sin(angle)) + (NDET - 1) / 2.0
            low = pos.min() if first else min(low, pos.min())
            top = pos.max() if first else max(top, pos.max())
            first = False
    return math.ceil(low - 1.0 - 0.01), math.floor(top + 1.0 + 0.01)


def pair_list(n_det):
    pairs = []
    for q in range(NQ):
        low, top = reach(q)
        pairs.append(list(range(max(low, 0) // n_det, min(top, NDET - 1) // n_det + 1)))
    return pairs


def rounded(table):
    return np.asarray(table, np.float32).astype(jnp.bfloat16)


def plane_tables():
    kz = np.repeat(np.arange(KZ), LEN)
    kx = np.tile(np.arange(LEN), KZ)
    mid = (EDGE - 1) / 2.0

    def waves(k, at, length, width):
        p = 2.0 * np.pi * (np.outer(at, k) % length) / length
        out = np.zeros((2, len(at), width), np.float32)
        out[0, :, : len(k)], out[1, :, : len(k)] = np.cos(p), np.sin(p)
        return out

    vx = np.repeat(np.arange(EDGE // 2) - mid, EDGE)
    vz = np.tile(np.arange(EDGE) - mid, EDGE // 2)
    weight = np.full((KZ, 1), 2.0)
    weight[0] = weight[-1] = 1.0
    turn = np.zeros((2, XT, FP))
    for col in range(XT):
        back = HALO if col == 0 else 0
        p = 2.0 * np.pi * (kx * (mid - back) / LEN + kz * (mid - HALO) / LZ)
        turn[0, col, :NF], turn[1, col, :NF] = np.cos(p), np.sin(p)
    return (
        waves(kx, np.arange(XR // 2) - (XR - 1) / 2.0, LEN, FP),
        waves(kz, np.arange(Z) - (Z - 1) / 2.0, LZ, FP),
        waves(vx, np.arange(LEN // 2), LEN, OH),
        waves(vz, np.arange(KZ), LZ, OH) * weight,
        turn,
    )


def line_tables():
    def table(outs, ins, sign):
        p = 2.0 * np.pi * (np.outer(np.arange(outs), np.arange(ins)) % LEN) / LEN
        c, s = np.cos(p), np.sin(p) * sign
        return c, s

    c, s = table(LEN, LEN, 1.0)
    region = rounded(np.block([[c, s], [-s, c]]))
    c, s = table(LEN, K, 1.0)
    template = rounded(np.block([[c, s], [-s, c]]))
    c, s = table(EDGE, LEN, 1.0)
    back = rounded(np.block([[c, -s], [s, c]]))
    return region, template, back


def pack_kernel(
    near_bit,
    masks,
    at_ref,
    range_hbm,
    angle_hbm,
    proj_hbm,
    turns_ref,
    home_ref,
    near_ref,
    give_ref,
    mine_ref,
    proj_ref,
    angle_ref,
    range_ref,
    rows_ref,
    sem,
):
    fetch = [
        pltpu.make_async_copy(range_hbm, range_ref, sem.at[0]),
        pltpu.make_async_copy(angle_hbm, angle_ref, sem.at[1]),
        pltpu.make_async_copy(proj_hbm, proj_ref, sem.at[2]),
    ]
    for copy in fetch:
        copy.start()
    fetch[1].wait()
    turns_ref[0:1] = jnp.cos(angle_ref[...])
    turns_ref[1:2] = jnp.sin(angle_ref[...])
    fetch[0].wait()
    fetch[2].wait()
    n_tilt, n_det, y_count = proj_ref.shape
    depth = home_ref.shape[1]
    y = lax.broadcasted_iota(jnp.int32, (n_det, y_count), 1)
    parts = []
    for t in range(n_tilt):
        keep = (y >= range_ref[0, t]) & (y < range_ref[1, t])
        parts.append(jnp.where(keep, proj_ref[t].astype(F32), 0.0))
    if depth > n_tilt * n_det:
        parts.append(jnp.zeros((depth - n_tilt * n_det, y_count), F32))
    edge = jnp.zeros((HALO, depth), F32)
    rows_ref[...] = jnp.concatenate([edge, jnp.concatenate(parts, 0).T, edge], 0).astype(BF)
    chip, core = at_ref[0], at_ref[1]

    def rows(target):
        return rows_ref[pl.ds(pl.multiple_of(target * EDGE, EDGE), LEN)]

    home_ref[...] = rows(chip)
    near_ref[...] = rows(chip ^ near_bit)
    give_ref[0] = home_ref[...]
    for j, mask in enumerate(masks):
        mine_ref[j] = rows(chip ^ mask ^ (near_bit * core))
        give_ref[1 + j] = rows(chip ^ mask ^ (near_bit * (1 - core)))


def merge_kernel(mine_ref, got_ref, done_ref, *out_refs):
    done_ref[...] = jnp.zeros_like(done_ref)
    for j, out_ref in enumerate(out_refs):
        out_ref[0] = mine_ref[j]
        out_ref[1] = got_ref[1 + j]


def build_weights(n_det, n_tile, pairs, col, turns_ref, w_ref, whole_ref, part_ref):
    depth = whole_ref.shape[0]
    lane = lax.broadcasted_iota(jnp.int32, (n_det, LB), 1)
    step = lane // Z
    pack = 16 // n_det
    own = lax.broadcasted_iota(jnp.int32, (n_det, LB), 0).astype(F32)
    top = NTILT // pack * pack
    tail = depth - top * n_det
    base = 0
    for q, sources in enumerate(pairs):
        block = jnp.where(col == 0, q, NQ - 1 - q)
        flip = (block * LB + lane) >= VH
        x = jnp.where(flip, XB - 1 - step + jnp.where(block == NQ // 2, XB // 2, 0), step)
        x = x + (block * XB + col * (X - XR))
        x = VOXEL * (x.astype(F32) - (X - 1) / 2.0)
        z = jnp.where(flip, Z - 1 - lane % Z, lane % Z)
        z = VOXEL * (z.astype(F32) - (Z - 1) / 2.0)

        def tilt(t, z=z, x=x):
            pos = x * turns_ref[0, t] + z * turns_ref[1, t] + (NDET - 1) / 2.0
            whole = jnp.floor(pos)
            return own - whole, pos - whole

        for first in range(0, NTILT, pack):
            got = [tilt(t) for t in range(first, min(first + pack, NTILT))]
            rows = pack * n_det if first < top else tail
            gap = rows - len(got) * n_det
            for ref, values in ((whole_ref, [g[0] for g in got]), (part_ref, [g[1] for g in got])):
                if gap:
                    values.append(jnp.zeros((gap, LB), F32))
                ref[first * n_det : first * n_det + rows] = jnp.concatenate(values, 0).astype(BF)

        def build(j, carry, base=base, first=sources[0]):
            src = first + j
            src = jnp.where(col == 0, src, n_tile - 1 - src)
            shift = (src * n_det).astype(F32).astype(BF)
            off = (whole_ref[...] + shift) - part_ref[...]
            one = jnp.ones((), BF)
            w_ref[base + j] = jnp.maximum(one - jnp.abs(off), jnp.zeros((), BF))
            return carry

        lax.fori_loop(0, len(sources), build, 0)
        base += len(sources)


def build_planes(fx_ref, fz_ref, ix_ref, iz_ref, plane_ref, inverse_ref):
    def forward(x, carry):
        cos_x, sin_x = fx_ref[0, pl.ds(x, 1)], fx_ref[1, pl.ds(x, 1)]
        cos_z, sin_z = fz_ref[0], fz_ref[1]
        at = pl.ds(pl.multiple_of(x * Z, Z), Z)
        plane_ref[at, :FP] = (cos_x * cos_z - sin_x * sin_z).astype(BF)
        plane_ref[at, FP:] = (-sin_x * cos_z - cos_x * sin_z).astype(BF)
        return carry

    lax.fori_loop(0, XR // 2, forward, 0)
    odd = lax.broadcasted_iota(jnp.int32, (1, OH), 1) // EDGE % 2
    turn = 1.0 - 2.0 * odd.astype(F32)

    def inverse(k, carry):
        cos_z, sin_z = iz_ref[0, pl.ds(k, 1)], iz_ref[1, pl.ds(k, 1)]
        cos_x, sin_x = ix_ref[0], ix_ref[1]
        real = cos_x * cos_z - sin_x * sin_z
        imag = -sin_x * cos_z - cos_x * sin_z
        low = pl.multiple_of(k * LEN, 16)
        inverse_ref[pl.ds(low, LEN)] = jnp.concatenate([real, imag * turn], 0).astype(BF)
        inverse_ref[pl.ds(FP + low, LEN)] = jnp.concatenate([imag, -real * turn], 0).astype(BF)
        return carry

    lax.fori_loop(0, KZ, inverse, 0)
    inverse_ref[NF:FP] = jnp.zeros((FP - NF, OH), BF)
    inverse_ref[FP + NF :] = jnp.zeros((FP - NF, OH), BF)


def build_templates(col, rot_ref, bank_ref, plane_ref, line_ref, turn_ref, out_ref):
    chosen = jnp.concatenate([bank_ref[rot_ref[r]] for r in range(NTPL)], 0)
    plane = jnp.concatenate([plane_ref[b * Z : b * Z + K] for b in range(K)], 0)
    flat = jnp.dot(chosen, plane, preferred_element_type=F32).astype(BF)
    cos = jnp.where(col == 0, turn_ref[0, 0:1], turn_ref[0, 1:2])
    sin = jnp.where(col == 0, turn_ref[1, 0:1], turn_ref[1, 1:2])
    for r in range(NTPL):
        part = flat[r * K : (r + 1) * K]
        stacked = jnp.concatenate([part[:, :FP], part[:, FP:]], 0)
        full = jnp.dot(line_ref[...], stacked, preferred_element_type=F32)
        real, imag = full[:LEN], -full[LEN:]
        out_ref[r, :LEN] = (real * cos - imag * sin).astype(BF)
        out_ref[r, LEN:] = (real * sin + imag * cos).astype(BF)


def prepare_kernel(n_det, n_tile, pairs, at_ref, turns_ref, _, *refs):
    sources, outs, targets, (sem, whole_ref, part_ref) = refs[:8], refs[8:13], refs[13:21], refs[21:]
    fetch = [
        pltpu.make_async_copy(a, b, sem.at[i]) for i, (a, b) in enumerate(zip(sources, targets))
    ]
    for copy in fetch:
        copy.start()
    w_ref, plane_ref, inverse_ref, tmpl_ref, done_ref = outs
    col = at_ref[1]
    build_weights(n_det, n_tile, pairs, col, turns_ref, w_ref, whole_ref, part_ref)
    for copy in fetch:
        copy.wait()
    rot_ref, bank_ref, fx_ref, fz_ref, ix_ref, iz_ref, line_ref, turn_ref = targets
    build_planes(fx_ref, fz_ref, ix_ref, iz_ref, plane_ref, inverse_ref)
    build_templates(col, rot_ref, bank_ref, plane_ref, line_ref, turn_ref, tmpl_ref)
    done_ref[...] = jnp.zeros_like(done_ref)


def score_kernel(near_bit, masks, pairs, n_tile, *refs):
    n_op = len(masks)
    at_ref, home_ref, got_ref, near_ref, near_swap_ref = refs[:5]
    recv_refs, swap_refs = refs[5 : 5 + n_op], refs[5 + n_op : 5 + 2 * n_op]
    w_ref, tmpl_ref, plane_ref, line_ref, back_ref, inverse_ref = refs[5 + 2 * n_op : 11 + 2 * n_op]
    _, out_ref, data_ref, vol_ref, mid_ref = refs[11 + 2 * n_op :]
    chip, core = at_ref[0], at_ref[1]
    mate = 1 - core
    data_ref[chip * XT + core] = home_ref[...]
    data_ref[chip * XT + mate] = got_ref[0]
    data_ref[(chip ^ near_bit) * XT + core] = near_ref[...]
    data_ref[(chip ^ near_bit) * XT + mate] = near_swap_ref[...]
    for j, mask in enumerate(masks):
        here = (chip ^ mask ^ (near_bit * core)) * XT
        there = (chip ^ mask ^ (near_bit * mate)) * XT
        data_ref[here + core] = recv_refs[j][0]
        data_ref[here + mate] = recv_refs[j][1]
        data_ref[there + mate] = swap_refs[j][0]
        data_ref[there + core] = swap_refs[j][1]
    base = 0
    for q, sources in enumerate(pairs):
        total = jnp.zeros((LEN, LB), F32)
        for j, src in enumerate(sources):
            part = data_ref[jnp.where(core == 0, src, n_tile - 1 - src)]
            total += jnp.dot(part, w_ref[base + j], preferred_element_type=F32)
        base += len(sources)
        block = jnp.where(core == 0, q, NQ - 1 - q)
        vol_ref[:, pl.ds(pl.multiple_of(block * LB, LB), LB)] = total
    near_half = vol_ref[:, :VH]
    far_half = jnp.concatenate(
        [vol_ref[:, 4 * LB :], vol_ref[:, 3 * LB : 4 * LB], vol_ref[:, VH : 3 * LB]], 1
    )
    even, odd = (near_half + far_half).astype(BF), (near_half - far_half).astype(BF)
    stacked = jnp.concatenate(
        [
            jnp.dot(even, plane_ref[:, :FP], preferred_element_type=F32).astype(BF),
            jnp.dot(odd, plane_ref[:, FP:], preferred_element_type=F32).astype(BF),
        ],
        0,
    )
    full = jnp.dot(line_ref[...], stacked, preferred_element_type=F32)
    real, imag = full[:LEN], full[LEN:]
    for r in range(NTPL):
        t_real = tmpl_ref[r, :LEN].astype(F32)
        t_imag = tmpl_ref[r, LEN:].astype(F32)
        prod = jnp.concatenate(
            [
                (t_real * real - t_imag * imag).astype(BF),
                (t_real * imag + t_imag * real).astype(BF),
            ],
            0,
        )
        line = jnp.dot(back_ref[...], prod, preferred_element_type=F32).astype(BF)
        mid_ref[r * EDGE : (r + 1) * EDGE, :FP] = line[:EDGE]
        mid_ref[r * EDGE : (r + 1) * EDGE, FP:] = line[EDGE:]
    even = jnp.dot(mid_ref[:, :FP], inverse_ref[:FP], preferred_element_type=F32)
    odd = jnp.dot(mid_ref[:, FP:], inverse_ref[FP:], preferred_element_type=F32)
    best = even[:EDGE] + odd[:EDGE]
    mirrored = even[:EDGE] - odd[:EDGE]
    for r in range(1, NTPL):
        at = slice(r * EDGE, (r + 1) * EDGE)
        best = jnp.maximum(best, even[at] + odd[at])
        mirrored = jnp.maximum(mirrored, even[at] - odd[at])
    out_ref[0, :, :OH] = best * SCALE
    mirrored = mirrored * SCALE
    order = 127 - lax.broadcasted_iota(jnp.int32, (EDGE, 128), 1)
    for low in range(0, OH, 128):
        part = jnp.take_along_axis(mirrored[:, low : low + 128], order, axis=1)
        out_ref[0, :, 2 * OH - 128 - low : 2 * OH - low] = part


VMEM = pl.BlockSpec(memory_space=pltpu.VMEM)
SMEM = pl.BlockSpec(memory_space=pltpu.SMEM)
HBM = pl.BlockSpec(memory_space=pltpu.HBM)


def limit(mib):
    return pltpu.CompilerParams(vmem_limit_bytes=mib << 20)


def cost(flops, nbytes):
    return pl.CostEstimate(flops=flops, bytes_accessed=nbytes, transcendentals=0)


def pinned(array):
    return pltpu.with_memory_space_constraint(array, pltpu.HBM)


def shape(*dims, dtype=BF):
    return jax.ShapeDtypeStruct(dims, dtype)


def solution(mesh):
    n_tile = mesh.shape["tile"]
    n_block = n_tile // XT
    n_det = NDET // n_tile
    depth = (NTILT * n_det + 127) // 128 * 128
    near_bit = n_block // 2
    masks = [k for k in range(1, n_block) if not k & near_bit]
    n_op = len(masks)
    pairs = pair_list(n_det)
    n_pair = sum(len(p) for p in pairs)
    tables = plane_tables()
    line, line_t, back = line_tables()
    mate = [(i, i ^ 1) for i in range(n_tile)]
    near_pairs = [(i, i ^ (near_bit * XT)) for i in range(n_tile)]

    def route(mask):
        return [(i, i ^ (mask * XT) ^ (near_bit * XT * (i % XT))) for i in range(n_tile)]

    def local(projections, tilt_angle, row_range, template_bank, rot_index):
        y_count = projections.shape[0]
        position = lax.axis_index("tile").astype(jnp.int32)
        at = jnp.stack([position // XT, position % XT])
        by_y = jnp.transpose(projections, (1, 2, 0))
        turns, home, near, give, mine = pl.pallas_call(
            lambda *refs: pack_kernel(near_bit, masks, *refs),
            out_shape=(
                shape(2, NTILT, dtype=F32),
                shape(LEN, depth),
                shape(LEN, depth),
                shape(1 + n_op, LEN, depth),
                shape(n_op, LEN, depth),
            ),
            in_specs=[SMEM, HBM, HBM, HBM],
            out_specs=(VMEM,) * 5,
            scratch_shapes=[
                pltpu.VMEM(by_y.shape, BF),
                pltpu.VMEM((1, NTILT), F32),
                pltpu.SMEM((2, NTILT), jnp.int32),
                pltpu.VMEM((y_count + 2 * HALO, depth), BF),
                pltpu.SemaphoreType.DMA((3,)),
            ],
            compiler_params=limit(8),
        )(at, pinned(row_range.T), pinned(tilt_angle.reshape(1, NTILT)), pinned(by_y))
        got = lax.ppermute(give, "tile", mate)
        near_in = lax.ppermute(near, "tile", near_pairs)
        merged, *payload = pl.pallas_call(
            merge_kernel,
            out_shape=(shape(8, 128, dtype=F32),) + (shape(2, LEN, depth),) * n_op,
            in_specs=[VMEM, VMEM],
            out_specs=(VMEM,) * (1 + n_op),
            compiler_params=limit(8),
        )(mine, got)
        arrived = [lax.ppermute(p, "tile", route(m)) for p, m in zip(payload, masks)]
        constants = (
            rot_index,
            template_bank,
            *[jnp.asarray(t, F32) for t in tables[:4]],
            jnp.asarray(line_t),
            jnp.asarray(tables[4], F32),
        )
        weights, plane, inverse, spectra, done = pl.pallas_call(
            lambda *refs: prepare_kernel(n_det, n_tile, pairs, *refs),
            out_shape=(
                shape(n_pair, depth, LB),
                shape(VH, 2 * FP),
                shape(2 * FP, OH),
                shape(NTPL, 2 * LEN, FP),
                shape(8, 128, dtype=F32),
            ),
            in_specs=[SMEM, SMEM, VMEM] + [HBM] * 8,
            out_specs=(VMEM,) * 5,
            scratch_shapes=[
                pltpu.SMEM((NTPL,), jnp.int32),
                *[pltpu.VMEM(c.shape, c.dtype) for c in constants[1:]],
                pltpu.SemaphoreType.DMA((8,)),
                pltpu.VMEM((depth, LB), BF),
                pltpu.VMEM((depth, LB), BF),
            ],
            compiler_params=limit(24),
            cost_estimate=cost(1 << 32, 16 << 20),
        )(at, turns, merged, *[pinned(c) for c in constants])
        near_in, done, *arrived = lax.optimization_barrier((near_in, done, *arrived))
        near_swap = lax.ppermute(near_in, "tile", mate)
        swapped = [lax.ppermute(a, "tile", mate) for a in arrived]
        return pl.pallas_call(
            lambda *refs: score_kernel(near_bit, masks, pairs, n_tile, *refs),
            out_shape=shape(1, EDGE, EDGE * Z, dtype=F32),
            in_specs=[SMEM] + [VMEM] * (11 + 2 * n_op),
            out_specs=VMEM,
            scratch_shapes=[
                pltpu.VMEM((n_tile, LEN, depth), BF),
                pltpu.VMEM((LEN, XR * Z), F32),
                pltpu.VMEM((NTPL * EDGE, 2 * FP), BF),
            ],
            compiler_params=limit(28),
            cost_estimate=cost(4 << 30, 20 << 20),
        )(
            at,
            home,
            got,
            near_in,
            near_swap,
            *arrived,
            *swapped,
            weights,
            spectra,
            plane,
            jnp.asarray(line),
            jnp.asarray(back),
            inverse,
            done,
        )

    return jax.shard_map(
        local,
        mesh=mesh,
        in_specs=(P("grp", None, "tile"), P("grp"), P("grp", None), P(), P()),
        out_specs=P("tile", "grp", None),
        check_vma=False,
    )
```

```python
import math

import jax
import jax.numpy as jnp
import numpy as np
from jax import lax
from jax.experimental import pallas as pl
from jax.experimental.pallas import tpu as pltpu
from jax.sharding import PartitionSpec as P

EDGE = 32
XT = 2
K = 16
NTILT = 61
NTPL = 8
NDET = 128
HALO = K // 2
LEN = EDGE + K
X = XT * EDGE
Z = EDGE
XR = EDGE + HALO
LZ = Z + HALO
KZ = LZ // 2 + 1
NF = LEN * KZ
FP = 1024
TB = 4
PB = 2
VH = XR * Z // 2
OH = EDGE * EDGE // 2
XB = 8
NQ = XR // XB
LB = XB * Z
MAX_ANGLE = 1.05
VOXEL = 1.4
SCALE = 1.0 / (LEN * LEN * LZ)
BF = jnp.bfloat16
F32 = jnp.float32


def reach(q):
    x = np.arange(q * XB, (q + 1) * XB) - (X - 1) / 2.0
    z = np.arange(Z) - (Z - 1) / 2.0
    top = 0.0
    low = 0.0
    angle = np.linspace(-MAX_ANGLE, MAX_ANGLE, 4001)
    first = True
    for xv in (x[0], x[-1]):
        for zv in (z[0], z[-1]):
            pos = VOXEL * (xv * np.cos(angle) + zv * np.sin(angle)) + (NDET - 1) / 2.0
            low = pos.min() if first else min(low, pos.min())
            top = pos.max() if first else max(top, pos.max())
            first = False
    return math.ceil(low - 1.0 - 0.01), math.floor(top + 1.0 + 0.01)


def pair_list(n_det):
    pairs = []
    for q in range(NQ):
        low, top = reach(q)
        pairs.append(list(range(max(low, 0) // n_det, min(top, NDET - 1) // n_det + 1)))
    return pairs


def rounded(table):
    return np.asarray(table, np.float32).astype(jnp.bfloat16)


def plane_tables():
    kz = np.repeat(np.arange(KZ), LEN)
    kx = np.tile(np.arange(LEN), KZ)
    mid = (EDGE - 1) / 2.0

    def waves(k, at, length, width):
        p = 2.0 * np.pi * (np.outer(at, k) % length) / length
        out = np.zeros((2, len(at), width), np.float32)
        out[0, :, : len(k)], out[1, :, : len(k)] = np.cos(p), np.sin(p)
        return out

    vx = np.repeat(np.arange(EDGE // 2) - mid, EDGE)
    vz = np.tile(np.arange(EDGE) - mid, EDGE // 2)
    weight = np.full((KZ, 1), 2.0)
    weight[0] = weight[-1] = 1.0
    turn = np.zeros((2, XT, FP))
    for col in range(XT):
        back = HALO if col == 0 else 0
        p = 2.0 * np.pi * (kx * (mid - back) / LEN + kz * (mid - HALO) / LZ)
        turn[0, col, :NF], turn[1, col, :NF] = np.cos(p), np.sin(p)
    return (
        waves(kx, np.arange(XR // 2) - (XR - 1) / 2.0, LEN, FP),
        waves(kz, np.arange(Z) - (Z - 1) / 2.0, LZ, FP),
        waves(vx, np.arange(LEN // 2), LEN, OH),
        waves(vz, np.arange(KZ), LZ, OH) * weight,
        turn,
    )


def line_tables():
    def table(outs, ins, sign):
        p = 2.0 * np.pi * (np.outer(np.arange(outs), np.arange(ins)) % LEN) / LEN
        c, s = np.cos(p), np.sin(p) * sign
        return c, s

    c, s = table(LEN, LEN, 1.0)
    region = rounded(np.block([[c, s], [-s, c]]))
    c, s = table(LEN, K, 1.0)
    template = rounded(np.kron(np.eye(TB), np.block([[c, s], [-s, c]])))
    c, s = table(EDGE, LEN, 1.0)
    back = rounded(np.kron(np.eye(PB), np.block([[c, -s], [s, c]])))
    return region, template, back


def pack_kernel(
    near_bit,
    masks,
    at_ref,
    range_hbm,
    angle_hbm,
    proj_hbm,
    turns_ref,
    home_ref,
    near_ref,
    give_ref,
    mine_ref,
    proj_ref,
    angle_ref,
    range_ref,
    rows_ref,
    sem,
):
    n_tilt, n_det, y_count = proj_ref.shape
    depth = home_ref.shape[1]
    group = 128 // n_det
    spans = [(low, min(low + group, n_tilt)) for low in range(0, n_tilt, group)]
    fetch = [
        pltpu.make_async_copy(angle_hbm, angle_ref, sem.at[0]),
        pltpu.make_async_copy(range_hbm, range_ref, sem.at[1]),
    ]
    for i, (low, top) in enumerate(spans):
        at = pl.ds(low, top - low)
        fetch.append(pltpu.make_async_copy(proj_hbm.at[at], proj_ref.at[at], sem.at[2 + i]))
    for copy in fetch[1:] + fetch[:1]:
        copy.start()
    fetch[0].wait()
    turns_ref[0:1] = jnp.cos(angle_ref[...])
    turns_ref[1:2] = jnp.sin(angle_ref[...])
    fetch[1].wait()
    y = lax.broadcasted_iota(jnp.int32, (n_det, y_count), 1)
    edge = jnp.zeros((HALO, 128), F32)
    for i, (low, top) in enumerate(spans):
        fetch[2 + i].wait()
        parts = []
        for t in range(low, top):
            keep = (y >= range_ref[0, t]) & (y < range_ref[1, t])
            parts.append(jnp.where(keep, proj_ref[t].astype(F32), 0.0))
        if (top - low) * n_det < 128:
            parts.append(jnp.zeros((128 - (top - low) * n_det, y_count), F32))
        block = jnp.concatenate([edge, jnp.concatenate(parts, 0).T, edge], 0)
        rows_ref[:, i * 128 : (i + 1) * 128] = block.astype(BF)
    chip, core = at_ref[0], at_ref[1]

    def rows(target):
        return rows_ref[pl.ds(pl.multiple_of(target * EDGE, EDGE), LEN)]

    home_ref[...] = rows(chip)
    near_ref[...] = rows(chip ^ near_bit)
    give_ref[0] = home_ref[...]
    for j, mask in enumerate(masks):
        mine_ref[j] = rows(chip ^ mask ^ (near_bit * core))
        give_ref[1 + j] = rows(chip ^ mask ^ (near_bit * (1 - core)))


def merge_kernel(mine_ref, got_ref, done_ref, *out_refs):
    done_ref[...] = jnp.zeros_like(done_ref)
    for j, out_ref in enumerate(out_refs):
        out_ref[0] = mine_ref[j]
        out_ref[1] = got_ref[1 + j]


def build_weights(n_det, n_tile, pairs, col, turns_ref, w_ref, whole_ref, part_ref):
    depth = whole_ref.shape[0]
    lane = lax.broadcasted_iota(jnp.int32, (n_det, LB), 1)
    step = lane // Z
    pack = 16 // n_det
    own = lax.broadcasted_iota(jnp.int32, (n_det, LB), 0).astype(F32)
    top = NTILT // pack * pack
    tail = depth - top * n_det
    base = 0
    for q, sources in enumerate(pairs):
        block = jnp.where(col == 0, q, NQ - 1 - q)
        flip = (block * LB + lane) >= VH
        x = jnp.where(flip, XB - 1 - step + jnp.where(block == NQ // 2, XB // 2, 0), step)
        x = x + (block * XB + col * (X - XR))
        x = VOXEL * (x.astype(F32) - (X - 1) / 2.0)
        z = jnp.where(flip, Z - 1 - lane % Z, lane % Z)
        z = VOXEL * (z.astype(F32) - (Z - 1) / 2.0)

        def tilt(t, z=z, x=x):
            pos = x * turns_ref[0, t] + z * turns_ref[1, t] + (NDET - 1) / 2.0
            whole = jnp.floor(pos)
            return own - whole, pos - whole

        for first in range(0, NTILT, pack):
            got = [tilt(t) for t in range(first, min(first + pack, NTILT))]
            rows = pack * n_det if first < top else tail
            gap = rows - len(got) * n_det
            for ref, values in ((whole_ref, [g[0] for g in got]), (part_ref, [g[1] for g in got])):
                if gap:
                    values.append(jnp.zeros((gap, LB), F32))
                ref[first * n_det : first * n_det + rows] = jnp.concatenate(values, 0).astype(BF)

        def build(j, carry, base=base, first=sources[0]):
            src = first + j
            src = jnp.where(col == 0, src, n_tile - 1 - src)
            shift = (src * n_det).astype(F32).astype(BF)
            off = (whole_ref[...] + shift) - part_ref[...]
            one = jnp.ones((), BF)
            w_ref[base + j] = jnp.maximum(one - jnp.abs(off), jnp.zeros((), BF))
            return carry

        lax.fori_loop(0, len(sources), build, 0)
        base += len(sources)


def build_planes(fx_ref, fz_ref, ix_ref, iz_ref, plane_ref, inverse_ref):
    def forward(x, carry):
        cos_x, sin_x = fx_ref[0, pl.ds(x, 1)], fx_ref[1, pl.ds(x, 1)]
        cos_z, sin_z = fz_ref[0], fz_ref[1]
        at = pl.ds(pl.multiple_of(x * Z, Z), Z)
        plane_ref[at, :FP] = (cos_x * cos_z - sin_x * sin_z).astype(BF)
        plane_ref[at, FP:] = (-sin_x * cos_z - cos_x * sin_z).astype(BF)
        return carry

    lax.fori_loop(0, XR // 2, forward, 0)
    odd = lax.broadcasted_iota(jnp.int32, (1, OH), 1) // EDGE % 2
    turn = 1.0 - 2.0 * odd.astype(F32)

    def inverse(k, carry):
        cos_z, sin_z = iz_ref[0, pl.ds(k, 1)], iz_ref[1, pl.ds(k, 1)]
        cos_x, sin_x = ix_ref[0], ix_ref[1]
        real = cos_x * cos_z - sin_x * sin_z
        imag = -sin_x * cos_z - cos_x * sin_z
        low = pl.multiple_of(k * LEN, 16)
        inverse_ref[pl.ds(low, LEN)] = jnp.concatenate([real, imag * turn], 0).astype(BF)
        inverse_ref[pl.ds(FP + low, LEN)] = jnp.concatenate([imag, -real * turn], 0).astype(BF)
        return carry

    lax.fori_loop(0, KZ, inverse, 0)
    inverse_ref[NF:FP] = jnp.zeros((FP - NF, OH), BF)
    inverse_ref[FP + NF :] = jnp.zeros((FP - NF, OH), BF)


def build_templates(col, rot_ref, bank_ref, plane_ref, line_ref, turn_ref, out_ref):
    chosen = jnp.concatenate([bank_ref[rot_ref[r]] for r in range(NTPL)], 0)
    plane = jnp.concatenate([plane_ref[b * Z : b * Z + K] for b in range(K)], 0)
    flat = jnp.dot(chosen, plane, preferred_element_type=F32).astype(BF)
    cos = jnp.where(col == 0, turn_ref[0, 0:1], turn_ref[0, 1:2])
    sin = jnp.where(col == 0, turn_ref[1, 0:1], turn_ref[1, 1:2])
    for first in range(0, NTPL, TB):
        stacked = []
        for r in range(first, first + TB):
            part = flat[r * K : (r + 1) * K]
            stacked += [part[:, :FP], part[:, FP:]]
        stacked = jnp.concatenate(stacked, 0)
        full = jnp.dot(line_ref[...], stacked, preferred_element_type=F32)
        for i in range(TB):
            low = i * 2 * LEN
            real, imag = full[low : low + LEN], -full[low + LEN : low + 2 * LEN]
            out_ref[first + i, :LEN] = (real * cos - imag * sin).astype(BF)
            out_ref[first + i, LEN:] = (real * sin + imag * cos).astype(BF)


def prepare_kernel(n_det, n_tile, pairs, at_ref, turns_ref, _, *refs):
    sources, outs, targets, (sem, whole_ref, part_ref) = refs[:8], refs[8:13], refs[13:21], refs[21:]
    fetch = [
        pltpu.make_async_copy(a, b, sem.at[i]) for i, (a, b) in enumerate(zip(sources, targets))
    ]
    for copy in fetch:
        copy.start()
    w_ref, plane_ref, inverse_ref, tmpl_ref, done_ref = outs
    col = at_ref[1]
    build_weights(n_det, n_tile, pairs, col, turns_ref, w_ref, whole_ref, part_ref)
    for copy in fetch:
        copy.wait()
    rot_ref, bank_ref, fx_ref, fz_ref, ix_ref, iz_ref, line_ref, turn_ref = targets
    build_planes(fx_ref, fz_ref, ix_ref, iz_ref, plane_ref, inverse_ref)
    build_templates(col, rot_ref, bank_ref, plane_ref, line_ref, turn_ref, tmpl_ref)
    done_ref[...] = jnp.zeros_like(done_ref)


def score_kernel(near_bit, masks, pairs, n_tile, *refs):
    n_op = len(masks)
    at_ref, home_ref, got_ref, near_ref, near_swap_ref = refs[:5]
    recv_refs, swap_refs = refs[5 : 5 + n_op], refs[5 + n_op : 5 + 2 * n_op]
    w_ref, tmpl_ref, plane_ref, line_ref, back_ref, inverse_ref = refs[5 + 2 * n_op : 11 + 2 * n_op]
    _, out_ref, data_ref, vol_ref, mid_ref = refs[11 + 2 * n_op :]
    chip, core = at_ref[0], at_ref[1]
    mate = 1 - core
    data_ref[chip * XT + core] = home_ref[...]
    data_ref[chip * XT + mate] = got_ref[0]
    data_ref[(chip ^ near_bit) * XT + core] = near_ref[...]
    data_ref[(chip ^ near_bit) * XT + mate] = near_swap_ref[...]
    for j, mask in enumerate(masks):
        here = (chip ^ mask ^ (near_bit * core)) * XT
        there = (chip ^ mask ^ (near_bit * mate)) * XT
        data_ref[here + core] = recv_refs[j][0]
        data_ref[here + mate] = recv_refs[j][1]
        data_ref[there + mate] = swap_refs[j][0]
        data_ref[there + core] = swap_refs[j][1]
    base = 0
    for q, sources in enumerate(pairs):
        total = jnp.zeros((LEN, LB), F32)
        for j, src in enumerate(sources):
            part = data_ref[jnp.where(core == 0, src, n_tile - 1 - src)]
            total += jnp.dot(part, w_ref[base + j], preferred_element_type=F32)
        base += len(sources)
        block = jnp.where(core == 0, q, NQ - 1 - q)
        vol_ref[:, pl.ds(pl.multiple_of(block * LB, LB), LB)] = total
    near_half = vol_ref[:, :VH]
    far_half = jnp.concatenate(
        [vol_ref[:, 4 * LB :], vol_ref[:, 3 * LB : 4 * LB], vol_ref[:, VH : 3 * LB]], 1
    )
    even, odd = (near_half + far_half).astype(BF), (near_half - far_half).astype(BF)
    stacked = jnp.concatenate(
        [
            jnp.dot(even, plane_ref[:, :FP], preferred_element_type=F32).astype(BF),
            jnp.dot(odd, plane_ref[:, FP:], preferred_element_type=F32).astype(BF),
        ],
        0,
    )
    full = jnp.dot(line_ref[...], stacked, preferred_element_type=F32)
    real, imag = full[:LEN], full[LEN:]
    for first in range(0, NTPL, PB):
        prod = []
        for r in range(first, first + PB):
            t_real = tmpl_ref[r, :LEN].astype(F32)
            t_imag = tmpl_ref[r, LEN:].astype(F32)
            prod.append((t_real * real - t_imag * imag).astype(BF))
            prod.append((t_real * imag + t_imag * real).astype(BF))
        prod = jnp.concatenate(prod, 0)
        line = jnp.dot(back_ref[...], prod, preferred_element_type=F32).astype(BF)
        for i in range(PB):
            at = slice((first + i) * EDGE, (first + i + 1) * EDGE)
            mid_ref[at, :FP] = line[2 * i * EDGE : (2 * i + 1) * EDGE]
            mid_ref[at, FP:] = line[(2 * i + 1) * EDGE : (2 * i + 2) * EDGE]
    even = jnp.dot(mid_ref[:, :FP], inverse_ref[:FP], preferred_element_type=F32)
    odd = jnp.dot(mid_ref[:, FP:], inverse_ref[FP:], preferred_element_type=F32)
    best = even[:EDGE] + odd[:EDGE]
    mirrored = even[:EDGE] - odd[:EDGE]
    for r in range(1, NTPL):
        at = slice(r * EDGE, (r + 1) * EDGE)
        best = jnp.maximum(best, even[at] + odd[at])
        mirrored = jnp.maximum(mirrored, even[at] - odd[at])
    out_ref[0, :, :OH] = best * SCALE
    mirrored = mirrored * SCALE
    order = 127 - lax.broadcasted_iota(jnp.int32, (EDGE, 128), 1)
    for low in range(0, OH, 128):
        part = jnp.take_along_axis(mirrored[:, low : low + 128], order, axis=1)
        out_ref[0, :, 2 * OH - 128 - low : 2 * OH - low] = part


VMEM = pl.BlockSpec(memory_space=pltpu.VMEM)
SMEM = pl.BlockSpec(memory_space=pltpu.SMEM)
HBM = pl.BlockSpec(memory_space=pltpu.HBM)


def limit(mib):
    return pltpu.CompilerParams(vmem_limit_bytes=mib << 20)


def cost(flops, nbytes):
    return pl.CostEstimate(flops=flops, bytes_accessed=nbytes, transcendentals=0)


def pinned(array):
    return pltpu.with_memory_space_constraint(array, pltpu.HBM)


def shape(*dims, dtype=BF):
    return jax.ShapeDtypeStruct(dims, dtype)


def solution(mesh):
    n_tile = mesh.shape["tile"]
    n_block = n_tile // XT
    n_det = NDET // n_tile
    depth = (NTILT * n_det + 127) // 128 * 128
    near_bit = n_block // 2
    masks = [k for k in range(1, n_block) if not k & near_bit]
    n_op = len(masks)
    pairs = pair_list(n_det)
    n_pair = sum(len(p) for p in pairs)
    tables = plane_tables()
    line, line_t, back = line_tables()
    mate = [(i, i ^ 1) for i in range(n_tile)]
    near_pairs = [(i, i ^ (near_bit * XT)) for i in range(n_tile)]

    def route(mask):
        return [(i, i ^ (mask * XT) ^ (near_bit * XT * (i % XT))) for i in range(n_tile)]

    def local(projections, tilt_angle, row_range, template_bank, rot_index):
        y_count = projections.shape[0]
        position = lax.axis_index("tile").astype(jnp.int32)
        at = jnp.stack([position // XT, position % XT])
        by_y = jnp.transpose(projections, (1, 2, 0))
        turns, home, near, give, mine = pl.pallas_call(
            lambda *refs: pack_kernel(near_bit, masks, *refs),
            out_shape=(
                shape(2, NTILT, dtype=F32),
                shape(LEN, depth),
                shape(LEN, depth),
                shape(1 + n_op, LEN, depth),
                shape(n_op, LEN, depth),
            ),
            in_specs=[SMEM, HBM, HBM, HBM],
            out_specs=(VMEM,) * 5,
            scratch_shapes=[
                pltpu.VMEM(by_y.shape, BF),
                pltpu.VMEM((1, NTILT), F32),
                pltpu.SMEM((2, NTILT), jnp.int32),
                pltpu.VMEM((y_count + 2 * HALO, depth), BF),
                pltpu.SemaphoreType.DMA((2 + depth // 128,)),
            ],
            compiler_params=limit(8),
        )(at, pinned(row_range.T), pinned(tilt_angle.reshape(1, NTILT)), pinned(by_y))
        got = lax.ppermute(give, "tile", mate)
        near_in = lax.ppermute(near, "tile", near_pairs)
        merged, *payload = pl.pallas_call(
            merge_kernel,
            out_shape=(shape(8, 128, dtype=F32),) + (shape(2, LEN, depth),) * n_op,
            in_specs=[VMEM, VMEM],
            out_specs=(VMEM,) * (1 + n_op),
            compiler_params=limit(8),
        )(mine, got)
        arrived = [lax.ppermute(p, "tile", route(m)) for p, m in zip(payload, masks)]
        constants = (
            rot_index,
            template_bank,
            *[jnp.asarray(t, F32) for t in tables[:4]],
            jnp.asarray(line_t),
            jnp.asarray(tables[4], F32),
        )
        weights, plane, inverse, spectra, done = pl.pallas_call(
            lambda *refs: prepare_kernel(n_det, n_tile, pairs, *refs),
            out_shape=(
                shape(n_pair, depth, LB),
                shape(VH, 2 * FP),
                shape(2 * FP, OH),
                shape(NTPL, 2 * LEN, FP),
                shape(8, 128, dtype=F32),
            ),
            in_specs=[SMEM, SMEM, VMEM] + [HBM] * 8,
            out_specs=(VMEM,) * 5,
            scratch_shapes=[
                pltpu.SMEM((NTPL,), jnp.int32),
                *[pltpu.VMEM(c.shape, c.dtype) for c in constants[1:]],
                pltpu.SemaphoreType.DMA((8,)),
                pltpu.VMEM((depth, LB), BF),
                pltpu.VMEM((depth, LB), BF),
            ],
            compiler_params=limit(24),
            cost_estimate=cost(1 << 32, 16 << 20),
        )(at, turns, merged, *[pinned(c) for c in constants])
        near_in, done, *arrived = lax.optimization_barrier((near_in, done, *arrived))
        near_swap = lax.ppermute(near_in, "tile", mate)
        swapped = [lax.ppermute(a, "tile", mate) for a in arrived]
        return pl.pallas_call(
            lambda *refs: score_kernel(near_bit, masks, pairs, n_tile, *refs),
            out_shape=shape(1, EDGE, EDGE * Z, dtype=F32),
            in_specs=[SMEM] + [VMEM] * (11 + 2 * n_op),
            out_specs=VMEM,
            scratch_shapes=[
                pltpu.VMEM((n_tile, LEN, depth), BF),
                pltpu.VMEM((LEN, XR * Z), F32),
                pltpu.VMEM((NTPL * EDGE, 2 * FP), BF),
            ],
            compiler_params=limit(28),
            cost_estimate=cost(4 << 30, 20 << 20),
        )(
            at,
            home,
            got,
            near_in,
            near_swap,
            *arrived,
            *swapped,
            weights,
            spectra,
            plane,
            jnp.asarray(line),
            jnp.asarray(back),
            inverse,
            done,
        )

    return jax.shard_map(
        local,
        mesh=mesh,
        in_specs=(P("grp", None, "tile"), P("grp"), P("grp", None), P(), P()),
        out_specs=P("tile", "grp", None),
        check_vma=False,
    )
```

```python
import math

import jax
import jax.numpy as jnp
import numpy as np
from jax import lax
from jax.experimental import pallas as pl
from jax.experimental.pallas import tpu as pltpu
from jax.sharding import PartitionSpec as P

EDGE = 32
XT = 2
K = 16
NTILT = 61
NTPL = 8
NDET = 128
HALO = K // 2
LEN = EDGE + K
X = XT * EDGE
Z = EDGE
XR = EDGE + HALO
LZ = Z + HALO
KZ = LZ // 2 + 1
NF = LEN * KZ
FP = 1024
VH = XR * Z // 2
OH = EDGE * EDGE // 2
XB = 8
NQ = XR // XB
LB = XB * Z
MAX_ANGLE = 1.05
VOXEL = 1.4
SCALE = 1.0 / (LEN * LEN * LZ)
BF = jnp.bfloat16
F32 = jnp.float32


def reach(q):
    x = np.arange(q * XB, (q + 1) * XB) - (X - 1) / 2.0
    z = np.arange(Z) - (Z - 1) / 2.0
    top = 0.0
    low = 0.0
    angle = np.linspace(-MAX_ANGLE, MAX_ANGLE, 4001)
    first = True
    for xv in (x[0], x[-1]):
        for zv in (z[0], z[-1]):
            pos = VOXEL * (xv * np.cos(angle) + zv * np.sin(angle)) + (NDET - 1) / 2.0
            low = pos.min() if first else min(low, pos.min())
            top = pos.max() if first else max(top, pos.max())
            first = False
    return math.ceil(low - 1.0 - 0.01), math.floor(top + 1.0 + 0.01)


def pair_list(n_det):
    pairs = []
    for q in range(NQ):
        low, top = reach(q)
        pairs.append(list(range(max(low, 0) // n_det, min(top, NDET - 1) // n_det + 1)))
    return pairs


def rounded(table):
    return np.asarray(table, np.float32).astype(jnp.bfloat16)


def plane_tables():
    kz = np.repeat(np.arange(KZ), LEN)
    kx = np.tile(np.arange(LEN), KZ)
    mid = (EDGE - 1) / 2.0

    def waves(k, at, length, width):
        p = 2.0 * np.pi * (np.outer(at, k) % length) / length
        out = np.zeros((2, len(at), width), np.float32)
        out[0, :, : len(k)], out[1, :, : len(k)] = np.cos(p), np.sin(p)
        return out

    vx = np.repeat(np.arange(EDGE // 2) - mid, EDGE)
    vz = np.tile(np.arange(EDGE) - mid, EDGE // 2)
    weight = np.full((KZ, 1), 2.0)
    weight[0] = weight[-1] = 1.0
    turn = np.zeros((2, XT, FP))
    for col in range(XT):
        back = HALO if col == 0 else 0
        p = 2.0 * np.pi * (kx * (mid - back) / LEN + kz * (mid - HALO) / LZ)
        turn[0, col, :NF], turn[1, col, :NF] = np.cos(p), np.sin(p)
    return (
        waves(kx, np.arange(XR // 2) - (XR - 1) / 2.0, LEN, FP),
        waves(kz, np.arange(Z) - (Z - 1) / 2.0, LZ, FP),
        waves(vx, np.arange(LEN // 2), LEN, OH),
        waves(vz, np.arange(KZ), LZ, OH) * weight,
        turn,
    )


def line_tables():
    def table(outs, ins, sign):
        p = 2.0 * np.pi * (np.outer(np.arange(outs), np.arange(ins)) % LEN) / LEN
        c, s = np.cos(p), np.sin(p) * sign
        return c, s

    c, s = table(LEN, LEN, 1.0)
    region = rounded(np.block([[c, s], [-s, c]]))
    c, s = table(LEN, K, 1.0)
    template = rounded(np.block([[c, s], [-s, c]]))
    c, s = table(EDGE, LEN, 1.0)
    back = rounded(np.block([[c, -s], [s, c]]))
    return region, template, back


def place():
    position = lax.axis_index("tile").astype(jnp.int32)
    return position // XT, position % XT


def pack_kernel(
    near_bit,
    masks,
    range_hbm,
    angle_hbm,
    proj_hbm,
    turns_ref,
    home_ref,
    near_ref,
    give_ref,
    mine_ref,
    proj_ref,
    angle_ref,
    range_ref,
    rows_ref,
    sem,
):
    fetch = [
        pltpu.make_async_copy(range_hbm, range_ref, sem.at[0]),
        pltpu.make_async_copy(angle_hbm, angle_ref, sem.at[1]),
        pltpu.make_async_copy(proj_hbm, proj_ref, sem.at[2]),
    ]
    for copy in fetch:
        copy.start()
    fetch[1].wait()
    for i, wave in enumerate((jnp.cos, jnp.sin)):
        spread = jnp.broadcast_to(wave(angle_ref[...]), (128, angle_ref.shape[1])).T
        turns_ref[i, :, :128] = spread
        turns_ref[i, :, 128:] = spread
    fetch[0].wait()
    fetch[2].wait()
    n_tilt, n_det, y_count = proj_ref.shape
    depth = home_ref.shape[1]
    y = lax.broadcasted_iota(jnp.int32, (n_det, y_count), 1)
    parts = []
    for t in range(n_tilt):
        keep = (y >= range_ref[0, t]) & (y < range_ref[1, t])
        parts.append(jnp.where(keep, proj_ref[t].astype(F32), 0.0))
    if depth > n_tilt * n_det:
        parts.append(jnp.zeros((depth - n_tilt * n_det, y_count), F32))
    edge = jnp.zeros((HALO, depth), F32)
    rows_ref[...] = jnp.concatenate([edge, jnp.concatenate(parts, 0).T, edge], 0).astype(BF)
    chip, core = place()

    def rows(target):
        return rows_ref[pl.ds(pl.multiple_of(target * EDGE, EDGE), LEN)]

    home_ref[...] = rows(chip)
    near_ref[...] = rows(chip ^ near_bit)
    give_ref[0] = home_ref[...]
    for j, mask in enumerate(masks):
        mine_ref[j] = rows(chip ^ mask ^ (near_bit * core))
        give_ref[1 + j] = rows(chip ^ mask ^ (near_bit * (1 - core)))


def merge_kernel(mine_ref, got_ref, done_ref, *out_refs):
    done_ref[...] = jnp.zeros_like(done_ref)
    for j, out_ref in enumerate(out_refs):
        out_ref[0] = mine_ref[j]
        out_ref[1] = got_ref[1 + j]


def build_weights(n_det, n_tile, pairs, col, turns_ref, w_ref, whole_ref, part_ref):
    depth = whole_ref.shape[0]
    lane = lax.broadcasted_iota(jnp.int32, (n_det, LB), 1)
    step = lane // Z
    pack = 16 // n_det
    own = lax.broadcasted_iota(jnp.int32, (n_det, LB), 0).astype(F32)
    top = NTILT // pack * pack
    tail = depth - top * n_det
    base = 0
    for q, sources in enumerate(pairs):
        block = jnp.where(col == 0, q, NQ - 1 - q)
        flip = (block * LB + lane) >= VH
        x = jnp.where(flip, XB - 1 - step + jnp.where(block == NQ // 2, XB // 2, 0), step)
        x = x + (block * XB + col * (X - XR))
        x = VOXEL * (x.astype(F32) - (X - 1) / 2.0)
        z = jnp.where(flip, Z - 1 - lane % Z, lane % Z)
        z = VOXEL * (z.astype(F32) - (Z - 1) / 2.0)

        def tilt(t, z=z, x=x):
            pos = x * turns_ref[0, t : t + 1] + z * turns_ref[1, t : t + 1] + (NDET - 1) / 2.0
            whole = jnp.floor(pos)
            return own - whole, pos - whole

        for first in range(0, NTILT, pack):
            got = [tilt(t) for t in range(first, min(first + pack, NTILT))]
            rows = pack * n_det if first < top else tail
            gap = rows - len(got) * n_det
            for ref, values in ((whole_ref, [g[0] for g in got]), (part_ref, [g[1] for g in got])):
                if gap:
                    values.append(jnp.zeros((gap, LB), F32))
                ref[first * n_det : first * n_det + rows] = jnp.concatenate(values, 0).astype(BF)

        def build(j, carry, base=base, first=sources[0]):
            src = first + j
            src = jnp.where(col == 0, src, n_tile - 1 - src)
            shift = (src * n_det).astype(F32).astype(BF)
            off = (whole_ref[...] + shift) - part_ref[...]
            one = jnp.ones((), BF)
            w_ref[base + j] = jnp.maximum(one - jnp.abs(off), jnp.zeros((), BF))
            return carry

        lax.fori_loop(0, len(sources), build, 0)
        base += len(sources)


def build_planes(fx_ref, fz_ref, ix_ref, iz_ref, plane_ref, inverse_ref):
    def forward(x, carry):
        cos_x, sin_x = fx_ref[0, pl.ds(x, 1)], fx_ref[1, pl.ds(x, 1)]
        cos_z, sin_z = fz_ref[0], fz_ref[1]
        at = pl.ds(pl.multiple_of(x * Z, Z), Z)
        plane_ref[at, :FP] = (cos_x * cos_z - sin_x * sin_z).astype(BF)
        plane_ref[at, FP:] = (-sin_x * cos_z - cos_x * sin_z).astype(BF)
        return carry

    lax.fori_loop(0, XR // 2, forward, 0)
    odd = lax.broadcasted_iota(jnp.int32, (1, OH), 1) // EDGE % 2
    turn = 1.0 - 2.0 * odd.astype(F32)

    def inverse(k, carry):
        cos_z, sin_z = iz_ref[0, pl.ds(k, 1)], iz_ref[1, pl.ds(k, 1)]
        cos_x, sin_x = ix_ref[0], ix_ref[1]
        real = cos_x * cos_z - sin_x * sin_z
        imag = -sin_x * cos_z - cos_x * sin_z
        low = pl.multiple_of(k * LEN, 16)
        inverse_ref[pl.ds(low, LEN)] = jnp.concatenate([real, imag * turn], 0).astype(BF)
        inverse_ref[pl.ds(FP + low, LEN)] = jnp.concatenate([imag, -real * turn], 0).astype(BF)
        return carry

    lax.fori_loop(0, KZ, inverse, 0)
    inverse_ref[NF:FP] = jnp.zeros((FP - NF, OH), BF)
    inverse_ref[FP + NF :] = jnp.zeros((FP - NF, OH), BF)


def build_templates(col, rot_ref, bank_ref, plane_ref, line_ref, turn_ref, out_ref):
    chosen = jnp.concatenate([bank_ref[rot_ref[r]] for r in range(NTPL)], 0)
    plane = jnp.concatenate([plane_ref[b * Z : b * Z + K] for b in range(K)], 0)
    flat = jnp.dot(chosen, plane, preferred_element_type=F32).astype(BF)
    cos = jnp.where(col == 0, turn_ref[0, 0:1], turn_ref[0, 1:2])
    sin = jnp.where(col == 0, turn_ref[1, 0:1], turn_ref[1, 1:2])
    for r in range(NTPL):
        part = flat[r * K : (r + 1) * K]
        stacked = jnp.concatenate([part[:, :FP], part[:, FP:]], 0)
        full = jnp.dot(line_ref[...], stacked, preferred_element_type=F32)
        real, imag = full[:LEN], -full[LEN:]
        out_ref[r, :LEN] = (real * cos - imag * sin).astype(BF)
        out_ref[r, LEN:] = (real * sin + imag * cos).astype(BF)


def prepare_kernel(n_det, n_tile, pairs, turns_ref, _, *refs):
    sources, outs, targets, (sem, whole_ref, part_ref) = refs[:8], refs[8:13], refs[13:21], refs[21:]
    fetch = [
        pltpu.make_async_copy(a, b, sem.at[i]) for i, (a, b) in enumerate(zip(sources, targets))
    ]
    for copy in fetch:
        copy.start()
    w_ref, plane_ref, inverse_ref, tmpl_ref, done_ref = outs
    _, col = place()
    build_weights(n_det, n_tile, pairs, col, turns_ref, w_ref, whole_ref, part_ref)
    for copy in fetch:
        copy.wait()
    rot_ref, bank_ref, fx_ref, fz_ref, ix_ref, iz_ref, line_ref, turn_ref = targets
    build_planes(fx_ref, fz_ref, ix_ref, iz_ref, plane_ref, inverse_ref)
    build_templates(col, rot_ref, bank_ref, plane_ref, line_ref, turn_ref, tmpl_ref)
    done_ref[...] = jnp.zeros_like(done_ref)


def score_kernel(near_bit, masks, pairs, n_tile, *refs):
    n_op = len(masks)
    home_ref, got_ref, near_ref, near_swap_ref = refs[:4]
    recv_refs, swap_refs = refs[4 : 4 + n_op], refs[4 + n_op : 4 + 2 * n_op]
    w_ref, tmpl_ref, plane_ref, line_ref, back_ref, inverse_ref = refs[4 + 2 * n_op : 10 + 2 * n_op]
    _, out_ref, data_ref, vol_ref, mid_ref = refs[10 + 2 * n_op :]
    chip, core = place()
    mate = 1 - core
    data_ref[chip * XT + core] = home_ref[...]
    data_ref[chip * XT + mate] = got_ref[0]
    data_ref[(chip ^ near_bit) * XT + core] = near_ref[...]
    data_ref[(chip ^ near_bit) * XT + mate] = near_swap_ref[...]
    for j, mask in enumerate(masks):
        here = (chip ^ mask ^ (near_bit * core)) * XT
        there = (chip ^ mask ^ (near_bit * mate)) * XT
        data_ref[here + core] = recv_refs[j][0]
        data_ref[here + mate] = recv_refs[j][1]
        data_ref[there + mate] = swap_refs[j][0]
        data_ref[there + core] = swap_refs[j][1]
    base = 0
    for q, sources in enumerate(pairs):
        total = jnp.zeros((LEN, LB), F32)
        for j, src in enumerate(sources):
            part = data_ref[jnp.where(core == 0, src, n_tile - 1 - src)]
            total += jnp.dot(part, w_ref[base + j], preferred_element_type=F32)
        base += len(sources)
        block = jnp.where(core == 0, q, NQ - 1 - q)
        vol_ref[:, pl.ds(pl.multiple_of(block * LB, LB), LB)] = total
    near_half = vol_ref[:, :VH]
    far_half = jnp.concatenate(
        [vol_ref[:, 4 * LB :], vol_ref[:, 3 * LB : 4 * LB], vol_ref[:, VH : 3 * LB]], 1
    )
    even, odd = (near_half + far_half).astype(BF), (near_half - far_half).astype(BF)
    stacked = jnp.concatenate(
        [
            jnp.dot(even, plane_ref[:, :FP], preferred_element_type=F32).astype(BF),
            jnp.dot(odd, plane_ref[:, FP:], preferred_element_type=F32).astype(BF),
        ],
        0,
    )
    full = jnp.dot(line_ref[...], stacked, preferred_element_type=F32)
    real, imag = full[:LEN], full[LEN:]
    for r in range(NTPL):
        t_real = tmpl_ref[r, :LEN].astype(F32)
        t_imag = tmpl_ref[r, LEN:].astype(F32)
        prod = jnp.concatenate(
            [
                (t_real * real - t_imag * imag).astype(BF),
                (t_real * imag + t_imag * real).astype(BF),
            ],
            0,
        )
        line = jnp.dot(back_ref[...], prod, preferred_element_type=F32).astype(BF)
        mid_ref[r * EDGE : (r + 1) * EDGE, :FP] = line[:EDGE]
        mid_ref[r * EDGE : (r + 1) * EDGE, FP:] = line[EDGE:]
    even = jnp.dot(mid_ref[:, :FP], inverse_ref[:FP], preferred_element_type=F32)
    odd = jnp.dot(mid_ref[:, FP:], inverse_ref[FP:], preferred_element_type=F32)
    best = even[:EDGE] + odd[:EDGE]
    mirrored = even[:EDGE] - odd[:EDGE]
    for r in range(1, NTPL):
        at = slice(r * EDGE, (r + 1) * EDGE)
        best = jnp.maximum(best, even[at] + odd[at])
        mirrored = jnp.maximum(mirrored, even[at] - odd[at])
    out_ref[0, :, :OH] = best * SCALE
    mirrored = mirrored * SCALE
    order = 127 - lax.broadcasted_iota(jnp.int32, (EDGE, 128), 1)
    for low in range(0, OH, 128):
        part = jnp.take_along_axis(mirrored[:, low : low + 128], order, axis=1)
        out_ref[0, :, 2 * OH - 128 - low : 2 * OH - low] = part


VMEM = pl.BlockSpec(memory_space=pltpu.VMEM)
SMEM = pl.BlockSpec(memory_space=pltpu.SMEM)
HBM = pl.BlockSpec(memory_space=pltpu.HBM)


def limit(mib):
    return pltpu.CompilerParams(vmem_limit_bytes=mib << 20)


def cost(flops, nbytes):
    return pl.CostEstimate(flops=flops, bytes_accessed=nbytes, transcendentals=0)


def pinned(array):
    return pltpu.with_memory_space_constraint(array, pltpu.HBM)


def shape(*dims, dtype=BF):
    return jax.ShapeDtypeStruct(dims, dtype)


def solution(mesh):
    n_tile = mesh.shape["tile"]
    n_block = n_tile // XT
    n_det = NDET // n_tile
    depth = (NTILT * n_det + 127) // 128 * 128
    near_bit = n_block // 2
    masks = [k for k in range(1, n_block) if not k & near_bit]
    n_op = len(masks)
    pairs = pair_list(n_det)
    n_pair = sum(len(p) for p in pairs)
    tables = plane_tables()
    line, line_t, back = line_tables()
    mate = [(i, i ^ 1) for i in range(n_tile)]
    near_pairs = [(i, i ^ (near_bit * XT)) for i in range(n_tile)]

    def route(mask):
        return [(i, i ^ (mask * XT) ^ (near_bit * XT * (i % XT))) for i in range(n_tile)]

    def local(projections, tilt_angle, row_range, template_bank, rot_index):
        y_count = projections.shape[0]
        by_y = jnp.transpose(projections, (1, 2, 0))
        turns, home, near, give, mine = pl.pallas_call(
            lambda *refs: pack_kernel(near_bit, masks, *refs),
            out_shape=(
                shape(2, NTILT, LB, dtype=F32),
                shape(LEN, depth),
                shape(LEN, depth),
                shape(1 + n_op, LEN, depth),
                shape(n_op, LEN, depth),
            ),
            in_specs=[HBM, HBM, HBM],
            out_specs=(VMEM,) * 5,
            scratch_shapes=[
                pltpu.VMEM(by_y.shape, BF),
                pltpu.VMEM((1, NTILT), F32),
                pltpu.SMEM((2, NTILT), jnp.int32),
                pltpu.VMEM((y_count + 2 * HALO, depth), BF),
                pltpu.SemaphoreType.DMA((3,)),
            ],
            compiler_params=limit(8),
        )(pinned(row_range.T), pinned(tilt_angle.reshape(1, NTILT)), pinned(by_y))
        got = lax.ppermute(give, "tile", mate)
        near_in = lax.ppermute(near, "tile", near_pairs)
        merged, *payload = pl.pallas_call(
            merge_kernel,
            out_shape=(shape(8, 128, dtype=F32),) + (shape(2, LEN, depth),) * n_op,
            in_specs=[VMEM, VMEM],
            out_specs=(VMEM,) * (1 + n_op),
            compiler_params=limit(8),
        )(mine, got)
        arrived = [lax.ppermute(p, "tile", route(m)) for p, m in zip(payload, masks)]
        constants = (
            rot_index,
            template_bank,
            *[jnp.asarray(t, F32) for t in tables[:4]],
            jnp.asarray(line_t),
            jnp.asarray(tables[4], F32),
        )
        weights, plane, inverse, spectra, done = pl.pallas_call(
            lambda *refs: prepare_kernel(n_det, n_tile, pairs, *refs),
            out_shape=(
                shape(n_pair, depth, LB),
                shape(VH, 2 * FP),
                shape(2 * FP, OH),
                shape(NTPL, 2 * LEN, FP),
                shape(8, 128, dtype=F32),
            ),
            in_specs=[VMEM, VMEM] + [HBM] * 8,
            out_specs=(VMEM,) * 5,
            scratch_shapes=[
                pltpu.SMEM((NTPL,), jnp.int32),
                *[pltpu.VMEM(c.shape, c.dtype) for c in constants[1:]],
                pltpu.SemaphoreType.DMA((8,)),
                pltpu.VMEM((depth, LB), BF),
                pltpu.VMEM((depth, LB), BF),
            ],
            compiler_params=limit(24),
            cost_estimate=cost(1 << 32, 16 << 20),
        )(turns, merged, *[pinned(c) for c in constants])
        near_in, done, *arrived = lax.optimization_barrier((near_in, done, *arrived))
        near_swap = lax.ppermute(near_in, "tile", mate)
        swapped = [lax.ppermute(a, "tile", mate) for a in arrived]
        return pl.pallas_call(
            lambda *refs: score_kernel(near_bit, masks, pairs, n_tile, *refs),
            out_shape=shape(1, EDGE, EDGE * Z, dtype=F32),
            in_specs=[VMEM] * (11 + 2 * n_op),
            out_specs=VMEM,
            scratch_shapes=[
                pltpu.VMEM((n_tile, LEN, depth), BF),
                pltpu.VMEM((LEN, XR * Z), F32),
                pltpu.VMEM((NTPL * EDGE, 2 * FP), BF),
            ],
            compiler_params=limit(28),
            cost_estimate=cost(4 << 30, 20 << 20),
        )(
            home,
            got,
            near_in,
            near_swap,
            *arrived,
            *swapped,
            weights,
            spectra,
            plane,
            jnp.asarray(line),
            jnp.asarray(back),
            inverse,
            done,
        )

    return jax.shard_map(
        local,
        mesh=mesh,
        in_specs=(P("grp", None, "tile"), P("grp"), P("grp", None), P(), P()),
        out_specs=P("tile", "grp", None),
        check_vma=False,
    )
```

```python
import math

import jax
import jax.numpy as jnp
import numpy as np
from jax import lax
from jax.experimental import pallas as pl
from jax.experimental.pallas import tpu as pltpu
from jax.sharding import PartitionSpec as P

EDGE = 32
XT = 2
K = 16
NTILT = 61
NTPL = 8
NDET = 128
HALO = K // 2
LEN = EDGE + K
X = XT * EDGE
Z = EDGE
XR = EDGE + HALO
LZ = Z + HALO
KZ = LZ // 2 + 1
NF = LEN * KZ
FP = 1024
VH = XR * Z // 2
OH = EDGE * EDGE // 2
XB = 8
NQ = XR // XB
LB = XB * Z
MAX_ANGLE = 1.05
VOXEL = 1.4
SCALE = 1.0 / (LEN * LEN * LZ)
BF = jnp.bfloat16
F32 = jnp.float32


def reach(q):
    x = np.arange(q * XB, (q + 1) * XB) - (X - 1) / 2.0
    z = np.arange(Z) - (Z - 1) / 2.0
    top = 0.0
    low = 0.0
    angle = np.linspace(-MAX_ANGLE, MAX_ANGLE, 4001)
    first = True
    for xv in (x[0], x[-1]):
        for zv in (z[0], z[-1]):
            pos = VOXEL * (xv * np.cos(angle) + zv * np.sin(angle)) + (NDET - 1) / 2.0
            low = pos.min() if first else min(low, pos.min())
            top = pos.max() if first else max(top, pos.max())
            first = False
    return math.ceil(low - 1.0 - 0.01), math.floor(top + 1.0 + 0.01)


def pair_list(n_det):
    pairs = []
    for q in range(NQ):
        low, top = reach(q)
        pairs.append(list(range(max(low, 0) // n_det, min(top, NDET - 1) // n_det + 1)))
    return pairs


def rounded(table):
    return np.asarray(table, np.float32).astype(jnp.bfloat16)


def plane_tables():
    kz = np.repeat(np.arange(KZ), LEN)
    kx = np.tile(np.arange(LEN), KZ)
    mid = (EDGE - 1) / 2.0

    def waves(k, at, length, width):
        p = 2.0 * np.pi * (np.outer(at, k) % length) / length
        out = np.zeros((2, len(at), width), np.float32)
        out[0, :, : len(k)], out[1, :, : len(k)] = np.cos(p), np.sin(p)
        return out

    vx = np.repeat(np.arange(EDGE // 2) - mid, EDGE)
    vz = np.tile(np.arange(EDGE) - mid, EDGE // 2)
    weight = np.full((KZ, 1), 2.0)
    weight[0] = weight[-1] = 1.0
    turn = np.zeros((2, XT, FP))
    for col in range(XT):
        back = HALO if col == 0 else 0
        p = 2.0 * np.pi * (kx * (mid - back) / LEN + kz * (mid - HALO) / LZ)
        turn[0, col, :NF], turn[1, col, :NF] = np.cos(p), np.sin(p)
    return (
        waves(kx, np.arange(XR // 2) - (XR - 1) / 2.0, LEN, FP),
        waves(kz, np.arange(Z) - (Z - 1) / 2.0, LZ, FP),
        waves(vx, np.arange(LEN // 2), LEN, OH),
        waves(vz, np.arange(KZ), LZ, OH) * weight,
        turn,
    )


def line_tables():
    def table(outs, ins, sign):
        p = 2.0 * np.pi * (np.outer(np.arange(outs), np.arange(ins)) % LEN) / LEN
        c, s = np.cos(p), np.sin(p) * sign
        return c, s

    c, s = table(LEN, LEN, 1.0)
    region = rounded(np.block([[c, s], [-s, c]]))
    c, s = table(LEN, K, 1.0)
    template = rounded(np.block([[c, s], [-s, c]]))
    c, s = table(EDGE, LEN, 1.0)
    back = rounded(np.block([[c, -s], [s, c]]))
    return region, template, back


def place():
    position = lax.axis_index("tile").astype(jnp.int32)
    return position // XT, position % XT


def pack_kernel(
    near_bit,
    masks,
    range_hbm,
    angle_hbm,
    proj_hbm,
    turns_ref,
    home_ref,
    near_ref,
    give_ref,
    mine_ref,
    proj_ref,
    angle_ref,
    range_ref,
    rows_ref,
    sem,
):
    fetch = [
        pltpu.make_async_copy(range_hbm, range_ref, sem.at[0]),
        pltpu.make_async_copy(angle_hbm, angle_ref, sem.at[1]),
        pltpu.make_async_copy(proj_hbm, proj_ref, sem.at[2]),
    ]
    for copy in fetch:
        copy.start()
    fetch[1].wait()
    for i, wave in enumerate((jnp.cos, jnp.sin)):
        spread = jnp.broadcast_to(wave(angle_ref[...]), (128, angle_ref.shape[1])).T
        turns_ref[i, :, :128] = spread
        turns_ref[i, :, 128:] = spread
    fetch[0].wait()
    fetch[2].wait()
    n_tilt, n_det, y_count = proj_ref.shape
    depth = home_ref.shape[1]
    y = lax.broadcasted_iota(jnp.int32, (n_det, y_count), 1)
    parts = []
    for t in range(n_tilt):
        keep = (y >= range_ref[0, t]) & (y < range_ref[1, t])
        parts.append(jnp.where(keep, proj_ref[t].astype(F32), 0.0))
    if depth > n_tilt * n_det:
        parts.append(jnp.zeros((depth - n_tilt * n_det, y_count), F32))
    edge = jnp.zeros((HALO, depth), F32)
    rows_ref[...] = jnp.concatenate([edge, jnp.concatenate(parts, 0).T, edge], 0).astype(BF)
    chip, core = place()

    def rows(target):
        return rows_ref[pl.ds(pl.multiple_of(target * EDGE, EDGE), LEN)]

    home_ref[...] = rows(chip)
    near_ref[...] = rows(chip ^ near_bit)
    give_ref[0] = home_ref[...]
    for j, mask in enumerate(masks):
        mine_ref[j] = rows(chip ^ mask ^ (near_bit * core))
        give_ref[1 + j] = rows(chip ^ mask ^ (near_bit * (1 - core)))


def merge_kernel(mine_ref, got_ref, done_ref, *out_refs):
    done_ref[...] = jnp.zeros_like(done_ref)
    for j, out_ref in enumerate(out_refs):
        out_ref[0] = mine_ref[j]
        out_ref[1] = got_ref[1 + j]


def build_weights(n_det, n_tile, pairs, col, turns_ref, w_ref, whole_ref, part_ref):
    depth = whole_ref.shape[0]
    lane = lax.broadcasted_iota(jnp.int32, (n_det, LB), 1)
    step = lane // Z
    pack = 16 // n_det
    own = lax.broadcasted_iota(jnp.int32, (n_det, LB), 0).astype(F32)
    top = NTILT // pack * pack
    tail = depth - top * n_det
    base = 0
    for q, sources in enumerate(pairs):
        block = jnp.where(col == 0, q, NQ - 1 - q)
        flip = (block * LB + lane) >= VH
        x = jnp.where(flip, XB - 1 - step + jnp.where(block == NQ // 2, XB // 2, 0), step)
        x = x + (block * XB + col * (X - XR))
        x = VOXEL * (x.astype(F32) - (X - 1) / 2.0)
        z = jnp.where(flip, Z - 1 - lane % Z, lane % Z)
        z = VOXEL * (z.astype(F32) - (Z - 1) / 2.0)

        def tilt(t, z=z, x=x):
            pos = x * turns_ref[0, t : t + 1] + z * turns_ref[1, t : t + 1] + (NDET - 1) / 2.0
            whole = jnp.floor(pos)
            return own - whole, pos - whole

        for first in range(0, NTILT, pack):
            got = [tilt(t) for t in range(first, min(first + pack, NTILT))]
            rows = pack * n_det if first < top else tail
            gap = rows - len(got) * n_det
            for ref, values in ((whole_ref, [g[0] for g in got]), (part_ref, [g[1] for g in got])):
                if gap:
                    values.append(jnp.zeros((gap, LB), F32))
                ref[first * n_det : first * n_det + rows] = jnp.concatenate(values, 0).astype(BF)

        def build(j, carry, base=base, first=sources[0]):
            src = first + j
            src = jnp.where(col == 0, src, n_tile - 1 - src)
            shift = (src * n_det).astype(F32).astype(BF)
            off = (whole_ref[...] + shift) - part_ref[...]
            one = jnp.ones((), BF)
            w_ref[base + j] = jnp.maximum(one - jnp.abs(off), jnp.zeros((), BF))
            return carry

        lax.fori_loop(0, len(sources), build, 0)
        base += len(sources)


def build_planes(fx_ref, fz_ref, ix_ref, iz_ref, plane_ref, inverse_ref):
    def forward(x, carry):
        cos_x, sin_x = fx_ref[0, pl.ds(x, 1)], fx_ref[1, pl.ds(x, 1)]
        cos_z, sin_z = fz_ref[0], fz_ref[1]
        at = pl.ds(pl.multiple_of(x * Z, Z), Z)
        plane_ref[at, :FP] = (cos_x * cos_z - sin_x * sin_z).astype(BF)
        plane_ref[at, FP:] = (-sin_x * cos_z - cos_x * sin_z).astype(BF)
        return carry

    lax.fori_loop(0, XR // 2, forward, 0)
    odd = lax.broadcasted_iota(jnp.int32, (1, OH), 1) // EDGE % 2
    turn = 1.0 - 2.0 * odd.astype(F32)

    def inverse(k, carry):
        cos_z, sin_z = iz_ref[0, pl.ds(k, 1)], iz_ref[1, pl.ds(k, 1)]
        cos_x, sin_x = ix_ref[0], ix_ref[1]
        real = cos_x * cos_z - sin_x * sin_z
        imag = -sin_x * cos_z - cos_x * sin_z
        low = pl.multiple_of(k * LEN, 16)
        inverse_ref[pl.ds(low, LEN)] = jnp.concatenate([real, imag * turn], 0).astype(BF)
        inverse_ref[pl.ds(FP + low, LEN)] = jnp.concatenate([imag, -real * turn], 0).astype(BF)
        return carry

    lax.fori_loop(0, KZ, inverse, 0)
    inverse_ref[NF:FP] = jnp.zeros((FP - NF, OH), BF)
    inverse_ref[FP + NF :] = jnp.zeros((FP - NF, OH), BF)


def build_templates(col, rot_ref, bank_ref, plane_ref, line_ref, turn_ref, out_ref):
    chosen = jnp.concatenate([bank_ref[rot_ref[r]] for r in range(NTPL)], 0)
    plane = jnp.concatenate([plane_ref[b * Z : b * Z + K] for b in range(K)], 0)
    flat = jnp.dot(chosen, plane, preferred_element_type=F32).astype(BF)
    cos = jnp.where(col == 0, turn_ref[0, 0:1], turn_ref[0, 1:2])
    sin = jnp.where(col == 0, turn_ref[1, 0:1], turn_ref[1, 1:2])
    for r in range(NTPL):
        part = flat[r * K : (r + 1) * K]
        stacked = jnp.concatenate([part[:, :FP], part[:, FP:]], 0)
        full = jnp.dot(line_ref[...], stacked, preferred_element_type=F32)
        real, imag = full[:LEN], -full[LEN:]
        out_ref[r, :LEN] = (real * cos - imag * sin).astype(BF)
        out_ref[r, LEN:] = (real * sin + imag * cos).astype(BF)


def prepare_kernel(n_det, n_tile, pairs, turns_ref, _, *refs):
    sources, outs, targets, (sem, whole_ref, part_ref) = refs[:8], refs[8:13], refs[13:21], refs[21:]
    fetch = [
        pltpu.make_async_copy(a, b, sem.at[i]) for i, (a, b) in enumerate(zip(sources, targets))
    ]
    for copy in fetch:
        copy.start()
    w_ref, plane_ref, inverse_ref, tmpl_ref, done_ref = outs
    _, col = place()
    build_weights(n_det, n_tile, pairs, col, turns_ref, w_ref, whole_ref, part_ref)
    for copy in fetch:
        copy.wait()
    rot_ref, bank_ref, fx_ref, fz_ref, ix_ref, iz_ref, line_ref, turn_ref = targets
    build_planes(fx_ref, fz_ref, ix_ref, iz_ref, plane_ref, inverse_ref)
    build_templates(col, rot_ref, bank_ref, plane_ref, line_ref, turn_ref, tmpl_ref)
    done_ref[...] = jnp.zeros_like(done_ref)


def gather_pieces(near_bit, masks, from_mate, data_ref, home_ref, got_ref, near_ref, refs):
    chip, core = place()
    mate = 1 - core
    data_ref[chip * XT + core] = home_ref[...]
    data_ref[chip * XT + mate] = got_ref[0]
    data_ref[(chip ^ near_bit) * XT + core] = near_ref[...]
    taker, other = (mate, core) if from_mate else (core, mate)
    for ref, mask in zip(refs, masks):
        source = (chip ^ mask ^ (near_bit * taker)) * XT
        data_ref[source + taker] = ref[0]
        data_ref[source + other] = ref[1]
    return (chip ^ near_bit) * XT + mate


def partial_sums(n_tile, pairs, upper, core, data_ref, w_ref):
    base = 0
    for sources in pairs:
        total = jnp.zeros((LEN, LB), F32)
        for j, src in enumerate(sources):
            if (src >= n_tile // 2) == upper:
                part = data_ref[jnp.where(core == 0, src, n_tile - 1 - src)]
                total += jnp.dot(part, w_ref[base + j], preferred_element_type=F32)
        base += len(sources)
        yield total


def half_kernel(near_bit, masks, pairs, n_tile, *refs):
    w_ref, _, half_ref, data_ref = refs[3 + len(masks) :]
    held = refs[3 : 3 + len(masks)]
    absent = gather_pieces(near_bit, masks, False, data_ref, *refs[:3], held)
    data_ref[absent] = jnp.zeros(data_ref.shape[1:], BF)
    chip, core = place()
    for upper in (False, True):

        @pl.when((chip >= near_bit) == upper)
        def _():
            for q, total in enumerate(partial_sums(n_tile, pairs, upper, core, data_ref, w_ref)):
                half_ref[q] = total


def score_kernel(near_bit, masks, pairs, n_tile, *refs):
    held, near_swap_ref = refs[3 : 3 + len(masks)], refs[3 + len(masks)]
    half_ref, w_ref, tmpl_ref, plane_ref, line_ref, back_ref, inverse_ref = refs[
        4 + len(masks) : 11 + len(masks)
    ]
    out_ref, data_ref, vol_ref, mid_ref = refs[11 + len(masks) :]
    absent = gather_pieces(near_bit, masks, True, data_ref, *refs[:3], held)
    data_ref[absent] = near_swap_ref[...]
    chip, core = place()

    def volume(q):
        block = jnp.where(core == 0, q, NQ - 1 - q)
        return pl.ds(pl.multiple_of(block * LB, LB), LB)

    for upper in (False, True):

        @pl.when((chip < near_bit) == upper)
        def _():
            for q, total in enumerate(partial_sums(n_tile, pairs, upper, core, data_ref, w_ref)):
                vol_ref[:, volume(q)] = total + half_ref[q]

    late = n_tile - 1 - absent
    base = 0
    for q, sources in enumerate(pairs):

        @pl.when((core == 1) & (late >= sources[0]) & (late <= sources[-1]))
        def _():
            weight = w_ref[base + late - sources[0]]
            vol_ref[:, volume(q)] += jnp.dot(data_ref[absent], weight, preferred_element_type=F32)

        base += len(sources)
    near_half = vol_ref[:, :VH]
    far_half = jnp.concatenate(
        [vol_ref[:, 4 * LB :], vol_ref[:, 3 * LB : 4 * LB], vol_ref[:, VH : 3 * LB]], 1
    )
    even, odd = (near_half + far_half).astype(BF), (near_half - far_half).astype(BF)
    stacked = jnp.concatenate(
        [
            jnp.dot(even, plane_ref[:, :FP], preferred_element_type=F32).astype(BF),
            jnp.dot(odd, plane_ref[:, FP:], preferred_element_type=F32).astype(BF),
        ],
        0,
    )
    full = jnp.dot(line_ref[...], stacked, preferred_element_type=F32)
    real, imag = full[:LEN], full[LEN:]
    for r in range(NTPL):
        t_real = tmpl_ref[r, :LEN].astype(F32)
        t_imag = tmpl_ref[r, LEN:].astype(F32)
        prod = jnp.concatenate(
            [
                (t_real * real - t_imag * imag).astype(BF),
                (t_real * imag + t_imag * real).astype(BF),
            ],
            0,
        )
        line = jnp.dot(back_ref[...], prod, preferred_element_type=F32).astype(BF)
        mid_ref[r * EDGE : (r + 1) * EDGE, :FP] = line[:EDGE]
        mid_ref[r * EDGE : (r + 1) * EDGE, FP:] = line[EDGE:]
    even = jnp.dot(mid_ref[:, :FP], inverse_ref[:FP], preferred_element_type=F32)
    odd = jnp.dot(mid_ref[:, FP:], inverse_ref[FP:], preferred_element_type=F32)
    best = even[:EDGE] + odd[:EDGE]
    mirrored = even[:EDGE] - odd[:EDGE]
    for r in range(1, NTPL):
        at = slice(r * EDGE, (r + 1) * EDGE)
        best = jnp.maximum(best, even[at] + odd[at])
        mirrored = jnp.maximum(mirrored, even[at] - odd[at])
    out_ref[0, :, :OH] = best * SCALE
    mirrored = mirrored * SCALE
    order = 127 - lax.broadcasted_iota(jnp.int32, (EDGE, 128), 1)
    for low in range(0, OH, 128):
        part = jnp.take_along_axis(mirrored[:, low : low + 128], order, axis=1)
        out_ref[0, :, 2 * OH - 128 - low : 2 * OH - low] = part


VMEM = pl.BlockSpec(memory_space=pltpu.VMEM)
SMEM = pl.BlockSpec(memory_space=pltpu.SMEM)
HBM = pl.BlockSpec(memory_space=pltpu.HBM)


def limit(mib):
    return pltpu.CompilerParams(vmem_limit_bytes=mib << 20)


def cost(flops, nbytes):
    return pl.CostEstimate(flops=flops, bytes_accessed=nbytes, transcendentals=0)


def pinned(array):
    return pltpu.with_memory_space_constraint(array, pltpu.HBM)


def shape(*dims, dtype=BF):
    return jax.ShapeDtypeStruct(dims, dtype)


def solution(mesh):
    n_tile = mesh.shape["tile"]
    n_block = n_tile // XT
    n_det = NDET // n_tile
    depth = (NTILT * n_det + 127) // 128 * 128
    near_bit = n_block // 2
    masks = [k for k in range(1, n_block) if not k & near_bit]
    n_op = len(masks)
    pairs = pair_list(n_det)
    n_pair = sum(len(p) for p in pairs)
    tables = plane_tables()
    line, line_t, back = line_tables()
    mate = [(i, i ^ 1) for i in range(n_tile)]
    near_pairs = [(i, i ^ (near_bit * XT)) for i in range(n_tile)]

    def route(mask):
        return [(i, i ^ (mask * XT) ^ (near_bit * XT * (i % XT))) for i in range(n_tile)]

    def local(projections, tilt_angle, row_range, template_bank, rot_index):
        y_count = projections.shape[0]
        by_y = jnp.transpose(projections, (1, 2, 0))
        turns, home, near, give, mine = pl.pallas_call(
            lambda *refs: pack_kernel(near_bit, masks, *refs),
            out_shape=(
                shape(2, NTILT, LB, dtype=F32),
                shape(LEN, depth),
                shape(LEN, depth),
                shape(1 + n_op, LEN, depth),
                shape(n_op, LEN, depth),
            ),
            in_specs=[HBM, HBM, HBM],
            out_specs=(VMEM,) * 5,
            scratch_shapes=[
                pltpu.VMEM(by_y.shape, BF),
                pltpu.VMEM((1, NTILT), F32),
                pltpu.SMEM((2, NTILT), jnp.int32),
                pltpu.VMEM((y_count + 2 * HALO, depth), BF),
                pltpu.SemaphoreType.DMA((3,)),
            ],
            compiler_params=limit(8),
        )(pinned(row_range.T), pinned(tilt_angle.reshape(1, NTILT)), pinned(by_y))
        got = lax.ppermute(give, "tile", mate)
        near_in = lax.ppermute(near, "tile", near_pairs)
        merged, *payload = pl.pallas_call(
            merge_kernel,
            out_shape=(shape(8, 128, dtype=F32),) + (shape(2, LEN, depth),) * n_op,
            in_specs=[VMEM, VMEM],
            out_specs=(VMEM,) * (1 + n_op),
            compiler_params=limit(8),
        )(mine, got)
        arrived = [lax.ppermute(p, "tile", route(m)) for p, m in zip(payload, masks)]
        constants = (
            rot_index,
            template_bank,
            *[jnp.asarray(t, F32) for t in tables[:4]],
            jnp.asarray(line_t),
            jnp.asarray(tables[4], F32),
        )
        weights, plane, inverse, spectra, done = pl.pallas_call(
            lambda *refs: prepare_kernel(n_det, n_tile, pairs, *refs),
            out_shape=(
                shape(n_pair, depth, LB),
                shape(VH, 2 * FP),
                shape(2 * FP, OH),
                shape(NTPL, 2 * LEN, FP),
                shape(8, 128, dtype=F32),
            ),
            in_specs=[VMEM, VMEM] + [HBM] * 8,
            out_specs=(VMEM,) * 5,
            scratch_shapes=[
                pltpu.SMEM((NTPL,), jnp.int32),
                *[pltpu.VMEM(c.shape, c.dtype) for c in constants[1:]],
                pltpu.SemaphoreType.DMA((8,)),
                pltpu.VMEM((depth, LB), BF),
                pltpu.VMEM((depth, LB), BF),
            ],
            compiler_params=limit(24),
            cost_estimate=cost(1 << 32, 16 << 20),
        )(turns, merged, *[pinned(c) for c in constants])
        near_in, done, *arrived = lax.optimization_barrier((near_in, done, *arrived))
        swapped = [lax.ppermute(a, "tile", mate) for a in arrived]
        near_swap = lax.ppermute(near_in, "tile", mate)
        held = (home, got, near_in)
        pieces = pltpu.VMEM((n_tile, LEN, depth), BF)
        half = pl.pallas_call(
            lambda *refs: half_kernel(near_bit, masks, pairs, n_tile, *refs),
            out_shape=shape(NQ, LEN, LB, dtype=F32),
            in_specs=[VMEM] * (5 + n_op),
            out_specs=VMEM,
            scratch_shapes=[pieces],
            compiler_params=limit(12),
            cost_estimate=cost(n_pair * LEN * depth * LB, n_pair * depth * LB),
        )(*held, *arrived, weights, done)
        return pl.pallas_call(
            lambda *refs: score_kernel(near_bit, masks, pairs, n_tile, *refs),
            out_shape=shape(1, EDGE, EDGE * Z, dtype=F32),
            in_specs=[VMEM] * (11 + n_op),
            out_specs=VMEM,
            scratch_shapes=[
                pieces,
                pltpu.VMEM((LEN, XR * Z), F32),
                pltpu.VMEM((NTPL * EDGE, 2 * FP), BF),
            ],
            compiler_params=limit(28),
            cost_estimate=cost(4 << 30, 20 << 20),
        )(
            *held,
            *swapped,
            near_swap,
            half,
            weights,
            spectra,
            plane,
            jnp.asarray(line),
            jnp.asarray(back),
            inverse,
        )

    return jax.shard_map(
        local,
        mesh=mesh,
        in_specs=(P("grp", None, "tile"), P("grp"), P("grp", None), P(), P()),
        out_specs=P("tile", "grp", None),
        check_vma=False,
    )
```

```python
import math

import jax
import jax.numpy as jnp
import numpy as np
from jax import lax
from jax.experimental import pallas as pl
from jax.experimental.pallas import tpu as pltpu
from jax.sharding import PartitionSpec as P

EDGE = 32
XT = 2
K = 16
NTILT = 61
NTPL = 8
NDET = 128
HALO = K // 2
LEN = EDGE + K
X = XT * EDGE
Z = EDGE
XR = EDGE + HALO
LZ = Z + HALO
KZ = LZ // 2 + 1
NF = LEN * KZ
FP = 1024
VH = XR * Z // 2
OH = EDGE * EDGE // 2
XB = 8
NQ = XR // XB
LB = XB * Z
MAX_ANGLE = 1.05
VOXEL = 1.4
SCALE = 1.0 / (LEN * LEN * LZ)
BF = jnp.bfloat16
F32 = jnp.float32


def reach(q):
    x = np.arange(q * XB, (q + 1) * XB) - (X - 1) / 2.0
    z = np.arange(Z) - (Z - 1) / 2.0
    top = 0.0
    low = 0.0
    angle = np.linspace(-MAX_ANGLE, MAX_ANGLE, 4001)
    first = True
    for xv in (x[0], x[-1]):
        for zv in (z[0], z[-1]):
            pos = VOXEL * (xv * np.cos(angle) + zv * np.sin(angle)) + (NDET - 1) / 2.0
            low = pos.min() if first else min(low, pos.min())
            top = pos.max() if first else max(top, pos.max())
            first = False
    return math.ceil(low - 1.0 - 0.01), math.floor(top + 1.0 + 0.01)


def pair_list(n_det):
    pairs = []
    for q in range(NQ):
        low, top = reach(q)
        pairs.append(list(range(max(low, 0) // n_det, min(top, NDET - 1) // n_det + 1)))
    return pairs


def rounded(table):
    return np.asarray(table, np.float32).astype(jnp.bfloat16)


def plane_tables():
    kz = np.repeat(np.arange(KZ), LEN)
    kx = np.tile(np.arange(LEN), KZ)
    mid = (EDGE - 1) / 2.0

    def waves(k, at, length, width):
        p = 2.0 * np.pi * (np.outer(at, k) % length) / length
        out = np.zeros((2, len(at), width), np.float32)
        out[0, :, : len(k)], out[1, :, : len(k)] = np.cos(p), np.sin(p)
        return out

    vx = np.repeat(np.arange(EDGE // 2) - mid, EDGE)
    vz = np.tile(np.arange(EDGE) - mid, EDGE // 2)
    weight = np.full((KZ, 1), 2.0)
    weight[0] = weight[-1] = 1.0
    turn = np.zeros((2, XT, FP))
    for col in range(XT):
        back = HALO if col == 0 else 0
        p = 2.0 * np.pi * (kx * (mid - back) / LEN + kz * (mid - HALO) / LZ)
        turn[0, col, :NF], turn[1, col, :NF] = np.cos(p), np.sin(p)
    return (
        waves(kx, np.arange(XR // 2) - (XR - 1) / 2.0, LEN, FP),
        waves(kz, np.arange(Z) - (Z - 1) / 2.0, LZ, FP),
        waves(vx, np.arange(LEN // 2), LEN, OH),
        waves(vz, np.arange(KZ), LZ, OH) * weight,
        turn,
    )


def line_tables():
    def table(outs, ins, sign):
        p = 2.0 * np.pi * (np.outer(np.arange(outs), np.arange(ins)) % LEN) / LEN
        c, s = np.cos(p), np.sin(p) * sign
        return c, s

    c, s = table(LEN, LEN, 1.0)
    region = rounded(np.block([[c, s], [-s, c]]))
    c, s = table(LEN, K, 1.0)
    template = rounded(np.block([[c, s], [-s, c]]))
    c, s = table(EDGE, LEN, 1.0)
    back = rounded(np.block([[c, -s], [s, c]]))
    return region, template, back


def place():
    position = lax.axis_index("tile").astype(jnp.int32)
    return position // XT, position % XT


def pack_kernel(
    near_bit,
    masks,
    range_hbm,
    angle_hbm,
    proj_hbm,
    turns_ref,
    home_ref,
    near_ref,
    give_ref,
    mine_ref,
    proj_ref,
    angle_ref,
    range_ref,
    rows_ref,
    sem,
):
    fetch = [
        pltpu.make_async_copy(range_hbm, range_ref, sem.at[0]),
        pltpu.make_async_copy(angle_hbm, angle_ref, sem.at[1]),
        pltpu.make_async_copy(proj_hbm, proj_ref, sem.at[2]),
    ]
    for copy in fetch:
        copy.start()
    fetch[1].wait()
    for i, wave in enumerate((jnp.cos, jnp.sin)):
        spread = jnp.broadcast_to(wave(angle_ref[...]), (128, angle_ref.shape[1])).T
        turns_ref[i, :, :128] = spread
        turns_ref[i, :, 128:] = spread
    fetch[0].wait()
    fetch[2].wait()
    n_tilt, n_det, y_count = proj_ref.shape
    depth = home_ref.shape[1]
    y = lax.broadcasted_iota(jnp.int32, (n_det, y_count), 1)
    parts = []
    for t in range(n_tilt):
        keep = (y >= range_ref[0, t]) & (y < range_ref[1, t])
        parts.append(jnp.where(keep, proj_ref[t].astype(F32), 0.0))
    if depth > n_tilt * n_det:
        parts.append(jnp.zeros((depth - n_tilt * n_det, y_count), F32))
    edge = jnp.zeros((HALO, depth), F32)
    rows_ref[...] = jnp.concatenate([edge, jnp.concatenate(parts, 0).T, edge], 0).astype(BF)
    chip, core = place()

    def rows(target):
        return rows_ref[pl.ds(pl.multiple_of(target * EDGE, EDGE), LEN)]

    home_ref[...] = rows(chip)
    near_ref[...] = rows(chip ^ near_bit)
    give_ref[0] = home_ref[...]
    for j, mask in enumerate(masks):
        mine_ref[j] = rows(chip ^ mask ^ (near_bit * core))
        give_ref[1 + j] = rows(chip ^ mask ^ (near_bit * (1 - core)))


def merge_kernel(mine_ref, got_ref, done_ref, *out_refs):
    done_ref[...] = jnp.zeros_like(done_ref)
    for j, out_ref in enumerate(out_refs):
        out_ref[0] = mine_ref[j]
        out_ref[1] = got_ref[1 + j]


def build_weights(n_det, n_tile, pairs, col, turns_ref, w_ref, whole_ref, part_ref):
    depth = whole_ref.shape[0]
    lane = lax.broadcasted_iota(jnp.int32, (n_det, LB), 1)
    step = lane // Z
    pack = 16 // n_det
    own = lax.broadcasted_iota(jnp.int32, (n_det, LB), 0).astype(F32)
    top = NTILT // pack * pack
    tail = depth - top * n_det
    base = 0
    for q, sources in enumerate(pairs):
        block = jnp.where(col == 0, q, NQ - 1 - q)
        flip = (block * LB + lane) >= VH
        x = jnp.where(flip, XB - 1 - step + jnp.where(block == NQ // 2, XB // 2, 0), step)
        x = x + (block * XB + col * (X - XR))
        x = VOXEL * (x.astype(F32) - (X - 1) / 2.0)
        z = jnp.where(flip, Z - 1 - lane % Z, lane % Z)
        z = VOXEL * (z.astype(F32) - (Z - 1) / 2.0)

        def tilt(t, z=z, x=x):
            pos = x * turns_ref[0, t : t + 1] + z * turns_ref[1, t : t + 1] + (NDET - 1) / 2.0
            whole = jnp.floor(pos)
            return own - whole, pos - whole

        for first in range(0, NTILT, pack):
            got = [tilt(t) for t in range(first, min(first + pack, NTILT))]
            rows = pack * n_det if first < top else tail
            gap = rows - len(got) * n_det
            for ref, values in ((whole_ref, [g[0] for g in got]), (part_ref, [g[1] for g in got])):
                if gap:
                    values.append(jnp.zeros((gap, LB), F32))
                ref[first * n_det : first * n_det + rows] = jnp.concatenate(values, 0).astype(BF)

        def build(j, carry, base=base, first=sources[0]):
            src = first + j
            src = jnp.where(col == 0, src, n_tile - 1 - src)
            shift = (src * n_det).astype(F32).astype(BF)
            off = (whole_ref[...] + shift) - part_ref[...]
            one = jnp.ones((), BF)
            w_ref[base + j] = jnp.maximum(one - jnp.abs(off), jnp.zeros((), BF))
            return carry

        lax.fori_loop(0, len(sources), build, 0)
        base += len(sources)


def build_planes(fx_ref, fz_ref, ix_ref, iz_ref, plane_ref, inverse_ref):
    def forward(x, carry):
        cos_x, sin_x = fx_ref[0, pl.ds(x, 1)], fx_ref[1, pl.ds(x, 1)]
        cos_z, sin_z = fz_ref[0], fz_ref[1]
        at = pl.ds(pl.multiple_of(x * Z, Z), Z)
        plane_ref[at, :FP] = (cos_x * cos_z - sin_x * sin_z).astype(BF)
        plane_ref[at, FP:] = (-sin_x * cos_z - cos_x * sin_z).astype(BF)
        return carry

    lax.fori_loop(0, XR // 2, forward, 0)
    odd = lax.broadcasted_iota(jnp.int32, (1, OH), 1) // EDGE % 2
    turn = 1.0 - 2.0 * odd.astype(F32)

    def inverse(k, carry):
        cos_z, sin_z = iz_ref[0, pl.ds(k, 1)], iz_ref[1, pl.ds(k, 1)]
        cos_x, sin_x = ix_ref[0], ix_ref[1]
        real = cos_x * cos_z - sin_x * sin_z
        imag = -sin_x * cos_z - cos_x * sin_z
        low = pl.multiple_of(k * LEN, 16)
        inverse_ref[pl.ds(low, LEN)] = jnp.concatenate([real, imag * turn], 0).astype(BF)
        inverse_ref[pl.ds(FP + low, LEN)] = jnp.concatenate([imag, -real * turn], 0).astype(BF)
        return carry

    lax.fori_loop(0, KZ, inverse, 0)
    inverse_ref[NF:FP] = jnp.zeros((FP - NF, OH), BF)
    inverse_ref[FP + NF :] = jnp.zeros((FP - NF, OH), BF)


def build_templates(col, rot_ref, bank_ref, plane_ref, line_ref, turn_ref, out_ref):
    chosen = jnp.concatenate([bank_ref[rot_ref[r]] for r in range(NTPL)], 0)
    plane = jnp.concatenate([plane_ref[b * Z : b * Z + K] for b in range(K)], 0)
    flat = jnp.dot(chosen, plane, preferred_element_type=F32).astype(BF)
    cos = jnp.where(col == 0, turn_ref[0, 0:1], turn_ref[0, 1:2])
    sin = jnp.where(col == 0, turn_ref[1, 0:1], turn_ref[1, 1:2])
    for r in range(NTPL):
        part = flat[r * K : (r + 1) * K]
        stacked = jnp.concatenate([part[:, :FP], part[:, FP:]], 0)
        full = jnp.dot(line_ref[...], stacked, preferred_element_type=F32)
        real, imag = full[:LEN], -full[LEN:]
        out_ref[r, :LEN] = (real * cos - imag * sin).astype(BF)
        out_ref[r, LEN:] = (real * sin + imag * cos).astype(BF)


def prepare_kernel(n_det, n_tile, pairs, turns_ref, _, *refs):
    sources, outs, targets, (sem, whole_ref, part_ref) = refs[:8], refs[8:13], refs[13:21], refs[21:]
    fetch = [
        pltpu.make_async_copy(a, b, sem.at[i]) for i, (a, b) in enumerate(zip(sources, targets))
    ]
    for copy in fetch:
        copy.start()
    w_ref, plane_ref, inverse_ref, tmpl_ref, done_ref = outs
    _, col = place()
    build_weights(n_det, n_tile, pairs, col, turns_ref, w_ref, whole_ref, part_ref)
    for copy in fetch:
        copy.wait()
    rot_ref, bank_ref, fx_ref, fz_ref, ix_ref, iz_ref, line_ref, turn_ref = targets
    build_planes(fx_ref, fz_ref, ix_ref, iz_ref, plane_ref, inverse_ref)
    build_templates(col, rot_ref, bank_ref, plane_ref, line_ref, turn_ref, tmpl_ref)
    done_ref[...] = jnp.zeros_like(done_ref)


def gather_pieces(near_bit, masks, from_mate, data_ref, home_ref, got_ref, near_ref, refs):
    chip, core = place()
    mate = 1 - core
    data_ref[chip * XT + core] = home_ref[...]
    data_ref[chip * XT + mate] = got_ref[0]
    data_ref[(chip ^ near_bit) * XT + core] = near_ref[...]
    taker, other = (mate, core) if from_mate else (core, mate)
    for ref, mask in zip(refs, masks):
        source = (chip ^ mask ^ (near_bit * taker)) * XT
        data_ref[source + taker] = ref[0]
        data_ref[source + other] = ref[1]
    return (chip ^ near_bit) * XT + mate


def partial_sums(n_tile, pairs, upper, core, data_ref, w_ref, late=None):
    base = 0
    for sources in pairs:
        total = jnp.zeros((LEN, LB), F32)
        if late is not None:
            inside = (late >= sources[0]) & (late <= sources[-1])
            part = data_ref[jnp.where(inside, n_tile - 1 - late, n_tile)]
            weight = w_ref[base + jnp.clip(late, sources[0], sources[-1]) - sources[0]]
            total += jnp.dot(part, weight, preferred_element_type=F32)
        for j, src in enumerate(sources):
            if (src >= n_tile // 2) == upper:
                part = data_ref[jnp.where(core == 0, src, n_tile - 1 - src)]
                total += jnp.dot(part, w_ref[base + j], preferred_element_type=F32)
        base += len(sources)
        yield total


def half_kernel(near_bit, masks, pairs, n_tile, *refs):
    w_ref, _, half_ref, data_ref = refs[3 + len(masks) :]
    held = refs[3 : 3 + len(masks)]
    absent = gather_pieces(near_bit, masks, False, data_ref, *refs[:3], held)
    data_ref[absent] = jnp.zeros(data_ref.shape[1:], BF)
    chip, core = place()
    for upper in (False, True):

        @pl.when((chip >= near_bit) == upper)
        def _():
            for q, total in enumerate(partial_sums(n_tile, pairs, upper, core, data_ref, w_ref)):
                half_ref[q] = total


def score_kernel(near_bit, masks, pairs, n_tile, *refs):
    held, near_swap_ref = refs[3 : 3 + len(masks)], refs[3 + len(masks)]
    half_ref, w_ref, tmpl_ref, plane_ref, line_ref, back_ref, inverse_ref = refs[
        4 + len(masks) : 11 + len(masks)
    ]
    out_ref, data_ref, vol_ref, mid_ref = refs[11 + len(masks) :]
    absent = gather_pieces(near_bit, masks, True, data_ref, *refs[:3], held)
    data_ref[absent] = near_swap_ref[...]
    chip, core = place()
    data_ref[n_tile] = jnp.zeros(data_ref.shape[1:], BF)
    for upper in (False, True):
        for col in range(XT):

            @pl.when(((chip < near_bit) == upper) & (core == col))
            def _():
                late = n_tile - 1 - absent if col else None
                sums = partial_sums(n_tile, pairs, upper, col, data_ref, w_ref, late)
                for q, total in enumerate(sums):
                    low = (NQ - 1 - q if col else q) * LB
                    vol_ref[:, low : low + LB] = total + half_ref[q]

    near_half = vol_ref[:, :VH]
    far_half = jnp.concatenate(
        [vol_ref[:, 4 * LB :], vol_ref[:, 3 * LB : 4 * LB], vol_ref[:, VH : 3 * LB]], 1
    )
    even, odd = (near_half + far_half).astype(BF), (near_half - far_half).astype(BF)
    stacked = jnp.concatenate(
        [
            jnp.dot(even, plane_ref[:, :FP], preferred_element_type=F32).astype(BF),
            jnp.dot(odd, plane_ref[:, FP:], preferred_element_type=F32).astype(BF),
        ],
        0,
    )
    full = jnp.dot(line_ref[...], stacked, preferred_element_type=F32)
    real, imag = full[:LEN], full[LEN:]
    for r in range(NTPL):
        t_real = tmpl_ref[r, :LEN].astype(F32)
        t_imag = tmpl_ref[r, LEN:].astype(F32)
        prod = jnp.concatenate(
            [
                (t_real * real - t_imag * imag).astype(BF),
                (t_real * imag + t_imag * real).astype(BF),
            ],
            0,
        )
        line = jnp.dot(back_ref[...], prod, preferred_element_type=F32).astype(BF)
        mid_ref[r * EDGE : (r + 1) * EDGE, :FP] = line[:EDGE]
        mid_ref[r * EDGE : (r + 1) * EDGE, FP:] = line[EDGE:]
    even = jnp.dot(mid_ref[:, :FP], inverse_ref[:FP], preferred_element_type=F32)
    odd = jnp.dot(mid_ref[:, FP:], inverse_ref[FP:], preferred_element_type=F32)
    best = even[:EDGE] + odd[:EDGE]
    mirrored = even[:EDGE] - odd[:EDGE]
    for r in range(1, NTPL):
        at = slice(r * EDGE, (r + 1) * EDGE)
        best = jnp.maximum(best, even[at] + odd[at])
        mirrored = jnp.maximum(mirrored, even[at] - odd[at])
    out_ref[0, :, :OH] = best * SCALE
    mirrored = mirrored * SCALE
    order = 127 - lax.broadcasted_iota(jnp.int32, (EDGE, 128), 1)
    for low in range(0, OH, 128):
        part = jnp.take_along_axis(mirrored[:, low : low + 128], order, axis=1)
        out_ref[0, :, 2 * OH - 128 - low : 2 * OH - low] = part


VMEM = pl.BlockSpec(memory_space=pltpu.VMEM)
SMEM = pl.BlockSpec(memory_space=pltpu.SMEM)
HBM = pl.BlockSpec(memory_space=pltpu.HBM)


def limit(mib):
    return pltpu.CompilerParams(vmem_limit_bytes=mib << 20)


def cost(flops, nbytes):
    return pl.CostEstimate(flops=flops, bytes_accessed=nbytes, transcendentals=0)


def pinned(array):
    return pltpu.with_memory_space_constraint(array, pltpu.HBM)


def shape(*dims, dtype=BF):
    return jax.ShapeDtypeStruct(dims, dtype)


def solution(mesh):
    n_tile = mesh.shape["tile"]
    n_block = n_tile // XT
    n_det = NDET // n_tile
    depth = (NTILT * n_det + 127) // 128 * 128
    near_bit = n_block // 2
    masks = [k for k in range(1, n_block) if not k & near_bit]
    n_op = len(masks)
    pairs = pair_list(n_det)
    n_pair = sum(len(p) for p in pairs)
    tables = plane_tables()
    line, line_t, back = line_tables()
    mate = [(i, i ^ 1) for i in range(n_tile)]
    near_pairs = [(i, i ^ (near_bit * XT)) for i in range(n_tile)]

    def route(mask):
        return [(i, i ^ (mask * XT) ^ (near_bit * XT * (i % XT))) for i in range(n_tile)]

    def local(projections, tilt_angle, row_range, template_bank, rot_index):
        y_count = projections.shape[0]
        by_y = jnp.transpose(projections, (1, 2, 0))
        turns, home, near, give, mine = pl.pallas_call(
            lambda *refs: pack_kernel(near_bit, masks, *refs),
            out_shape=(
                shape(2, NTILT, LB, dtype=F32),
                shape(LEN, depth),
                shape(LEN, depth),
                shape(1 + n_op, LEN, depth),
                shape(n_op, LEN, depth),
            ),
            in_specs=[HBM, HBM, HBM],
            out_specs=(VMEM,) * 5,
            scratch_shapes=[
                pltpu.VMEM(by_y.shape, BF),
                pltpu.VMEM((1, NTILT), F32),
                pltpu.SMEM((2, NTILT), jnp.int32),
                pltpu.VMEM((y_count + 2 * HALO, depth), BF),
                pltpu.SemaphoreType.DMA((3,)),
            ],
            compiler_params=limit(8),
        )(pinned(row_range.T), pinned(tilt_angle.reshape(1, NTILT)), pinned(by_y))
        got = lax.ppermute(give, "tile", mate)
        near_in = lax.ppermute(near, "tile", near_pairs)
        merged, *payload = pl.pallas_call(
            merge_kernel,
            out_shape=(shape(8, 128, dtype=F32),) + (shape(2, LEN, depth),) * n_op,
            in_specs=[VMEM, VMEM],
            out_specs=(VMEM,) * (1 + n_op),
            compiler_params=limit(8),
        )(mine, got)
        arrived = [lax.ppermute(p, "tile", route(m)) for p, m in zip(payload, masks)]
        constants = (
            rot_index,
            template_bank,
            *[jnp.asarray(t, F32) for t in tables[:4]],
            jnp.asarray(line_t),
            jnp.asarray(tables[4], F32),
        )
        weights, plane, inverse, spectra, done = pl.pallas_call(
            lambda *refs: prepare_kernel(n_det, n_tile, pairs, *refs),
            out_shape=(
                shape(n_pair, depth, LB),
                shape(VH, 2 * FP),
                shape(2 * FP, OH),
                shape(NTPL, 2 * LEN, FP),
                shape(8, 128, dtype=F32),
            ),
            in_specs=[VMEM, VMEM] + [HBM] * 8,
            out_specs=(VMEM,) * 5,
            scratch_shapes=[
                pltpu.SMEM((NTPL,), jnp.int32),
                *[pltpu.VMEM(c.shape, c.dtype) for c in constants[1:]],
                pltpu.SemaphoreType.DMA((8,)),
                pltpu.VMEM((depth, LB), BF),
                pltpu.VMEM((depth, LB), BF),
            ],
            compiler_params=limit(24),
            cost_estimate=cost(1 << 32, 16 << 20),
        )(turns, merged, *[pinned(c) for c in constants])
        near_in, done, *arrived = lax.optimization_barrier((near_in, done, *arrived))
        swapped = [lax.ppermute(a, "tile", mate) for a in arrived]
        near_swap = lax.ppermute(near_in, "tile", mate)
        held = (home, got, near_in)
        pieces = pltpu.VMEM((n_tile + 1, LEN, depth), BF)
        half = pl.pallas_call(
            lambda *refs: half_kernel(near_bit, masks, pairs, n_tile, *refs),
            out_shape=shape(NQ, LEN, LB, dtype=F32),
            in_specs=[VMEM] * (5 + n_op),
            out_specs=VMEM,
            scratch_shapes=[pieces],
            compiler_params=limit(12),
            cost_estimate=cost(n_pair * LEN * depth * LB, n_pair * depth * LB),
        )(*held, *arrived, weights, done)
        return pl.pallas_call(
            lambda *refs: score_kernel(near_bit, masks, pairs, n_tile, *refs),
            out_shape=shape(1, EDGE, EDGE * Z, dtype=F32),
            in_specs=[VMEM] * (11 + n_op),
            out_specs=VMEM,
            scratch_shapes=[
                pieces,
                pltpu.VMEM((LEN, XR * Z), F32),
                pltpu.VMEM((NTPL * EDGE, 2 * FP), BF),
            ],
            compiler_params=limit(28),
            cost_estimate=cost(4 << 30, 20 << 20),
        )(
            *held,
            *swapped,
            near_swap,
            half,
            weights,
            spectra,
            plane,
            jnp.asarray(line),
            jnp.asarray(back),
            inverse,
        )

    return jax.shard_map(
        local,
        mesh=mesh,
        in_specs=(P("grp", None, "tile"), P("grp"), P("grp", None), P(), P()),
        out_specs=P("tile", "grp", None),
        check_vma=False,
    )
```

```python
import math

import jax
import jax.numpy as jnp
import numpy as np
from jax import lax
from jax.experimental import pallas as pl
from jax.experimental.pallas import tpu as pltpu
from jax.sharding import PartitionSpec as P

EDGE = 32
XT = 2
K = 16
NTILT = 61
NTPL = 8
NDET = 128
HALO = K // 2
LEN = EDGE + K
X = XT * EDGE
Z = EDGE
XR = EDGE + HALO
LZ = Z + HALO
KZ = LZ // 2 + 1
NF = LEN * KZ
FP = 1024
VH = XR * Z // 2
OH = EDGE * EDGE // 2
XB = 8
NQ = XR // XB
LB = XB * Z
MAX_ANGLE = 1.05
VOXEL = 1.4
SCALE = 1.0 / (LEN * LEN * LZ)
BF = jnp.bfloat16
F32 = jnp.float32


def reach(q):
    x = np.arange(q * XB, (q + 1) * XB) - (X - 1) / 2.0
    z = np.arange(Z) - (Z - 1) / 2.0
    top = 0.0
    low = 0.0
    angle = np.linspace(-MAX_ANGLE, MAX_ANGLE, 4001)
    first = True
    for xv in (x[0], x[-1]):
        for zv in (z[0], z[-1]):
            pos = VOXEL * (xv * np.cos(angle) + zv * np.sin(angle)) + (NDET - 1) / 2.0
            low = pos.min() if first else min(low, pos.min())
            top = pos.max() if first else max(top, pos.max())
            first = False
    return math.ceil(low - 1.0 - 0.01), math.floor(top + 1.0 + 0.01)


def pair_list(n_det):
    pairs = []
    for q in range(NQ):
        low, top = reach(q)
        pairs.append(list(range(max(low, 0) // n_det, min(top, NDET - 1) // n_det + 1)))
    return pairs


def rounded(table):
    return np.asarray(table, np.float32).astype(jnp.bfloat16)


def plane_tables():
    kz = np.repeat(np.arange(KZ), LEN)
    kx = np.tile(np.arange(LEN), KZ)
    mid = (EDGE - 1) / 2.0

    def waves(k, at, length, width):
        p = 2.0 * np.pi * (np.outer(at, k) % length) / length
        out = np.zeros((2, len(at), width), np.float32)
        out[0, :, : len(k)], out[1, :, : len(k)] = np.cos(p), np.sin(p)
        return out

    vx = np.repeat(np.arange(EDGE // 2) - mid, EDGE)
    vz = np.tile(np.arange(EDGE) - mid, EDGE // 2)
    weight = np.full((KZ, 1), 2.0)
    weight[0] = weight[-1] = 1.0
    turn = np.zeros((2, XT, FP))
    for col in range(XT):
        back = HALO if col == 0 else 0
        p = 2.0 * np.pi * (kx * (mid - back) / LEN + kz * (mid - HALO) / LZ)
        turn[0, col, :NF], turn[1, col, :NF] = np.cos(p), np.sin(p)
    return (
        waves(kx, np.arange(XR // 2) - (XR - 1) / 2.0, LEN, FP),
        waves(kz, np.arange(Z) - (Z - 1) / 2.0, LZ, FP),
        waves(vx, np.arange(LEN // 2), LEN, OH),
        waves(vz, np.arange(KZ), LZ, OH) * weight,
        turn,
    )


def line_tables():
    def table(outs, ins, sign):
        p = 2.0 * np.pi * (np.outer(np.arange(outs), np.arange(ins)) % LEN) / LEN
        c, s = np.cos(p), np.sin(p) * sign
        return c, s

    c, s = table(LEN, LEN, 1.0)
    region = rounded(np.block([[c, s], [-s, c]]))
    c, s = table(LEN, K, 1.0)
    template = rounded(np.block([[c, s], [-s, c]]))
    c, s = table(EDGE, LEN, 1.0)
    back = rounded(np.block([[c, -s], [s, c]]))
    return region, template, back


def place():
    position = lax.axis_index("tile").astype(jnp.int32)
    return position // XT, position % XT


def pack_kernel(
    near_bit,
    masks,
    range_hbm,
    angle_hbm,
    proj_hbm,
    turns_ref,
    home_ref,
    near_ref,
    give_ref,
    mine_ref,
    proj_ref,
    angle_ref,
    range_ref,
    rows_ref,
    sem,
):
    fetch = [
        pltpu.make_async_copy(range_hbm, range_ref, sem.at[0]),
        pltpu.make_async_copy(angle_hbm, angle_ref, sem.at[1]),
        pltpu.make_async_copy(proj_hbm, proj_ref, sem.at[2]),
    ]
    for copy in fetch:
        copy.start()
    fetch[1].wait()
    for i, wave in enumerate((jnp.cos, jnp.sin)):
        spread = jnp.broadcast_to(wave(angle_ref[...]), (128, angle_ref.shape[1])).T
        turns_ref[i, :, :128] = spread
        turns_ref[i, :, 128:] = spread
    fetch[0].wait()
    fetch[2].wait()
    n_tilt, n_det, y_count = proj_ref.shape
    depth = home_ref.shape[1]
    y = lax.broadcasted_iota(jnp.int32, (n_det, y_count), 1)
    parts = []
    for t in range(n_tilt):
        keep = (y >= range_ref[0, t]) & (y < range_ref[1, t])
        parts.append(jnp.where(keep, proj_ref[t].astype(F32), 0.0))
    if depth > n_tilt * n_det:
        parts.append(jnp.zeros((depth - n_tilt * n_det, y_count), F32))
    edge = jnp.zeros((HALO, depth), F32)
    rows_ref[...] = jnp.concatenate([edge, jnp.concatenate(parts, 0).T, edge], 0).astype(BF)
    chip, core = place()

    def rows(target):
        return rows_ref[pl.ds(pl.multiple_of(target * EDGE, EDGE), LEN)]

    home_ref[...] = rows(chip)
    near_ref[...] = rows(chip ^ near_bit)
    give_ref[0] = home_ref[...]
    for j, mask in enumerate(masks):
        mine_ref[j] = rows(chip ^ mask ^ (near_bit * core))
        give_ref[1 + j] = rows(chip ^ mask ^ (near_bit * (1 - core)))


def merge_kernel(mine_ref, got_ref, done_ref, *out_refs):
    done_ref[...] = jnp.zeros_like(done_ref)
    for j, out_ref in enumerate(out_refs):
        out_ref[0] = mine_ref[j]
        out_ref[1] = got_ref[1 + j]


def build_weights(n_det, n_tile, pairs, col, turns_ref, w_ref, whole_ref, part_ref):
    depth = whole_ref.shape[0]
    lane = lax.broadcasted_iota(jnp.int32, (n_det, LB), 1)
    step = lane // Z
    pack = 16 // n_det
    own = lax.broadcasted_iota(jnp.int32, (n_det, LB), 0).astype(F32)
    top = NTILT // pack * pack
    tail = depth - top * n_det
    base = 0
    for q, sources in enumerate(pairs):
        block = jnp.where(col == 0, q, NQ - 1 - q)
        flip = (block * LB + lane) >= VH
        x = jnp.where(flip, XB - 1 - step + jnp.where(block == NQ // 2, XB // 2, 0), step)
        x = x + (block * XB + col * (X - XR))
        x = VOXEL * (x.astype(F32) - (X - 1) / 2.0)
        z = jnp.where(flip, Z - 1 - lane % Z, lane % Z)
        z = VOXEL * (z.astype(F32) - (Z - 1) / 2.0)

        def tilt(t, z=z, x=x):
            pos = x * turns_ref[0, t : t + 1] + z * turns_ref[1, t : t + 1] + (NDET - 1) / 2.0
            whole = jnp.floor(pos)
            return own - whole, pos - whole

        for first in range(0, NTILT, pack):
            got = [tilt(t) for t in range(first, min(first + pack, NTILT))]
            rows = pack * n_det if first < top else tail
            gap = rows - len(got) * n_det
            for ref, values in ((whole_ref, [g[0] for g in got]), (part_ref, [g[1] for g in got])):
                if gap:
                    values.append(jnp.zeros((gap, LB), F32))
                ref[first * n_det : first * n_det + rows] = jnp.concatenate(values, 0).astype(BF)

        def build(j, carry, base=base, first=sources[0]):
            src = first + j
            src = jnp.where(col == 0, src, n_tile - 1 - src)
            shift = (src * n_det).astype(F32).astype(BF)
            off = (whole_ref[...] + shift) - part_ref[...]
            one = jnp.ones((), BF)
            w_ref[base + j] = jnp.maximum(one - jnp.abs(off), jnp.zeros((), BF))
            return carry

        lax.fori_loop(0, len(sources), build, 0)
        base += len(sources)


def build_planes(fx_ref, fz_ref, ix_ref, iz_ref, plane_ref, inverse_ref):
    def forward(x, carry):
        cos_x, sin_x = fx_ref[0, pl.ds(x, 1)], fx_ref[1, pl.ds(x, 1)]
        cos_z, sin_z = fz_ref[0], fz_ref[1]
        at = pl.ds(pl.multiple_of(x * Z, Z), Z)
        plane_ref[at, :FP] = (cos_x * cos_z - sin_x * sin_z).astype(BF)
        plane_ref[at, FP:] = (-sin_x * cos_z - cos_x * sin_z).astype(BF)
        return carry

    lax.fori_loop(0, XR // 2, forward, 0)
    odd = lax.broadcasted_iota(jnp.int32, (1, OH), 1) // EDGE % 2
    turn = 1.0 - 2.0 * odd.astype(F32)

    def inverse(k, carry):
        cos_z, sin_z = iz_ref[0, pl.ds(k, 1)], iz_ref[1, pl.ds(k, 1)]
        cos_x, sin_x = ix_ref[0], ix_ref[1]
        real = cos_x * cos_z - sin_x * sin_z
        imag = -sin_x * cos_z - cos_x * sin_z
        low = pl.multiple_of(k * LEN, 16)
        inverse_ref[pl.ds(low, LEN)] = jnp.concatenate([real, imag * turn], 0).astype(BF)
        inverse_ref[pl.ds(FP + low, LEN)] = jnp.concatenate([imag, -real * turn], 0).astype(BF)
        return carry

    lax.fori_loop(0, KZ, inverse, 0)
    inverse_ref[NF:FP] = jnp.zeros((FP - NF, OH), BF)
    inverse_ref[FP + NF :] = jnp.zeros((FP - NF, OH), BF)


def build_templates(col, rot_ref, bank_ref, plane_ref, line_ref, turn_ref, out_ref):
    chosen = jnp.concatenate([bank_ref[rot_ref[r]] for r in range(NTPL)], 0)
    plane = jnp.concatenate([plane_ref[b * Z : b * Z + K] for b in range(K)], 0)
    flat = jnp.dot(chosen, plane, preferred_element_type=F32).astype(BF)
    cos = jnp.where(col == 0, turn_ref[0, 0:1], turn_ref[0, 1:2])
    sin = jnp.where(col == 0, turn_ref[1, 0:1], turn_ref[1, 1:2])
    for r in range(NTPL):
        part = flat[r * K : (r + 1) * K]
        stacked = jnp.concatenate([part[:, :FP], part[:, FP:]], 0)
        full = jnp.dot(line_ref[...], stacked, preferred_element_type=F32)
        real, imag = full[:LEN], -full[LEN:]
        out_ref[r, :LEN] = (real * cos - imag * sin).astype(BF)
        out_ref[r, LEN:] = (real * sin + imag * cos).astype(BF)


def prepare_kernel(n_det, n_tile, pairs, turns_ref, _, *refs):
    sources, outs, targets, (sem, whole_ref, part_ref) = refs[:8], refs[8:13], refs[13:21], refs[21:]
    fetch = [
        pltpu.make_async_copy(a, b, sem.at[i]) for i, (a, b) in enumerate(zip(sources, targets))
    ]
    for copy in fetch:
        copy.start()
    w_ref, plane_ref, inverse_ref, tmpl_ref, done_ref = outs
    _, col = place()
    build_weights(n_det, n_tile, pairs, col, turns_ref, w_ref, whole_ref, part_ref)
    for copy in fetch:
        copy.wait()
    rot_ref, bank_ref, fx_ref, fz_ref, ix_ref, iz_ref, line_ref, turn_ref = targets
    build_planes(fx_ref, fz_ref, ix_ref, iz_ref, plane_ref, inverse_ref)
    build_templates(col, rot_ref, bank_ref, plane_ref, line_ref, turn_ref, tmpl_ref)
    done_ref[...] = jnp.zeros_like(done_ref)


def join_kernel(near_ref, *refs):
    out_ref = refs[-1]
    out_ref[0] = near_ref[...]
    for j, ref in enumerate(refs[:-1]):
        out_ref[1 + 2 * j] = ref[0]
        out_ref[2 + 2 * j] = ref[1]


def gather_pieces(near_bit, masks, from_mate, data_ref, home_ref, got_ref, near_ref, held_ref):
    chip, core = place()
    mate = 1 - core
    data_ref[chip * XT + core] = home_ref[...]
    data_ref[chip * XT + mate] = got_ref[0]
    data_ref[(chip ^ near_bit) * XT + core] = near_ref[0]
    taker, other = (mate, core) if from_mate else (core, mate)
    for j, mask in enumerate(masks):
        source = (chip ^ mask ^ (near_bit * taker)) * XT
        data_ref[source + taker] = held_ref[1 + 2 * j]
        data_ref[source + other] = held_ref[2 + 2 * j]
    return (chip ^ near_bit) * XT + mate


def partial_sums(n_tile, pairs, upper, core, data_ref, w_ref, late=None):
    base = 0
    for sources in pairs:
        total = jnp.zeros((LEN, LB), F32)
        if late is not None:
            inside = (late >= sources[0]) & (late <= sources[-1])
            part = data_ref[jnp.where(inside, n_tile - 1 - late, n_tile)]
            weight = w_ref[base + jnp.clip(late, sources[0], sources[-1]) - sources[0]]
            total += jnp.dot(part, weight, preferred_element_type=F32)
        for j, src in enumerate(sources):
            if (src >= n_tile // 2) == upper:
                part = data_ref[jnp.where(core == 0, src, n_tile - 1 - src)]
                total += jnp.dot(part, w_ref[base + j], preferred_element_type=F32)
        base += len(sources)
        yield total


def half_kernel(near_bit, masks, pairs, n_tile, *refs):
    home_ref, got_ref, held_ref, w_ref, _, half_ref, data_ref = refs
    absent = gather_pieces(
        near_bit, masks, False, data_ref, home_ref, got_ref, held_ref, held_ref
    )
    data_ref[absent] = jnp.zeros(data_ref.shape[1:], BF)
    chip, core = place()
    for upper in (False, True):

        @pl.when((chip >= near_bit) == upper)
        def _():
            for q, total in enumerate(partial_sums(n_tile, pairs, upper, core, data_ref, w_ref)):
                half_ref[q] = total


def score_kernel(near_bit, masks, pairs, n_tile, *refs):
    home_ref, got_ref, held_ref, swap_ref = refs[:4]
    half_ref, w_ref, tmpl_ref, plane_ref, line_ref, back_ref, inverse_ref = refs[4:11]
    out_ref, data_ref, vol_ref, mid_ref = refs[11:]
    absent = gather_pieces(near_bit, masks, True, data_ref, home_ref, got_ref, held_ref, swap_ref)
    data_ref[absent] = swap_ref[0]
    chip, core = place()
    data_ref[n_tile] = jnp.zeros(data_ref.shape[1:], BF)
    for upper in (False, True):
        for col in range(XT):

            @pl.when(((chip < near_bit) == upper) & (core == col))
            def _():
                late = n_tile - 1 - absent if col else None
                sums = partial_sums(n_tile, pairs, upper, col, data_ref, w_ref, late)
                for q, total in enumerate(sums):
                    low = (NQ - 1 - q if col else q) * LB
                    vol_ref[:, low : low + LB] = total + half_ref[q]

    near_half = vol_ref[:, :VH]
    far_half = jnp.concatenate(
        [vol_ref[:, 4 * LB :], vol_ref[:, 3 * LB : 4 * LB], vol_ref[:, VH : 3 * LB]], 1
    )
    even, odd = (near_half + far_half).astype(BF), (near_half - far_half).astype(BF)
    stacked = jnp.concatenate(
        [
            jnp.dot(even, plane_ref[:, :FP], preferred_element_type=F32).astype(BF),
            jnp.dot(odd, plane_ref[:, FP:], preferred_element_type=F32).astype(BF),
        ],
        0,
    )
    full = jnp.dot(line_ref[...], stacked, preferred_element_type=F32)
    real, imag = full[:LEN], full[LEN:]
    for r in range(NTPL):
        t_real = tmpl_ref[r, :LEN].astype(F32)
        t_imag = tmpl_ref[r, LEN:].astype(F32)
        prod = jnp.concatenate(
            [
                (t_real * real - t_imag * imag).astype(BF),
                (t_real * imag + t_imag * real).astype(BF),
            ],
            0,
        )
        line = jnp.dot(back_ref[...], prod, preferred_element_type=F32).astype(BF)
        mid_ref[r * EDGE : (r + 1) * EDGE, :FP] = line[:EDGE]
        mid_ref[r * EDGE : (r + 1) * EDGE, FP:] = line[EDGE:]
    even = jnp.dot(mid_ref[:, :FP], inverse_ref[:FP], preferred_element_type=F32)
    odd = jnp.dot(mid_ref[:, FP:], inverse_ref[FP:], preferred_element_type=F32)
    best = even[:EDGE] + odd[:EDGE]
    mirrored = even[:EDGE] - odd[:EDGE]
    for r in range(1, NTPL):
        at = slice(r * EDGE, (r + 1) * EDGE)
        best = jnp.maximum(best, even[at] + odd[at])
        mirrored = jnp.maximum(mirrored, even[at] - odd[at])
    out_ref[0, :, :OH] = best * SCALE
    mirrored = mirrored * SCALE
    order = 127 - lax.broadcasted_iota(jnp.int32, (EDGE, 128), 1)
    for low in range(0, OH, 128):
        part = jnp.take_along_axis(mirrored[:, low : low + 128], order, axis=1)
        out_ref[0, :, 2 * OH - 128 - low : 2 * OH - low] = part


VMEM = pl.BlockSpec(memory_space=pltpu.VMEM)
SMEM = pl.BlockSpec(memory_space=pltpu.SMEM)
HBM = pl.BlockSpec(memory_space=pltpu.HBM)


def limit(mib):
    return pltpu.CompilerParams(vmem_limit_bytes=mib << 20)


def cost(flops, nbytes):
    return pl.CostEstimate(flops=flops, bytes_accessed=nbytes, transcendentals=0)


def pinned(array):
    return pltpu.with_memory_space_constraint(array, pltpu.HBM)


def shape(*dims, dtype=BF):
    return jax.ShapeDtypeStruct(dims, dtype)


def solution(mesh):
    n_tile = mesh.shape["tile"]
    n_block = n_tile // XT
    n_det = NDET // n_tile
    depth = (NTILT * n_det + 127) // 128 * 128
    near_bit = n_block // 2
    masks = [k for k in range(1, n_block) if not k & near_bit]
    masks.sort(key=lambda k: k != near_bit // 2)
    n_op = len(masks)
    pairs = pair_list(n_det)
    n_pair = sum(len(p) for p in pairs)
    tables = plane_tables()
    line, line_t, back = line_tables()
    mate = [(i, i ^ 1) for i in range(n_tile)]
    near_pairs = [(i, i ^ (near_bit * XT)) for i in range(n_tile)]

    def route(mask):
        return [(i, i ^ (mask * XT) ^ (near_bit * XT * (i % XT))) for i in range(n_tile)]

    def local(projections, tilt_angle, row_range, template_bank, rot_index):
        y_count = projections.shape[0]
        by_y = jnp.transpose(projections, (1, 2, 0))
        turns, home, near, give, mine = pl.pallas_call(
            lambda *refs: pack_kernel(near_bit, masks, *refs),
            out_shape=(
                shape(2, NTILT, LB, dtype=F32),
                shape(LEN, depth),
                shape(LEN, depth),
                shape(1 + n_op, LEN, depth),
                shape(n_op, LEN, depth),
            ),
            in_specs=[HBM, HBM, HBM],
            out_specs=(VMEM,) * 5,
            scratch_shapes=[
                pltpu.VMEM(by_y.shape, BF),
                pltpu.VMEM((1, NTILT), F32),
                pltpu.SMEM((2, NTILT), jnp.int32),
                pltpu.VMEM((y_count + 2 * HALO, depth), BF),
                pltpu.SemaphoreType.DMA((3,)),
            ],
            compiler_params=limit(8),
        )(pinned(row_range.T), pinned(tilt_angle.reshape(1, NTILT)), pinned(by_y))
        got = lax.ppermute(give, "tile", mate)
        near_in = lax.ppermute(near, "tile", near_pairs)
        merged, *payload = pl.pallas_call(
            merge_kernel,
            out_shape=(shape(8, 128, dtype=F32),) + (shape(2, LEN, depth),) * n_op,
            in_specs=[VMEM, VMEM],
            out_specs=(VMEM,) * (1 + n_op),
            compiler_params=limit(8),
        )(mine, got)
        arrived = [lax.ppermute(p, "tile", route(m)) for p, m in zip(payload, masks)]
        constants = (
            rot_index,
            template_bank,
            *[jnp.asarray(t, F32) for t in tables[:4]],
            jnp.asarray(line_t),
            jnp.asarray(tables[4], F32),
        )
        weights, plane, inverse, spectra, done = pl.pallas_call(
            lambda *refs: prepare_kernel(n_det, n_tile, pairs, *refs),
            out_shape=(
                shape(n_pair, depth, LB),
                shape(VH, 2 * FP),
                shape(2 * FP, OH),
                shape(NTPL, 2 * LEN, FP),
                shape(8, 128, dtype=F32),
            ),
            in_specs=[VMEM, VMEM] + [HBM] * 8,
            out_specs=(VMEM,) * 5,
            scratch_shapes=[
                pltpu.SMEM((NTPL,), jnp.int32),
                *[pltpu.VMEM(c.shape, c.dtype) for c in constants[1:]],
                pltpu.SemaphoreType.DMA((8,)),
                pltpu.VMEM((depth, LB), BF),
                pltpu.VMEM((depth, LB), BF),
            ],
            compiler_params=limit(24),
            cost_estimate=cost(1 << 32, 16 << 20),
        )(turns, merged, *[pinned(c) for c in constants])
        near_in, done, *arrived = lax.optimization_barrier((near_in, done, *arrived))
        held = pl.pallas_call(
            join_kernel,
            out_shape=shape(1 + 2 * n_op, LEN, depth),
            in_specs=[VMEM] * (1 + n_op),
            out_specs=VMEM,
            compiler_params=limit(4),
        )(near_in, *arrived)
        swapped = lax.ppermute(held, "tile", mate)
        pieces = pltpu.VMEM((n_tile + 1, LEN, depth), BF)
        half = pl.pallas_call(
            lambda *refs: half_kernel(near_bit, masks, pairs, n_tile, *refs),
            out_shape=shape(NQ, LEN, LB, dtype=F32),
            in_specs=[VMEM] * 5,
            out_specs=VMEM,
            scratch_shapes=[pieces],
            compiler_params=limit(12),
            cost_estimate=cost(n_pair * LEN * depth * LB, n_pair * depth * LB),
        )(home, got, held, weights, done)
        return pl.pallas_call(
            lambda *refs: score_kernel(near_bit, masks, pairs, n_tile, *refs),
            out_shape=shape(1, EDGE, EDGE * Z, dtype=F32),
            in_specs=[VMEM] * 11,
            out_specs=VMEM,
            scratch_shapes=[
                pieces,
                pltpu.VMEM((LEN, XR * Z), F32),
                pltpu.VMEM((NTPL * EDGE, 2 * FP), BF),
            ],
            compiler_params=limit(28),
            cost_estimate=cost(4 << 30, 20 << 20),
        )(
            home,
            got,
            held,
            swapped,
            half,
            weights,
            spectra,
            plane,
            jnp.asarray(line),
            jnp.asarray(back),
            inverse,
        )

    return jax.shard_map(
        local,
        mesh=mesh,
        in_specs=(P("grp", None, "tile"), P("grp"), P("grp", None), P(), P()),
        out_specs=P("tile", "grp", None),
        check_vma=False,
    )
```

```python
import math

import jax
import jax.numpy as jnp
import numpy as np
from jax import lax
from jax.experimental import pallas as pl
from jax.experimental.pallas import tpu as pltpu
from jax.sharding import PartitionSpec as P

EDGE = 32
XT = 2
K = 16
NTILT = 61
NTPL = 8
NDET = 128
HALO = K // 2
LEN = EDGE + K
X = XT * EDGE
Z = EDGE
XR = EDGE + HALO
LZ = Z + HALO
KZ = LZ // 2 + 1
NF = LEN * KZ
FP = 1024
VH = XR * Z // 2
OH = EDGE * EDGE // 2
XB = 8
NQ = XR // XB
LB = XB * Z
MAX_ANGLE = 1.05
VOXEL = 1.4
SCALE = 1.0 / (LEN * LEN * LZ)
BF = jnp.bfloat16
F32 = jnp.float32


def reach(q):
    x = np.arange(q * XB, (q + 1) * XB) - (X - 1) / 2.0
    z = np.arange(Z) - (Z - 1) / 2.0
    top = 0.0
    low = 0.0
    angle = np.linspace(-MAX_ANGLE, MAX_ANGLE, 4001)
    first = True
    for xv in (x[0], x[-1]):
        for zv in (z[0], z[-1]):
            pos = VOXEL * (xv * np.cos(angle) + zv * np.sin(angle)) + (NDET - 1) / 2.0
            low = pos.min() if first else min(low, pos.min())
            top = pos.max() if first else max(top, pos.max())
            first = False
    return math.ceil(low - 1.0 - 0.01), math.floor(top + 1.0 + 0.01)


def pair_list(n_det):
    pairs = []
    for q in range(NQ):
        low, top = reach(q)
        pairs.append(list(range(max(low, 0) // n_det, min(top, NDET - 1) // n_det + 1)))
    return pairs


def rounded(table):
    return np.asarray(table, np.float32).astype(jnp.bfloat16)


def plane_tables():
    kz = np.repeat(np.arange(KZ), LEN)
    kx = np.tile(np.arange(LEN), KZ)
    mid = (EDGE - 1) / 2.0

    def waves(k, at, length, width):
        p = 2.0 * np.pi * (np.outer(at, k) % length) / length
        out = np.zeros((2, len(at), width), np.float32)
        out[0, :, : len(k)], out[1, :, : len(k)] = np.cos(p), np.sin(p)
        return out

    vx = np.repeat(np.arange(EDGE // 2) - mid, EDGE)
    vz = np.tile(np.arange(EDGE) - mid, EDGE // 2)
    weight = np.full((KZ, 1), 2.0)
    weight[0] = weight[-1] = 1.0
    turn = np.zeros((2, XT, FP))
    for col in range(XT):
        back = HALO if col == 0 else 0
        p = 2.0 * np.pi * (kx * (mid - back) / LEN + kz * (mid - HALO) / LZ)
        turn[0, col, :NF], turn[1, col, :NF] = np.cos(p), np.sin(p)
    return (
        waves(kx, np.arange(XR // 2) - (XR - 1) / 2.0, LEN, FP),
        waves(kz, np.arange(Z) - (Z - 1) / 2.0, LZ, FP),
        waves(vx, np.arange(LEN // 2), LEN, OH),
        waves(vz, np.arange(KZ), LZ, OH) * weight,
        turn,
    )


def line_tables():
    def table(outs, ins, sign):
        p = 2.0 * np.pi * (np.outer(np.arange(outs), np.arange(ins)) % LEN) / LEN
        c, s = np.cos(p), np.sin(p) * sign
        return c, s

    c, s = table(LEN, LEN, 1.0)
    region = rounded(np.block([[c, s], [-s, c]]))
    c, s = table(LEN, K, 1.0)
    template = rounded(np.block([[c, s], [-s, c]]))
    c, s = table(EDGE, LEN, 1.0)
    back = rounded(np.block([[c, -s], [s, c]]))
    return region, template, back


def place():
    position = lax.axis_index("tile").astype(jnp.int32)
    return position // XT, position % XT


def pack_kernel(
    near_bit,
    masks,
    range_hbm,
    angle_hbm,
    proj_hbm,
    turns_ref,
    home_ref,
    near_ref,
    give_ref,
    mine_ref,
    proj_ref,
    angle_ref,
    range_ref,
    rows_ref,
    sem,
):
    fetch = [
        pltpu.make_async_copy(range_hbm, range_ref, sem.at[0]),
        pltpu.make_async_copy(angle_hbm, angle_ref, sem.at[1]),
        pltpu.make_async_copy(proj_hbm, proj_ref, sem.at[2]),
    ]
    for copy in fetch:
        copy.start()
    fetch[1].wait()
    for i, wave in enumerate((jnp.cos, jnp.sin)):
        spread = jnp.broadcast_to(wave(angle_ref[...]), (128, angle_ref.shape[1])).T
        turns_ref[i, :, :128] = spread
        turns_ref[i, :, 128:] = spread
    fetch[0].wait()
    fetch[2].wait()
    n_tilt, n_det, y_count = proj_ref.shape
    depth = home_ref.shape[1]
    y = lax.broadcasted_iota(jnp.int32, (n_det, y_count), 1)
    parts = []
    for t in range(n_tilt):
        keep = (y >= range_ref[0, t]) & (y < range_ref[1, t])
        parts.append(jnp.where(keep, proj_ref[t].astype(F32), 0.0))
    if depth > n_tilt * n_det:
        parts.append(jnp.zeros((depth - n_tilt * n_det, y_count), F32))
    edge = jnp.zeros((HALO, depth), F32)
    rows_ref[...] = jnp.concatenate([edge, jnp.concatenate(parts, 0).T, edge], 0).astype(BF)
    chip, core = place()

    def rows(target):
        return rows_ref[pl.ds(pl.multiple_of(target * EDGE, EDGE), LEN)]

    home_ref[...] = rows(chip)
    near_ref[...] = rows(chip ^ near_bit)
    give_ref[0] = home_ref[...]
    for j, mask in enumerate(masks):
        mine_ref[j] = rows(chip ^ mask ^ (near_bit * core))
        give_ref[1 + j] = rows(chip ^ mask ^ (near_bit * (1 - core)))


def merge_kernel(mine_ref, got_ref, done_ref, *out_refs):
    done_ref[...] = jnp.zeros_like(done_ref)
    for j, out_ref in enumerate(out_refs):
        out_ref[0] = mine_ref[j]
        out_ref[1] = got_ref[1 + j]


def build_weights(n_det, n_tile, pairs, col, turns_ref, w_ref, whole_ref, part_ref):
    depth = whole_ref.shape[0]
    lane = lax.broadcasted_iota(jnp.int32, (n_det, LB), 1)
    step = lane // Z
    pack = 16 // n_det
    own = lax.broadcasted_iota(jnp.int32, (n_det, LB), 0).astype(F32)
    top = NTILT // pack * pack
    tail = depth - top * n_det
    base = 0
    for q, sources in enumerate(pairs):
        block = jnp.where(col == 0, q, NQ - 1 - q)
        flip = (block * LB + lane) >= VH
        x = jnp.where(flip, XB - 1 - step + jnp.where(block == NQ // 2, XB // 2, 0), step)
        x = x + (block * XB + col * (X - XR))
        x = VOXEL * (x.astype(F32) - (X - 1) / 2.0)
        z = jnp.where(flip, Z - 1 - lane % Z, lane % Z)
        z = VOXEL * (z.astype(F32) - (Z - 1) / 2.0)

        def tilt(t, z=z, x=x):
            pos = x * turns_ref[0, t : t + 1] + z * turns_ref[1, t : t + 1] + (NDET - 1) / 2.0
            whole = jnp.floor(pos)
            return own - whole, pos - whole

        for first in range(0, NTILT, pack):
            got = [tilt(t) for t in range(first, min(first + pack, NTILT))]
            rows = pack * n_det if first < top else tail
            gap = rows - len(got) * n_det
            for ref, values in ((whole_ref, [g[0] for g in got]), (part_ref, [g[1] for g in got])):
                if gap:
                    values.append(jnp.zeros((gap, LB), F32))
                ref[first * n_det : first * n_det + rows] = jnp.concatenate(values, 0).astype(BF)

        def build(j, carry, base=base, first=sources[0]):
            src = first + j
            src = jnp.where(col == 0, src, n_tile - 1 - src)
            shift = (src * n_det).astype(F32).astype(BF)
            off = (whole_ref[...] + shift) - part_ref[...]
            one = jnp.ones((), BF)
            w_ref[base + j] = jnp.maximum(one - jnp.abs(off), jnp.zeros((), BF))
            return carry

        lax.fori_loop(0, len(sources), build, 0)
        base += len(sources)


def build_planes(fx_ref, fz_ref, ix_ref, iz_ref, plane_ref, inverse_ref):
    def forward(x, carry):
        cos_x, sin_x = fx_ref[0, pl.ds(x, 1)], fx_ref[1, pl.ds(x, 1)]
        cos_z, sin_z = fz_ref[0], fz_ref[1]
        at = pl.ds(pl.multiple_of(x * Z, Z), Z)
        plane_ref[at, :FP] = (cos_x * cos_z - sin_x * sin_z).astype(BF)
        plane_ref[at, FP:] = (-sin_x * cos_z - cos_x * sin_z).astype(BF)
        return carry

    lax.fori_loop(0, XR // 2, forward, 0)
    odd = lax.broadcasted_iota(jnp.int32, (1, OH), 1) // EDGE % 2
    turn = 1.0 - 2.0 * odd.astype(F32)

    def inverse(k, carry):
        cos_z, sin_z = iz_ref[0, pl.ds(k, 1)], iz_ref[1, pl.ds(k, 1)]
        cos_x, sin_x = ix_ref[0], ix_ref[1]
        real = cos_x * cos_z - sin_x * sin_z
        imag = -sin_x * cos_z - cos_x * sin_z
        low = pl.multiple_of(k * LEN, 16)
        inverse_ref[pl.ds(low, LEN)] = jnp.concatenate([real, imag * turn], 0).astype(BF)
        inverse_ref[pl.ds(FP + low, LEN)] = jnp.concatenate([imag, -real * turn], 0).astype(BF)
        return carry

    lax.fori_loop(0, KZ, inverse, 0)
    inverse_ref[NF:FP] = jnp.zeros((FP - NF, OH), BF)
    inverse_ref[FP + NF :] = jnp.zeros((FP - NF, OH), BF)


def flat_templates(rot_ref, bank_ref, plane_ref, flat_ref):
    chosen = jnp.concatenate([bank_ref[rot_ref[r]] for r in range(NTPL)], 0)
    plane = jnp.concatenate([plane_ref[b * Z : b * Z + K] for b in range(K)], 0)
    flat_ref[...] = jnp.dot(chosen, plane, preferred_element_type=F32).astype(BF)


def template_kernel(_, flat_ref, line_ref, turn_ref, out_ref, done_ref):
    done_ref[...] = jnp.zeros_like(done_ref)
    _, col = place()
    cos = jnp.where(col == 0, turn_ref[0, 0:1], turn_ref[0, 1:2])
    sin = jnp.where(col == 0, turn_ref[1, 0:1], turn_ref[1, 1:2])
    for r in range(NTPL):
        part = flat_ref[r * K : (r + 1) * K]
        stacked = jnp.concatenate([part[:, :FP], part[:, FP:]], 0)
        full = jnp.dot(line_ref[...], stacked, preferred_element_type=F32)
        real, imag = full[:LEN], -full[LEN:]
        out_ref[r, :LEN] = (real * cos - imag * sin).astype(BF)
        out_ref[r, LEN:] = (real * sin + imag * cos).astype(BF)


def prepare_kernel(n_det, n_tile, pairs, turns_ref, _, *refs):
    sources, outs, targets, (sem, whole_ref, part_ref) = refs[:6], refs[6:11], refs[11:17], refs[17:]
    fetch = [
        pltpu.make_async_copy(a, b, sem.at[i]) for i, (a, b) in enumerate(zip(sources, targets))
    ]
    for copy in fetch:
        copy.start()
    w_ref, plane_ref, inverse_ref, flat_ref, done_ref = outs
    _, col = place()
    build_weights(n_det, n_tile, pairs, col, turns_ref, w_ref, whole_ref, part_ref)
    for copy in fetch:
        copy.wait()
    rot_ref, bank_ref, fx_ref, fz_ref, ix_ref, iz_ref = targets
    build_planes(fx_ref, fz_ref, ix_ref, iz_ref, plane_ref, inverse_ref)
    flat_templates(rot_ref, bank_ref, plane_ref, flat_ref)
    done_ref[...] = jnp.zeros_like(done_ref)


def join_kernel(*refs):
    out_ref = refs[-1]
    for j, ref in enumerate(refs[:-1]):
        out_ref[2 * j] = ref[0]
        out_ref[2 * j + 1] = ref[1]


def gather_pieces(near_bit, masks, from_mate, data_ref, home_ref, got_ref, near_ref, near_swap_ref, held_ref):
    chip, core = place()
    mate = 1 - core
    data_ref[chip * XT + core] = home_ref[...]
    data_ref[chip * XT + mate] = got_ref[0]
    data_ref[(chip ^ near_bit) * XT + core] = near_ref[...]
    data_ref[(chip ^ near_bit) * XT + mate] = near_swap_ref[...]
    taker, other = (mate, core) if from_mate else (core, mate)
    for j, mask in enumerate(masks):
        source = (chip ^ mask ^ (near_bit * taker)) * XT
        data_ref[source + taker] = held_ref[2 * j]
        data_ref[source + other] = held_ref[2 * j + 1]


def partial_sums(n_tile, pairs, upper, core, data_ref, w_ref):
    base = 0
    for sources in pairs:
        total = jnp.zeros((LEN, LB), F32)
        for j, src in enumerate(sources):
            if (src >= n_tile // 2) == upper:
                part = data_ref[jnp.where(core == 0, src, n_tile - 1 - src)]
                total += jnp.dot(part, w_ref[base + j], preferred_element_type=F32)
        base += len(sources)
        yield total


def half_kernel(near_bit, masks, pairs, n_tile, *refs):
    *pieces, w_ref, _, half_ref, data_ref = refs
    gather_pieces(near_bit, masks, False, data_ref, *pieces)
    chip, core = place()
    for upper in (False, True):

        @pl.when((chip >= near_bit) == upper)
        def _():
            for q, total in enumerate(partial_sums(n_tile, pairs, upper, core, data_ref, w_ref)):
                half_ref[q] = total


def score_kernel(near_bit, masks, pairs, n_tile, *refs):
    half_ref, w_ref, tmpl_ref, plane_ref, line_ref, back_ref, inverse_ref = refs[5:12]
    out_ref, data_ref, vol_ref, mid_ref = refs[12:]
    gather_pieces(near_bit, masks, True, data_ref, *refs[:5])
    chip, core = place()
    for upper in (False, True):
        for col in range(XT):

            @pl.when(((chip < near_bit) == upper) & (core == col))
            def _():
                for q, total in enumerate(partial_sums(n_tile, pairs, upper, col, data_ref, w_ref)):
                    low = (NQ - 1 - q if col else q) * LB
                    vol_ref[:, low : low + LB] = total + half_ref[q]

    near_half = vol_ref[:, :VH]
    far_half = jnp.concatenate(
        [vol_ref[:, 4 * LB :], vol_ref[:, 3 * LB : 4 * LB], vol_ref[:, VH : 3 * LB]], 1
    )
    even, odd = (near_half + far_half).astype(BF), (near_half - far_half).astype(BF)
    stacked = jnp.concatenate(
        [
            jnp.dot(even, plane_ref[:, :FP], preferred_element_type=F32).astype(BF),
            jnp.dot(odd, plane_ref[:, FP:], preferred_element_type=F32).astype(BF),
        ],
        0,
    )
    full = jnp.dot(line_ref[...], stacked, preferred_element_type=F32)
    real, imag = full[:LEN], full[LEN:]
    for r in range(NTPL):
        t_real = tmpl_ref[r, :LEN].astype(F32)
        t_imag = tmpl_ref[r, LEN:].astype(F32)
        prod = jnp.concatenate(
            [
                (t_real * real - t_imag * imag).astype(BF),
                (t_real * imag + t_imag * real).astype(BF),
            ],
            0,
        )
        line = jnp.dot(back_ref[...], prod, preferred_element_type=F32).astype(BF)
        mid_ref[r * EDGE : (r + 1) * EDGE, :FP] = line[:EDGE]
        mid_ref[r * EDGE : (r + 1) * EDGE, FP:] = line[EDGE:]
    even = jnp.dot(mid_ref[:, :FP], inverse_ref[:FP], preferred_element_type=F32)
    odd = jnp.dot(mid_ref[:, FP:], inverse_ref[FP:], preferred_element_type=F32)
    best = even[:EDGE] + odd[:EDGE]
    mirrored = even[:EDGE] - odd[:EDGE]
    for r in range(1, NTPL):
        at = slice(r * EDGE, (r + 1) * EDGE)
        best = jnp.maximum(best, even[at] + odd[at])
        mirrored = jnp.maximum(mirrored, even[at] - odd[at])
    out_ref[0, :, :OH] = best * SCALE
    mirrored = mirrored * SCALE
    order = 127 - lax.broadcasted_iota(jnp.int32, (EDGE, 128), 1)
    for low in range(0, OH, 128):
        part = jnp.take_along_axis(mirrored[:, low : low + 128], order, axis=1)
        out_ref[0, :, 2 * OH - 128 - low : 2 * OH - low] = part


VMEM = pl.BlockSpec(memory_space=pltpu.VMEM)
SMEM = pl.BlockSpec(memory_space=pltpu.SMEM)
HBM = pl.BlockSpec(memory_space=pltpu.HBM)


def limit(mib):
    return pltpu.CompilerParams(vmem_limit_bytes=mib << 20)


def cost(flops, nbytes):
    return pl.CostEstimate(flops=flops, bytes_accessed=nbytes, transcendentals=0)


def pinned(array):
    return pltpu.with_memory_space_constraint(array, pltpu.HBM)


def shape(*dims, dtype=BF):
    return jax.ShapeDtypeStruct(dims, dtype)


def solution(mesh):
    n_tile = mesh.shape["tile"]
    n_block = n_tile // XT
    n_det = NDET // n_tile
    depth = (NTILT * n_det + 127) // 128 * 128
    near_bit = n_block // 2
    masks = [k for k in range(1, n_block) if not k & near_bit]
    masks.sort(key=lambda k: k != near_bit // 2)
    n_op = len(masks)
    pairs = pair_list(n_det)
    n_pair = sum(len(p) for p in pairs)
    tables = plane_tables()
    line, line_t, back = line_tables()
    mate = [(i, i ^ 1) for i in range(n_tile)]
    near_pairs = [(i, i ^ (near_bit * XT)) for i in range(n_tile)]

    def route(mask):
        return [(i, i ^ (mask * XT) ^ (near_bit * XT * (i % XT))) for i in range(n_tile)]

    def local(projections, tilt_angle, row_range, template_bank, rot_index):
        y_count = projections.shape[0]
        by_y = jnp.transpose(projections, (1, 2, 0))
        turns, home, near, give, mine = pl.pallas_call(
            lambda *refs: pack_kernel(near_bit, masks, *refs),
            out_shape=(
                shape(2, NTILT, LB, dtype=F32),
                shape(LEN, depth),
                shape(LEN, depth),
                shape(1 + n_op, LEN, depth),
                shape(n_op, LEN, depth),
            ),
            in_specs=[HBM, HBM, HBM],
            out_specs=(VMEM,) * 5,
            scratch_shapes=[
                pltpu.VMEM(by_y.shape, BF),
                pltpu.VMEM((1, NTILT), F32),
                pltpu.SMEM((2, NTILT), jnp.int32),
                pltpu.VMEM((y_count + 2 * HALO, depth), BF),
                pltpu.SemaphoreType.DMA((3,)),
            ],
            compiler_params=limit(8),
        )(pinned(row_range.T), pinned(tilt_angle.reshape(1, NTILT)), pinned(by_y))
        got = lax.ppermute(give, "tile", mate)
        near_in = lax.ppermute(near, "tile", near_pairs)
        merged, *payload = pl.pallas_call(
            merge_kernel,
            out_shape=(shape(8, 128, dtype=F32),) + (shape(2, LEN, depth),) * n_op,
            in_specs=[VMEM, VMEM],
            out_specs=(VMEM,) * (1 + n_op),
            compiler_params=limit(8),
        )(mine, got)
        arrived = [lax.ppermute(p, "tile", route(m)) for p, m in zip(payload, masks)]
        constants = (
            rot_index,
            template_bank,
            *[jnp.asarray(t, F32) for t in tables[:4]],
        )
        weights, plane, inverse, flat, done = pl.pallas_call(
            lambda *refs: prepare_kernel(n_det, n_tile, pairs, *refs),
            out_shape=(
                shape(n_pair, depth, LB),
                shape(VH, 2 * FP),
                shape(2 * FP, OH),
                shape(NTPL * K, 2 * FP),
                shape(8, 128, dtype=F32),
            ),
            in_specs=[VMEM, VMEM] + [HBM] * 6,
            out_specs=(VMEM,) * 5,
            scratch_shapes=[
                pltpu.SMEM((NTPL,), jnp.int32),
                *[pltpu.VMEM(c.shape, c.dtype) for c in constants[1:]],
                pltpu.SemaphoreType.DMA((6,)),
                pltpu.VMEM((depth, LB), BF),
                pltpu.VMEM((depth, LB), BF),
            ],
            compiler_params=limit(24),
            cost_estimate=cost(1 << 32, 16 << 20),
        )(turns, merged, *[pinned(c) for c in constants])
        near_in, done = lax.optimization_barrier((near_in, done))
        near_swap = lax.ppermute(near_in, "tile", mate)
        spectra, done = pl.pallas_call(
            template_kernel,
            out_shape=(shape(NTPL, 2 * LEN, FP), shape(8, 128, dtype=F32)),
            in_specs=[VMEM] * 4,
            out_specs=(VMEM,) * 2,
            compiler_params=limit(8),
            cost_estimate=cost(1 << 20, 1 << 14),
        )(done, flat, jnp.asarray(line_t), jnp.asarray(tables[4], F32))
        done, near_swap, *arrived = lax.optimization_barrier((done, near_swap, *arrived))
        held = pl.pallas_call(
            join_kernel,
            out_shape=shape(2 * n_op, LEN, depth),
            in_specs=[VMEM] * n_op,
            out_specs=VMEM,
            compiler_params=limit(4),
        )(*arrived)
        swapped = lax.ppermute(held, "tile", mate)
        pieces = pltpu.VMEM((n_tile, LEN, depth), BF)
        half = pl.pallas_call(
            lambda *refs: half_kernel(near_bit, masks, pairs, n_tile, *refs),
            out_shape=shape(NQ, LEN, LB, dtype=F32),
            in_specs=[VMEM] * 7,
            out_specs=VMEM,
            scratch_shapes=[pieces],
            compiler_params=limit(12),
            cost_estimate=cost(n_pair * LEN * depth * LB, n_pair * depth * LB),
        )(home, got, near_in, near_swap, held, weights, done)
        return pl.pallas_call(
            lambda *refs: score_kernel(near_bit, masks, pairs, n_tile, *refs),
            out_shape=shape(1, EDGE, EDGE * Z, dtype=F32),
            in_specs=[VMEM] * 12,
            out_specs=VMEM,
            scratch_shapes=[
                pieces,
                pltpu.VMEM((LEN, XR * Z), F32),
                pltpu.VMEM((NTPL * EDGE, 2 * FP), BF),
            ],
            compiler_params=limit(28),
            cost_estimate=cost(4 << 30, 20 << 20),
        )(
            home,
            got,
            near_in,
            near_swap,
            swapped,
            half,
            weights,
            spectra,
            plane,
            jnp.asarray(line),
            jnp.asarray(back),
            inverse,
        )

    return jax.shard_map(
        local,
        mesh=mesh,
        in_specs=(P("grp", None, "tile"), P("grp"), P("grp", None), P(), P()),
        out_specs=P("tile", "grp", None),
        check_vma=False,
    )
```

```python
import math

import jax
import jax.numpy as jnp
import numpy as np
from jax import lax
from jax.experimental import pallas as pl
from jax.experimental.pallas import tpu as pltpu
from jax.sharding import PartitionSpec as P

EDGE = 32
XT = 2
K = 16
NTILT = 61
NTPL = 8
NDET = 128
HALO = K // 2
LEN = EDGE + K
X = XT * EDGE
Z = EDGE
XR = EDGE + HALO
LZ = Z + HALO
KZ = LZ // 2 + 1
NF = LEN * KZ
FP = 1024
VH = XR * Z // 2
OH = EDGE * EDGE // 2
XB = 8
NQ = XR // XB
LB = XB * Z
MAX_ANGLE = 1.05
VOXEL = 1.4
SCALE = 1.0 / (LEN * LEN * LZ)
BF = jnp.bfloat16
F32 = jnp.float32


def reach(q):
    x = np.arange(q * XB, (q + 1) * XB) - (X - 1) / 2.0
    z = np.arange(Z) - (Z - 1) / 2.0
    top = 0.0
    low = 0.0
    angle = np.linspace(-MAX_ANGLE, MAX_ANGLE, 4001)
    first = True
    for xv in (x[0], x[-1]):
        for zv in (z[0], z[-1]):
            pos = VOXEL * (xv * np.cos(angle) + zv * np.sin(angle)) + (NDET - 1) / 2.0
            low = pos.min() if first else min(low, pos.min())
            top = pos.max() if first else max(top, pos.max())
            first = False
    return math.ceil(low - 1.0 - 0.01), math.floor(top + 1.0 + 0.01)


def pair_list(n_det):
    pairs = []
    for q in range(NQ):
        low, top = reach(q)
        pairs.append(list(range(max(low, 0) // n_det, min(top, NDET - 1) // n_det + 1)))
    return pairs


def rounded(table):
    return np.asarray(table, np.float32).astype(jnp.bfloat16)


def plane_tables():
    kz = np.repeat(np.arange(KZ), LEN)
    kx = np.tile(np.arange(LEN), KZ)
    mid = (EDGE - 1) / 2.0

    def waves(k, at, length, width):
        p = 2.0 * np.pi * (np.outer(at, k) % length) / length
        out = np.zeros((2, len(at), width), np.float32)
        out[0, :, : len(k)], out[1, :, : len(k)] = np.cos(p), np.sin(p)
        return out

    vx = np.repeat(np.arange(EDGE // 2) - mid, EDGE)
    vz = np.tile(np.arange(EDGE) - mid, EDGE // 2)
    weight = np.full((KZ, 1), 2.0)
    weight[0] = weight[-1] = 1.0
    turn = np.zeros((2, XT, FP))
    for col in range(XT):
        back = HALO if col == 0 else 0
        p = 2.0 * np.pi * (kx * (mid - back) / LEN + kz * (mid - HALO) / LZ)
        turn[0, col, :NF], turn[1, col, :NF] = np.cos(p), np.sin(p)
    return (
        waves(kx, np.arange(XR // 2) - (XR - 1) / 2.0, LEN, FP),
        waves(kz, np.arange(Z) - (Z - 1) / 2.0, LZ, FP),
        waves(vx, np.arange(LEN // 2), LEN, OH),
        waves(vz, np.arange(KZ), LZ, OH) * weight,
        turn,
    )


def line_tables():
    def table(outs, ins, sign):
        p = 2.0 * np.pi * (np.outer(np.arange(outs), np.arange(ins)) % LEN) / LEN
        c, s = np.cos(p), np.sin(p) * sign
        return c, s

    c, s = table(LEN, LEN, 1.0)
    region = rounded(np.block([[c, s], [-s, c]]))
    c, s = table(LEN, K, 1.0)
    template = rounded(np.block([[c, s], [-s, c]]))
    c, s = table(EDGE, LEN, 1.0)
    back = rounded(np.block([[c, -s], [s, c]]))
    return region, template, back


def place():
    position = lax.axis_index("tile").astype(jnp.int32)
    return position // XT, position % XT


def pack_kernel(
    near_bit,
    masks,
    range_hbm,
    angle_hbm,
    proj_hbm,
    turns_ref,
    home_ref,
    near_ref,
    give_ref,
    mine_ref,
    proj_ref,
    angle_ref,
    range_ref,
    rows_ref,
    sem,
):
    fetch = [
        pltpu.make_async_copy(range_hbm, range_ref, sem.at[0]),
        pltpu.make_async_copy(angle_hbm, angle_ref, sem.at[1]),
        pltpu.make_async_copy(proj_hbm, proj_ref, sem.at[2]),
    ]
    for copy in fetch:
        copy.start()
    fetch[1].wait()
    for i, wave in enumerate((jnp.cos, jnp.sin)):
        spread = jnp.broadcast_to(wave(angle_ref[...]), (128, angle_ref.shape[1])).T
        turns_ref[i, :, :128] = spread
        turns_ref[i, :, 128:] = spread
    fetch[0].wait()
    fetch[2].wait()
    n_tilt, n_det, y_count = proj_ref.shape
    depth = home_ref.shape[1]
    y = lax.broadcasted_iota(jnp.int32, (n_det, y_count), 1)
    parts = []
    for t in range(n_tilt):
        keep = (y >= range_ref[0, t]) & (y < range_ref[1, t])
        parts.append(jnp.where(keep, proj_ref[t].astype(F32), 0.0))
    if depth > n_tilt * n_det:
        parts.append(jnp.zeros((depth - n_tilt * n_det, y_count), F32))
    edge = jnp.zeros((HALO, depth), F32)
    rows_ref[...] = jnp.concatenate([edge, jnp.concatenate(parts, 0).T, edge], 0).astype(BF)
    chip, core = place()

    def rows(target):
        return rows_ref[pl.ds(pl.multiple_of(target * EDGE, EDGE), LEN)]

    home_ref[...] = rows(chip)
    near_ref[...] = rows(chip ^ near_bit)
    give_ref[0] = home_ref[...]
    for j, mask in enumerate(masks):
        mine_ref[j] = rows(chip ^ mask ^ (near_bit * core))
        give_ref[1 + j] = rows(chip ^ mask ^ (near_bit * (1 - core)))


def merge_kernel(mine_ref, got_ref, done_ref, *out_refs):
    done_ref[...] = jnp.zeros_like(done_ref)
    for j, out_ref in enumerate(out_refs):
        out_ref[0] = mine_ref[j]
        out_ref[1] = got_ref[1 + j]


def build_weights(n_det, n_tile, pairs, col, turns_ref, w_ref, whole_ref, part_ref):
    depth = whole_ref.shape[0]
    lane = lax.broadcasted_iota(jnp.int32, (n_det, LB), 1)
    step = lane // Z
    pack = 16 // n_det
    own = lax.broadcasted_iota(jnp.int32, (n_det, LB), 0).astype(F32)
    top = NTILT // pack * pack
    tail = depth - top * n_det
    base = 0
    for q, sources in enumerate(pairs):
        block = jnp.where(col == 0, q, NQ - 1 - q)
        flip = (block * LB + lane) >= VH
        x = jnp.where(flip, XB - 1 - step + jnp.where(block == NQ // 2, XB // 2, 0), step)
        x = x + (block * XB + col * (X - XR))
        x = VOXEL * (x.astype(F32) - (X - 1) / 2.0)
        z = jnp.where(flip, Z - 1 - lane % Z, lane % Z)
        z = VOXEL * (z.astype(F32) - (Z - 1) / 2.0)

        def tilt(t, z=z, x=x):
            pos = x * turns_ref[0, t : t + 1] + z * turns_ref[1, t : t + 1] + (NDET - 1) / 2.0
            whole = jnp.floor(pos)
            return own - whole, pos - whole

        for first in range(0, NTILT, pack):
            got = [tilt(t) for t in range(first, min(first + pack, NTILT))]
            rows = pack * n_det if first < top else tail
            gap = rows - len(got) * n_det
            for ref, values in ((whole_ref, [g[0] for g in got]), (part_ref, [g[1] for g in got])):
                if gap:
                    values.append(jnp.zeros((gap, LB), F32))
                ref[first * n_det : first * n_det + rows] = jnp.concatenate(values, 0).astype(BF)

        def build(j, carry, base=base, first=sources[0]):
            src = first + j
            src = jnp.where(col == 0, src, n_tile - 1 - src)
            shift = (src * n_det).astype(F32).astype(BF)
            off = (whole_ref[...] + shift) - part_ref[...]
            one = jnp.ones((), BF)
            w_ref[base + j] = jnp.maximum(one - jnp.abs(off), jnp.zeros((), BF))
            return carry

        lax.fori_loop(0, len(sources), build, 0)
        base += len(sources)


def build_plane(fx_ref, fz_ref, plane_ref):
    def forward(x, carry):
        cos_x, sin_x = fx_ref[0, pl.ds(x, 1)], fx_ref[1, pl.ds(x, 1)]
        cos_z, sin_z = fz_ref[0], fz_ref[1]
        at = pl.ds(pl.multiple_of(x * Z, Z), Z)
        plane_ref[at, :FP] = (cos_x * cos_z - sin_x * sin_z).astype(BF)
        plane_ref[at, FP:] = (-sin_x * cos_z - cos_x * sin_z).astype(BF)
        return carry

    lax.fori_loop(0, XR // 2, forward, 0)


def build_inverse(ix_ref, iz_ref, inverse_ref):
    odd = lax.broadcasted_iota(jnp.int32, (1, OH), 1) // EDGE % 2
    turn = 1.0 - 2.0 * odd.astype(F32)

    def inverse(k, carry):
        cos_z, sin_z = iz_ref[0, pl.ds(k, 1)], iz_ref[1, pl.ds(k, 1)]
        cos_x, sin_x = ix_ref[0], ix_ref[1]
        real = cos_x * cos_z - sin_x * sin_z
        imag = -sin_x * cos_z - cos_x * sin_z
        low = pl.multiple_of(k * LEN, 16)
        inverse_ref[pl.ds(low, LEN)] = jnp.concatenate([real, imag * turn], 0).astype(BF)
        inverse_ref[pl.ds(FP + low, LEN)] = jnp.concatenate([imag, -real * turn], 0).astype(BF)
        return carry

    lax.fori_loop(0, KZ, inverse, 0)
    inverse_ref[NF:FP] = jnp.zeros((FP - NF, OH), BF)
    inverse_ref[FP + NF :] = jnp.zeros((FP - NF, OH), BF)


def flat_templates(rot_ref, bank_ref, plane_ref, flat_ref):
    chosen = jnp.concatenate([bank_ref[rot_ref[r]] for r in range(NTPL)], 0)
    plane = jnp.concatenate([plane_ref[b * Z : b * Z + K] for b in range(K)], 0)
    flat_ref[...] = jnp.dot(chosen, plane, preferred_element_type=F32).astype(BF)


def template_kernel(
    _, flat_ref, ix_ref, iz_ref, line_ref, turn_ref, out_ref, inverse_ref, done_ref
):
    build_inverse(ix_ref, iz_ref, inverse_ref)
    done_ref[...] = jnp.zeros_like(done_ref)
    _, col = place()
    cos = jnp.where(col == 0, turn_ref[0, 0:1], turn_ref[0, 1:2])
    sin = jnp.where(col == 0, turn_ref[1, 0:1], turn_ref[1, 1:2])
    for r in range(NTPL):
        part = flat_ref[r * K : (r + 1) * K]
        stacked = jnp.concatenate([part[:, :FP], part[:, FP:]], 0)
        full = jnp.dot(line_ref[...], stacked, preferred_element_type=F32)
        real, imag = full[:LEN], -full[LEN:]
        out_ref[r, :LEN] = (real * cos - imag * sin).astype(BF)
        out_ref[r, LEN:] = (real * sin + imag * cos).astype(BF)


def prepare_kernel(n_det, n_tile, pairs, turns_ref, _, *refs):
    sources, outs, targets, (sem, whole_ref, part_ref) = refs[:4], refs[4:8], refs[8:12], refs[12:]
    fetch = [
        pltpu.make_async_copy(a, b, sem.at[i]) for i, (a, b) in enumerate(zip(sources, targets))
    ]
    for copy in fetch:
        copy.start()
    w_ref, plane_ref, flat_ref, done_ref = outs
    _, col = place()
    build_weights(n_det, n_tile, pairs, col, turns_ref, w_ref, whole_ref, part_ref)
    for copy in fetch:
        copy.wait()
    rot_ref, bank_ref, fx_ref, fz_ref = targets
    build_plane(fx_ref, fz_ref, plane_ref)
    flat_templates(rot_ref, bank_ref, plane_ref, flat_ref)
    done_ref[...] = jnp.zeros_like(done_ref)


def join_kernel(*refs):
    out_ref = refs[-1]
    for j, ref in enumerate(refs[:-1]):
        out_ref[2 * j] = ref[0]
        out_ref[2 * j + 1] = ref[1]


def gather_pieces(near_bit, masks, from_mate, data_ref, home_ref, got_ref, near_ref, near_swap_ref, held_ref):
    chip, core = place()
    mate = 1 - core
    data_ref[chip * XT + core] = home_ref[...]
    data_ref[chip * XT + mate] = got_ref[0]
    data_ref[(chip ^ near_bit) * XT + core] = near_ref[...]
    data_ref[(chip ^ near_bit) * XT + mate] = near_swap_ref[...]
    taker, other = (mate, core) if from_mate else (core, mate)
    for j, mask in enumerate(masks):
        source = (chip ^ mask ^ (near_bit * taker)) * XT
        data_ref[source + taker] = held_ref[2 * j]
        data_ref[source + other] = held_ref[2 * j + 1]


def partial_sums(n_tile, pairs, upper, core, data_ref, w_ref):
    base = 0
    for sources in pairs:
        total = jnp.zeros((LEN, LB), F32)
        for j, src in enumerate(sources):
            if (src >= n_tile // 2) == upper:
                part = data_ref[jnp.where(core == 0, src, n_tile - 1 - src)]
                total += jnp.dot(part, w_ref[base + j], preferred_element_type=F32)
        base += len(sources)
        yield total


def half_kernel(near_bit, masks, pairs, n_tile, *refs):
    *pieces, w_ref, _, half_ref, data_ref = refs
    gather_pieces(near_bit, masks, False, data_ref, *pieces)
    chip, core = place()
    for upper in (False, True):

        @pl.when((chip >= near_bit) == upper)
        def _():
            for q, total in enumerate(partial_sums(n_tile, pairs, upper, core, data_ref, w_ref)):
                half_ref[q] = total


def score_kernel(near_bit, masks, pairs, n_tile, *refs):
    half_ref, w_ref, tmpl_ref, plane_ref, line_ref, back_ref, inverse_ref = refs[5:12]
    out_ref, data_ref, vol_ref, mid_ref = refs[12:]
    gather_pieces(near_bit, masks, True, data_ref, *refs[:5])
    chip, core = place()
    for upper in (False, True):
        for col in range(XT):

            @pl.when(((chip < near_bit) == upper) & (core == col))
            def _():
                for q, total in enumerate(partial_sums(n_tile, pairs, upper, col, data_ref, w_ref)):
                    low = (NQ - 1 - q if col else q) * LB
                    vol_ref[:, low : low + LB] = total + half_ref[q]

    near_half = vol_ref[:, :VH]
    far_half = jnp.concatenate(
        [vol_ref[:, 4 * LB :], vol_ref[:, 3 * LB : 4 * LB], vol_ref[:, VH : 3 * LB]], 1
    )
    even, odd = (near_half + far_half).astype(BF), (near_half - far_half).astype(BF)
    stacked = jnp.concatenate(
        [
            jnp.dot(even, plane_ref[:, :FP], preferred_element_type=F32).astype(BF),
            jnp.dot(odd, plane_ref[:, FP:], preferred_element_type=F32).astype(BF),
        ],
        0,
    )
    full = jnp.dot(line_ref[...], stacked, preferred_element_type=F32)
    real, imag = full[:LEN], full[LEN:]
    for r in range(NTPL):
        t_real = tmpl_ref[r, :LEN].astype(F32)
        t_imag = tmpl_ref[r, LEN:].astype(F32)
        prod = jnp.concatenate(
            [
                (t_real * real - t_imag * imag).astype(BF),
                (t_real * imag + t_imag * real).astype(BF),
            ],
            0,
        )
        line = jnp.dot(back_ref[...], prod, preferred_element_type=F32).astype(BF)
        mid_ref[r * EDGE : (r + 1) * EDGE, :FP] = line[:EDGE]
        mid_ref[r * EDGE : (r + 1) * EDGE, FP:] = line[EDGE:]
    even = jnp.dot(mid_ref[:, :FP], inverse_ref[:FP], preferred_element_type=F32)
    odd = jnp.dot(mid_ref[:, FP:], inverse_ref[FP:], preferred_element_type=F32)
    best = even[:EDGE] + odd[:EDGE]
    mirrored = even[:EDGE] - odd[:EDGE]
    for r in range(1, NTPL):
        at = slice(r * EDGE, (r + 1) * EDGE)
        best = jnp.maximum(best, even[at] + odd[at])
        mirrored = jnp.maximum(mirrored, even[at] - odd[at])
    out_ref[0, :, :OH] = best * SCALE
    mirrored = mirrored * SCALE
    order = 127 - lax.broadcasted_iota(jnp.int32, (EDGE, 128), 1)
    for low in range(0, OH, 128):
        part = jnp.take_along_axis(mirrored[:, low : low + 128], order, axis=1)
        out_ref[0, :, 2 * OH - 128 - low : 2 * OH - low] = part


VMEM = pl.BlockSpec(memory_space=pltpu.VMEM)
SMEM = pl.BlockSpec(memory_space=pltpu.SMEM)
HBM = pl.BlockSpec(memory_space=pltpu.HBM)


def limit(mib):
    return pltpu.CompilerParams(vmem_limit_bytes=mib << 20)


def cost(flops, nbytes):
    return pl.CostEstimate(flops=flops, bytes_accessed=nbytes, transcendentals=0)


def pinned(array):
    return pltpu.with_memory_space_constraint(array, pltpu.HBM)


def shape(*dims, dtype=BF):
    return jax.ShapeDtypeStruct(dims, dtype)


def solution(mesh):
    n_tile = mesh.shape["tile"]
    n_block = n_tile // XT
    n_det = NDET // n_tile
    depth = (NTILT * n_det + 127) // 128 * 128
    near_bit = n_block // 2
    masks = [k for k in range(1, n_block) if not k & near_bit]
    masks.sort(key=lambda k: k != near_bit // 2)
    n_op = len(masks)
    pairs = pair_list(n_det)
    n_pair = sum(len(p) for p in pairs)
    tables = plane_tables()
    line, line_t, back = line_tables()
    mate = [(i, i ^ 1) for i in range(n_tile)]
    near_pairs = [(i, i ^ (near_bit * XT)) for i in range(n_tile)]

    def route(mask):
        return [(i, i ^ (mask * XT) ^ (near_bit * XT * (i % XT))) for i in range(n_tile)]

    def local(projections, tilt_angle, row_range, template_bank, rot_index):
        y_count = projections.shape[0]
        by_y = jnp.transpose(projections, (1, 2, 0))
        turns, home, near, give, mine = pl.pallas_call(
            lambda *refs: pack_kernel(near_bit, masks, *refs),
            out_shape=(
                shape(2, NTILT, LB, dtype=F32),
                shape(LEN, depth),
                shape(LEN, depth),
                shape(1 + n_op, LEN, depth),
                shape(n_op, LEN, depth),
            ),
            in_specs=[HBM, HBM, HBM],
            out_specs=(VMEM,) * 5,
            scratch_shapes=[
                pltpu.VMEM(by_y.shape, BF),
                pltpu.VMEM((1, NTILT), F32),
                pltpu.SMEM((2, NTILT), jnp.int32),
                pltpu.VMEM((y_count + 2 * HALO, depth), BF),
                pltpu.SemaphoreType.DMA((3,)),
            ],
            compiler_params=limit(8),
        )(pinned(row_range.T), pinned(tilt_angle.reshape(1, NTILT)), pinned(by_y))
        got = lax.ppermute(give, "tile", mate)
        near_in = lax.ppermute(near, "tile", near_pairs)
        merged, *payload = pl.pallas_call(
            merge_kernel,
            out_shape=(shape(8, 128, dtype=F32),) + (shape(2, LEN, depth),) * n_op,
            in_specs=[VMEM, VMEM],
            out_specs=(VMEM,) * (1 + n_op),
            compiler_params=limit(8),
        )(mine, got)
        arrived = [lax.ppermute(p, "tile", route(m)) for p, m in zip(payload, masks)]
        constants = (
            rot_index,
            template_bank,
            *[jnp.asarray(t, F32) for t in tables[:2]],
        )
        weights, plane, flat, done = pl.pallas_call(
            lambda *refs: prepare_kernel(n_det, n_tile, pairs, *refs),
            out_shape=(
                shape(n_pair, depth, LB),
                shape(VH, 2 * FP),
                shape(NTPL * K, 2 * FP),
                shape(8, 128, dtype=F32),
            ),
            in_specs=[VMEM, VMEM] + [HBM] * 4,
            out_specs=(VMEM,) * 4,
            scratch_shapes=[
                pltpu.SMEM((NTPL,), jnp.int32),
                *[pltpu.VMEM(c.shape, c.dtype) for c in constants[1:]],
                pltpu.SemaphoreType.DMA((4,)),
                pltpu.VMEM((depth, LB), BF),
                pltpu.VMEM((depth, LB), BF),
            ],
            compiler_params=limit(24),
            cost_estimate=cost(1 << 32, 16 << 20),
        )(turns, merged, *[pinned(c) for c in constants])
        near_in, done = lax.optimization_barrier((near_in, done))
        near_swap = lax.ppermute(near_in, "tile", mate)
        spectra, inverse, done = pl.pallas_call(
            template_kernel,
            out_shape=(
                shape(NTPL, 2 * LEN, FP),
                shape(2 * FP, OH),
                shape(8, 128, dtype=F32),
            ),
            in_specs=[VMEM] * 6,
            out_specs=(VMEM,) * 3,
            compiler_params=limit(8),
            cost_estimate=cost(1 << 20, 1 << 14),
        )(
            done,
            flat,
            jnp.asarray(tables[2], F32),
            jnp.asarray(tables[3], F32),
            jnp.asarray(line_t),
            jnp.asarray(tables[4], F32),
        )
        done, near_swap, *arrived = lax.optimization_barrier((done, near_swap, *arrived))
        held = pl.pallas_call(
            join_kernel,
            out_shape=shape(2 * n_op, LEN, depth),
            in_specs=[VMEM] * n_op,
            out_specs=VMEM,
            compiler_params=limit(4),
        )(*arrived)
        swapped = lax.ppermute(held, "tile", mate)
        pieces = pltpu.VMEM((n_tile, LEN, depth), BF)
        half = pl.pallas_call(
            lambda *refs: half_kernel(near_bit, masks, pairs, n_tile, *refs),
            out_shape=shape(NQ, LEN, LB, dtype=F32),
            in_specs=[VMEM] * 7,
            out_specs=VMEM,
            scratch_shapes=[pieces],
            compiler_params=limit(12),
            cost_estimate=cost(n_pair * LEN * depth * LB, n_pair * depth * LB),
        )(home, got, near_in, near_swap, held, weights, done)
        return pl.pallas_call(
            lambda *refs: score_kernel(near_bit, masks, pairs, n_tile, *refs),
            out_shape=shape(1, EDGE, EDGE * Z, dtype=F32),
            in_specs=[VMEM] * 12,
            out_specs=VMEM,
            scratch_shapes=[
                pieces,
                pltpu.VMEM((LEN, XR * Z), F32),
                pltpu.VMEM((NTPL * EDGE, 2 * FP), BF),
            ],
            compiler_params=limit(28),
            cost_estimate=cost(4 << 30, 20 << 20),
        )(
            home,
            got,
            near_in,
            near_swap,
            swapped,
            half,
            weights,
            spectra,
            plane,
            jnp.asarray(line),
            jnp.asarray(back),
            inverse,
        )

    return jax.shard_map(
        local,
        mesh=mesh,
        in_specs=(P("grp", None, "tile"), P("grp"), P("grp", None), P(), P()),
        out_specs=P("tile", "grp", None),
        check_vma=False,
    )
```

```python
import math

import jax
import jax.numpy as jnp
import numpy as np
from jax import lax
from jax.experimental import pallas as pl
from jax.experimental.pallas import tpu as pltpu
from jax.sharding import PartitionSpec as P

EDGE = 32
XT = 2
K = 16
NTILT = 61
NTPL = 8
NDET = 128
HALO = K // 2
LEN = EDGE + K
X = XT * EDGE
Z = EDGE
XR = EDGE + HALO
LZ = Z + HALO
KZ = LZ // 2 + 1
NF = LEN * KZ
FP = 1024
VH = XR * Z // 2
OH = EDGE * EDGE // 2
XB = 8
NQ = XR // XB
LB = XB * Z
MAX_ANGLE = 1.05
VOXEL = 1.4
SCALE = 1.0 / (LEN * LEN * LZ)
BF = jnp.bfloat16
F32 = jnp.float32


def reach(q):
    x = np.arange(q * XB, (q + 1) * XB) - (X - 1) / 2.0
    z = np.arange(Z) - (Z - 1) / 2.0
    top = 0.0
    low = 0.0
    angle = np.linspace(-MAX_ANGLE, MAX_ANGLE, 4001)
    first = True
    for xv in (x[0], x[-1]):
        for zv in (z[0], z[-1]):
            pos = VOXEL * (xv * np.cos(angle) + zv * np.sin(angle)) + (NDET - 1) / 2.0
            low = pos.min() if first else min(low, pos.min())
            top = pos.max() if first else max(top, pos.max())
            first = False
    return math.ceil(low - 1.0 - 0.01), math.floor(top + 1.0 + 0.01)


def pair_list(n_det):
    pairs = []
    for q in range(NQ):
        low, top = reach(q)
        pairs.append(list(range(max(low, 0) // n_det, min(top, NDET - 1) // n_det + 1)))
    return pairs


def rounded(table):
    return np.asarray(table, np.float32).astype(jnp.bfloat16)


def plane_tables():
    kz = np.repeat(np.arange(KZ), LEN)
    kx = np.tile(np.arange(LEN), KZ)
    mid = (EDGE - 1) / 2.0

    def waves(k, at, length, width):
        p = 2.0 * np.pi * (np.outer(at, k) % length) / length
        out = np.zeros((2, len(at), width), np.float32)
        out[0, :, : len(k)], out[1, :, : len(k)] = np.cos(p), np.sin(p)
        return out

    vx = np.repeat(np.arange(EDGE // 2) - mid, EDGE)
    vz = np.tile(np.arange(EDGE) - mid, EDGE // 2)
    weight = np.full((KZ, 1), 2.0)
    weight[0] = weight[-1] = 1.0
    turn = np.zeros((2, XT, FP))
    for col in range(XT):
        back = HALO if col == 0 else 0
        p = 2.0 * np.pi * (kx * (mid - back) / LEN + kz * (mid - HALO) / LZ)
        turn[0, col, :NF], turn[1, col, :NF] = np.cos(p), np.sin(p)
    return (
        waves(kx, np.arange(XR // 2) - (XR - 1) / 2.0, LEN, FP),
        waves(kz, np.arange(Z) - (Z - 1) / 2.0, LZ, FP),
        waves(vx, np.arange(LEN // 2), LEN, OH),
        waves(vz, np.arange(KZ), LZ, OH) * weight,
        turn,
    )


def line_tables():
    def table(outs, ins, sign):
        p = 2.0 * np.pi * (np.outer(np.arange(outs), np.arange(ins)) % LEN) / LEN
        c, s = np.cos(p), np.sin(p) * sign
        return c, s

    c, s = table(LEN, LEN, 1.0)
    region = rounded(np.block([[c, s], [-s, c]]))
    c, s = table(LEN, K, 1.0)
    template = rounded(np.block([[c, s], [-s, c]]))
    c, s = table(EDGE, LEN, 1.0)
    back = rounded(np.block([[c, -s], [s, c]]))
    return region, template, back


def place():
    position = lax.axis_index("tile").astype(jnp.int32)
    return position // XT, position % XT


def pack_kernel(
    near_bit,
    masks,
    range_hbm,
    angle_hbm,
    proj_hbm,
    turns_ref,
    home_ref,
    near_ref,
    give_ref,
    mine_ref,
    proj_ref,
    angle_ref,
    range_ref,
    rows_ref,
    sem,
):
    fetch = [
        pltpu.make_async_copy(range_hbm, range_ref, sem.at[0]),
        pltpu.make_async_copy(angle_hbm, angle_ref, sem.at[1]),
        pltpu.make_async_copy(proj_hbm, proj_ref, sem.at[2]),
    ]
    for copy in fetch:
        copy.start()
    fetch[1].wait()
    for i, wave in enumerate((jnp.cos, jnp.sin)):
        spread = jnp.broadcast_to(wave(angle_ref[...]), (128, angle_ref.shape[1])).T
        turns_ref[i, :, :128] = spread
        turns_ref[i, :, 128:] = spread
    fetch[0].wait()
    fetch[2].wait()
    n_tilt, n_det, y_count = proj_ref.shape
    depth = home_ref.shape[1]
    y = lax.broadcasted_iota(jnp.int32, (n_det, y_count), 1)
    parts = []
    for t in range(n_tilt):
        keep = (y >= range_ref[0, t]) & (y < range_ref[1, t])
        parts.append(jnp.where(keep, proj_ref[t].astype(F32), 0.0))
    if depth > n_tilt * n_det:
        parts.append(jnp.zeros((depth - n_tilt * n_det, y_count), F32))
    edge = jnp.zeros((HALO, depth), F32)
    rows_ref[...] = jnp.concatenate([edge, jnp.concatenate(parts, 0).T, edge], 0).astype(BF)
    chip, core = place()

    def rows(target):
        return rows_ref[pl.ds(pl.multiple_of(target * EDGE, EDGE), LEN)]

    home_ref[...] = rows(chip)
    near_ref[...] = rows(chip ^ near_bit)
    give_ref[0] = home_ref[...]
    for j, mask in enumerate(masks):
        mine_ref[j] = rows(chip ^ mask ^ (near_bit * core))
        give_ref[1 + j] = rows(chip ^ mask ^ (near_bit * (1 - core)))


def merge_kernel(mine_ref, got_ref, done_ref, *out_refs):
    done_ref[...] = jnp.zeros_like(done_ref)
    for j, out_ref in enumerate(out_refs):
        out_ref[0] = mine_ref[j]
        out_ref[1] = got_ref[1 + j]


def build_weights(n_det, n_tile, pairs, col, turns_ref, w_ref, whole_ref, part_ref):
    depth = whole_ref.shape[0]
    lane = lax.broadcasted_iota(jnp.int32, (n_det, LB), 1)
    step = lane // Z
    pack = 16 // n_det
    own = lax.broadcasted_iota(jnp.int32, (n_det, LB), 0).astype(F32)
    top = NTILT // pack * pack
    tail = depth - top * n_det
    base = 0
    for q, sources in enumerate(pairs):
        block = jnp.where(col == 0, q, NQ - 1 - q)
        flip = (block * LB + lane) >= VH
        x = jnp.where(flip, XB - 1 - step + jnp.where(block == NQ // 2, XB // 2, 0), step)
        x = x + (block * XB + col * (X - XR))
        x = VOXEL * (x.astype(F32) - (X - 1) / 2.0)
        z = jnp.where(flip, Z - 1 - lane % Z, lane % Z)
        z = VOXEL * (z.astype(F32) - (Z - 1) / 2.0)

        def tilt(t, z=z, x=x):
            pos = x * turns_ref[0, t : t + 1] + z * turns_ref[1, t : t + 1] + (NDET - 1) / 2.0
            whole = jnp.floor(pos)
            return own - whole, pos - whole

        for first in range(0, NTILT, pack):
            got = [tilt(t) for t in range(first, min(first + pack, NTILT))]
            rows = pack * n_det if first < top else tail
            gap = rows - len(got) * n_det
            for ref, values in ((whole_ref, [g[0] for g in got]), (part_ref, [g[1] for g in got])):
                if gap:
                    values.append(jnp.zeros((gap, LB), F32))
                ref[first * n_det : first * n_det + rows] = jnp.concatenate(values, 0).astype(BF)

        def build(j, carry, base=base, first=sources[0]):
            src = first + j
            src = jnp.where(col == 0, src, n_tile - 1 - src)
            shift = (src * n_det).astype(F32).astype(BF)
            off = (whole_ref[...] + shift) - part_ref[...]
            one = jnp.ones((), BF)
            w_ref[base + j] = jnp.maximum(one - jnp.abs(off), jnp.zeros((), BF))
            return carry

        lax.fori_loop(0, len(sources), build, 0, unroll=2)
        base += len(sources)


def build_planes(fx_ref, fz_ref, ix_ref, iz_ref, plane_ref, inverse_ref):
    def forward(x, carry):
        cos_x, sin_x = fx_ref[0, pl.ds(x, 1)], fx_ref[1, pl.ds(x, 1)]
        cos_z, sin_z = fz_ref[0], fz_ref[1]
        at = pl.ds(pl.multiple_of(x * Z, Z), Z)
        plane_ref[at, :FP] = (cos_x * cos_z - sin_x * sin_z).astype(BF)
        plane_ref[at, FP:] = (-sin_x * cos_z - cos_x * sin_z).astype(BF)
        return carry

    lax.fori_loop(0, XR // 2, forward, 0)
    odd = lax.broadcasted_iota(jnp.int32, (1, OH), 1) // EDGE % 2
    turn = 1.0 - 2.0 * odd.astype(F32)

    def inverse(k, carry):
        cos_z, sin_z = iz_ref[0, pl.ds(k, 1)], iz_ref[1, pl.ds(k, 1)]
        cos_x, sin_x = ix_ref[0], ix_ref[1]
        real = cos_x * cos_z - sin_x * sin_z
        imag = -sin_x * cos_z - cos_x * sin_z
        low = pl.multiple_of(k * LEN, 16)
        inverse_ref[pl.ds(low, LEN)] = jnp.concatenate([real, imag * turn], 0).astype(BF)
        inverse_ref[pl.ds(FP + low, LEN)] = jnp.concatenate([imag, -real * turn], 0).astype(BF)
        return carry

    lax.fori_loop(0, KZ, inverse, 0)
    inverse_ref[NF:FP] = jnp.zeros((FP - NF, OH), BF)
    inverse_ref[FP + NF :] = jnp.zeros((FP - NF, OH), BF)


def flat_templates(rot_ref, bank_ref, plane_ref, flat_ref):
    chosen = jnp.concatenate([bank_ref[rot_ref[r]] for r in range(NTPL)], 0)
    plane = jnp.concatenate([plane_ref[b * Z : b * Z + K] for b in range(K)], 0)
    flat_ref[...] = jnp.dot(chosen, plane, preferred_element_type=F32).astype(BF)


def template_kernel(_, flat_ref, line_ref, turn_ref, out_ref, done_ref):
    done_ref[...] = jnp.zeros_like(done_ref)
    _, col = place()
    cos = jnp.where(col == 0, turn_ref[0, 0:1], turn_ref[0, 1:2])
    sin = jnp.where(col == 0, turn_ref[1, 0:1], turn_ref[1, 1:2])
    for r in range(NTPL):
        part = flat_ref[r * K : (r + 1) * K]
        stacked = jnp.concatenate([part[:, :FP], part[:, FP:]], 0)
        full = jnp.dot(line_ref[...], stacked, preferred_element_type=F32)
        real, imag = full[:LEN], -full[LEN:]
        out_ref[r, :LEN] = (real * cos - imag * sin).astype(BF)
        out_ref[r, LEN:] = (real * sin + imag * cos).astype(BF)


def prepare_kernel(n_det, n_tile, pairs, turns_ref, _, *refs):
    sources, outs, targets, (sem, whole_ref, part_ref) = refs[:6], refs[6:11], refs[11:17], refs[17:]
    fetch = [
        pltpu.make_async_copy(a, b, sem.at[i]) for i, (a, b) in enumerate(zip(sources, targets))
    ]
    for copy in fetch:
        copy.start()
    w_ref, plane_ref, inverse_ref, flat_ref, done_ref = outs
    _, col = place()
    build_weights(n_det, n_tile, pairs, col, turns_ref, w_ref, whole_ref, part_ref)
    for copy in fetch:
        copy.wait()
    rot_ref, bank_ref, fx_ref, fz_ref, ix_ref, iz_ref = targets
    build_planes(fx_ref, fz_ref, ix_ref, iz_ref, plane_ref, inverse_ref)
    flat_templates(rot_ref, bank_ref, plane_ref, flat_ref)
    done_ref[...] = jnp.zeros_like(done_ref)


def join_kernel(*refs):
    out_ref = refs[-1]
    for j, ref in enumerate(refs[:-1]):
        out_ref[2 * j] = ref[0]
        out_ref[2 * j + 1] = ref[1]


def gather_pieces(near_bit, masks, from_mate, data_ref, home_ref, got_ref, near_ref, near_swap_ref, held_ref):
    chip, core = place()
    mate = 1 - core
    data_ref[chip * XT + core] = home_ref[...]
    data_ref[chip * XT + mate] = got_ref[0]
    data_ref[(chip ^ near_bit) * XT + core] = near_ref[...]
    data_ref[(chip ^ near_bit) * XT + mate] = near_swap_ref[...]
    taker, other = (mate, core) if from_mate else (core, mate)
    for j, mask in enumerate(masks):
        source = (chip ^ mask ^ (near_bit * taker)) * XT
        data_ref[source + taker] = held_ref[2 * j]
        data_ref[source + other] = held_ref[2 * j + 1]


def partial_sums(n_tile, pairs, upper, core, data_ref, w_ref):
    base = 0
    for sources in pairs:
        total = jnp.zeros((LEN, LB), F32)
        for j, src in enumerate(sources):
            if (src >= n_tile // 2) == upper:
                part = data_ref[jnp.where(core == 0, src, n_tile - 1 - src)]
                total += jnp.dot(part, w_ref[base + j], preferred_element_type=F32)
        base += len(sources)
        yield total


def half_kernel(near_bit, masks, pairs, n_tile, *refs):
    *pieces, w_ref, _, half_ref, data_ref = refs
    gather_pieces(near_bit, masks, False, data_ref, *pieces)
    chip, core = place()
    for upper in (False, True):

        @pl.when((chip >= near_bit) == upper)
        def _():
            for q, total in enumerate(partial_sums(n_tile, pairs, upper, core, data_ref, w_ref)):
                half_ref[q] = total


def score_kernel(near_bit, masks, pairs, n_tile, *refs):
    half_ref, w_ref, tmpl_ref, plane_ref, line_ref, back_ref, inverse_ref = refs[5:12]
    out_ref, data_ref, vol_ref, mid_ref = refs[12:]
    gather_pieces(near_bit, masks, True, data_ref, *refs[:5])
    chip, core = place()
    for upper in (False, True):
        for col in range(XT):

            @pl.when(((chip < near_bit) == upper) & (core == col))
            def _():
                for q, total in enumerate(partial_sums(n_tile, pairs, upper, col, data_ref, w_ref)):
                    low = (NQ - 1 - q if col else q) * LB
                    vol_ref[:, low : low + LB] = total + half_ref[q]

    near_half = vol_ref[:, :VH]
    far_half = jnp.concatenate(
        [vol_ref[:, 4 * LB :], vol_ref[:, 3 * LB : 4 * LB], vol_ref[:, VH : 3 * LB]], 1
    )
    even, odd = (near_half + far_half).astype(BF), (near_half - far_half).astype(BF)
    stacked = jnp.concatenate(
        [
            jnp.dot(even, plane_ref[:, :FP], preferred_element_type=F32).astype(BF),
            jnp.dot(odd, plane_ref[:, FP:], preferred_element_type=F32).astype(BF),
        ],
        0,
    )
    full = jnp.dot(line_ref[...], stacked, preferred_element_type=F32)
    real, imag = full[:LEN], full[LEN:]
    for r in range(NTPL):
        t_real = tmpl_ref[r, :LEN].astype(F32)
        t_imag = tmpl_ref[r, LEN:].astype(F32)
        prod = jnp.concatenate(
            [
                (t_real * real - t_imag * imag).astype(BF),
                (t_real * imag + t_imag * real).astype(BF),
            ],
            0,
        )
        line = jnp.dot(back_ref[...], prod, preferred_element_type=F32).astype(BF)
        mid_ref[r * EDGE : (r + 1) * EDGE, :FP] = line[:EDGE]
        mid_ref[r * EDGE : (r + 1) * EDGE, FP:] = line[EDGE:]
    even = jnp.dot(mid_ref[:, :FP], inverse_ref[:FP], preferred_element_type=F32)
    odd = jnp.dot(mid_ref[:, FP:], inverse_ref[FP:], preferred_element_type=F32)
    best = even[:EDGE] + odd[:EDGE]
    mirrored = even[:EDGE] - odd[:EDGE]
    for r in range(1, NTPL):
        at = slice(r * EDGE, (r + 1) * EDGE)
        best = jnp.maximum(best, even[at] + odd[at])
        mirrored = jnp.maximum(mirrored, even[at] - odd[at])
    out_ref[0, :, :OH] = best * SCALE
    mirrored = mirrored * SCALE
    order = 127 - lax.broadcasted_iota(jnp.int32, (EDGE, 128), 1)
    for low in range(0, OH, 128):
        part = jnp.take_along_axis(mirrored[:, low : low + 128], order, axis=1)
        out_ref[0, :, 2 * OH - 128 - low : 2 * OH - low] = part


VMEM = pl.BlockSpec(memory_space=pltpu.VMEM)
SMEM = pl.BlockSpec(memory_space=pltpu.SMEM)
HBM = pl.BlockSpec(memory_space=pltpu.HBM)


def limit(mib):
    return pltpu.CompilerParams(vmem_limit_bytes=mib << 20)


def cost(flops, nbytes):
    return pl.CostEstimate(flops=flops, bytes_accessed=nbytes, transcendentals=0)


def pinned(array):
    return pltpu.with_memory_space_constraint(array, pltpu.HBM)


def shape(*dims, dtype=BF):
    return jax.ShapeDtypeStruct(dims, dtype)


def solution(mesh):
    n_tile = mesh.shape["tile"]
    n_block = n_tile // XT
    n_det = NDET // n_tile
    depth = (NTILT * n_det + 127) // 128 * 128
    near_bit = n_block // 2
    masks = [k for k in range(1, n_block) if not k & near_bit]
    masks.sort(key=lambda k: k != near_bit // 2)
    n_op = len(masks)
    pairs = pair_list(n_det)
    n_pair = sum(len(p) for p in pairs)
    tables = plane_tables()
    line, line_t, back = line_tables()
    mate = [(i, i ^ 1) for i in range(n_tile)]
    near_pairs = [(i, i ^ (near_bit * XT)) for i in range(n_tile)]

    def route(mask):
        return [(i, i ^ (mask * XT) ^ (near_bit * XT * (i % XT))) for i in range(n_tile)]

    def local(projections, tilt_angle, row_range, template_bank, rot_index):
        y_count = projections.shape[0]
        by_y = jnp.transpose(projections, (1, 2, 0))
        turns, home, near, give, mine = pl.pallas_call(
            lambda *refs: pack_kernel(near_bit, masks, *refs),
            out_shape=(
                shape(2, NTILT, LB, dtype=F32),
                shape(LEN, depth),
                shape(LEN, depth),
                shape(1 + n_op, LEN, depth),
                shape(n_op, LEN, depth),
            ),
            in_specs=[HBM, HBM, HBM],
            out_specs=(VMEM,) * 5,
            scratch_shapes=[
                pltpu.VMEM(by_y.shape, BF),
                pltpu.VMEM((1, NTILT), F32),
                pltpu.SMEM((2, NTILT), jnp.int32),
                pltpu.VMEM((y_count + 2 * HALO, depth), BF),
                pltpu.SemaphoreType.DMA((3,)),
            ],
            compiler_params=limit(8),
        )(pinned(row_range.T), pinned(tilt_angle.reshape(1, NTILT)), pinned(by_y))
        got = lax.ppermute(give, "tile", mate)
        near_in = lax.ppermute(near, "tile", near_pairs)
        merged, *payload = pl.pallas_call(
            merge_kernel,
            out_shape=(shape(8, 128, dtype=F32),) + (shape(2, LEN, depth),) * n_op,
            in_specs=[VMEM, VMEM],
            out_specs=(VMEM,) * (1 + n_op),
            compiler_params=limit(8),
        )(mine, got)
        arrived = [lax.ppermute(p, "tile", route(m)) for p, m in zip(payload, masks)]
        constants = (
            rot_index,
            template_bank,
            *[jnp.asarray(t, F32) for t in tables[:4]],
        )
        weights, plane, inverse, flat, done = pl.pallas_call(
            lambda *refs: prepare_kernel(n_det, n_tile, pairs, *refs),
            out_shape=(
                shape(n_pair, depth, LB),
                shape(VH, 2 * FP),
                shape(2 * FP, OH),
                shape(NTPL * K, 2 * FP),
                shape(8, 128, dtype=F32),
            ),
            in_specs=[VMEM, VMEM] + [HBM] * 6,
            out_specs=(VMEM,) * 5,
            scratch_shapes=[
                pltpu.SMEM((NTPL,), jnp.int32),
                *[pltpu.VMEM(c.shape, c.dtype) for c in constants[1:]],
                pltpu.SemaphoreType.DMA((6,)),
                pltpu.VMEM((depth, LB), BF),
                pltpu.VMEM((depth, LB), BF),
            ],
            compiler_params=limit(24),
            cost_estimate=cost(1 << 32, 16 << 20),
        )(turns, merged, *[pinned(c) for c in constants])
        near_in, done = lax.optimization_barrier((near_in, done))
        near_swap = lax.ppermute(near_in, "tile", mate)
        spectra, done = pl.pallas_call(
            template_kernel,
            out_shape=(shape(NTPL, 2 * LEN, FP), shape(8, 128, dtype=F32)),
            in_specs=[VMEM] * 4,
            out_specs=(VMEM,) * 2,
            compiler_params=limit(8),
            cost_estimate=cost(1 << 20, 1 << 14),
        )(done, flat, jnp.asarray(line_t), jnp.asarray(tables[4], F32))
        done, near_swap, *arrived = lax.optimization_barrier((done, near_swap, *arrived))
        held = pl.pallas_call(
            join_kernel,
            out_shape=shape(2 * n_op, LEN, depth),
            in_specs=[VMEM] * n_op,
            out_specs=VMEM,
            compiler_params=limit(4),
        )(*arrived)
        swapped = lax.ppermute(held, "tile", mate)
        pieces = pltpu.VMEM((n_tile, LEN, depth), BF)
        half = pl.pallas_call(
            lambda *refs: half_kernel(near_bit, masks, pairs, n_tile, *refs),
            out_shape=shape(NQ, LEN, LB, dtype=F32),
            in_specs=[VMEM] * 7,
            out_specs=VMEM,
            scratch_shapes=[pieces],
            compiler_params=limit(12),
            cost_estimate=cost(n_pair * LEN * depth * LB, n_pair * depth * LB),
        )(home, got, near_in, near_swap, held, weights, done)
        return pl.pallas_call(
            lambda *refs: score_kernel(near_bit, masks, pairs, n_tile, *refs),
            out_shape=shape(1, EDGE, EDGE * Z, dtype=F32),
            in_specs=[VMEM] * 12,
            out_specs=VMEM,
            scratch_shapes=[
                pieces,
                pltpu.VMEM((LEN, XR * Z), F32),
                pltpu.VMEM((NTPL * EDGE, 2 * FP), BF),
            ],
            compiler_params=limit(28),
            cost_estimate=cost(4 << 30, 20 << 20),
        )(
            home,
            got,
            near_in,
            near_swap,
            swapped,
            half,
            weights,
            spectra,
            plane,
            jnp.asarray(line),
            jnp.asarray(back),
            inverse,
        )

    return jax.shard_map(
        local,
        mesh=mesh,
        in_specs=(P("grp", None, "tile"), P("grp"), P("grp", None), P(), P()),
        out_specs=P("tile", "grp", None),
        check_vma=False,
    )
```
